32 devices in a mesh: job: 2 (over x), actor: 8 (over z, y), tp: 2 (over core).
Axes of the slice: x: 2, y: 2, z: 4, core: 2. Of those that a mesh axis runs over, the one named last changes fastest.
Arguments:
- leaf_states: bfloat16 [4096, 5120], P(('job', 'actor')), parts along dimension 0, may hold values from -6 to 6
- norm_gain: bfloat16 [5120], replicated, may hold values from 0.25 to 1.75
- wq_quant: bfloat16 [5120, 2560], P('actor', 'tp'), may hold values from -4 to 4
- wq_scale: float32 [40, 20], P(None, 'tp'), may hold values from 0.0069877123 to 0.02795085
- key_weight_quantized: bfloat16 [5120, 512], P('actor', 'tp'), may hold values from -4 to 4
- key_weight_scale: float32 [40, 4], P(None, 'tp'), may hold values from 0.0069877123 to 0.02795085
- value_weight_quantized: bfloat16 [5120, 512], P('actor', 'tp'), may hold values from -4 to 4
- value_weight_scale: float32 [40, 4], P(None, 'tp'), may hold values from 0.0069877123 to 0.02795085
- wo_quant: bfloat16 [2560, 5120], P('tp', 'actor'), may hold values from -4 to 4
- wo_scale: float32 [20, 40], P('tp'), may hold values from 0.019764235 to 0.07905694
- q_bias: bfloat16 [2560], P('tp'), may hold values from -2 to 2
- key_bias: bfloat16 [512], P('tp'), may hold values from -2 to 2
- value_bias: bfloat16 [512], P('tp'), may hold values from -3 to 3
- prefix_key_cache: bfloat16 [32, 2048, 512], P(('job', 'actor'), None, 'tp'), parts along dimension 0, may hold values from -140 to 140
- prefix_value_cache: bfloat16 [32, 2048, 512], P(('job', 'actor'), None, 'tp'), parts along dimension 0, may hold values from -15 to 15
- parent_prefix_slot: int32 [4096], P(('job', 'actor')), parts along dimension 0, may hold values from 0 to 1
- prefix_length: int32 [4096], P(('job', 'actor')), parts along dimension 0, may hold values from 1 to 2048, as said below
Outputs:
- attn_out: bfloat16 [4096, 5120], P(('job', 'actor')), parts along dimension 0
The draws below stay inside these ranges and needn't reach their ends.
There are 2 independent parts, one for each index of `job`. The reference program is written for one: setup_inputs(seed, part) draws one part's arguments, and reference() takes and returns one part's arrays. A program takes and returns all parts, laid end to end along the dimension named above; an argument that names none is the same for every part. Nothing has to cross between parts.
Inputs may be any that keep to these rules, and one draw needn't show every extreme that they name: parent_prefix_slot numbers the leaf's prefix among the 2 prefixes of its own actor replica's block of the cache (leaf t belongs to replica t // 256, whose prefixes are cache rows 2 r to 2 r + 1). `prefix_length`: the first leaf of every actor replica sees all 2048 cached positions.
All inputs are finite; a program needn't handle non-finite values.
Results may differ from the reference program's by a relative error of at most 0.0045.
The reference program's roundings to bfloat16 on the way (of `normed` and `attended`) count: a program that leaves them out, or rounds other values in their place, can miss the bound.
Values may be sent and summed in bfloat16 or wider, within the bound.
A program may use at most 192 MiB of HBM per device.

```python
import math
import jax
import jax.numpy as jnp
from jax import lax

MODEL_WIDTH = 5120
HEAD_WIDTH = 128
QUERY_HEADS = 20
KEY_VALUE_HEADS = 4
SCALE_BLOCK = 128
CONTEXT_LENGTH = 2048
PREFIX_PER_ACTOR = 2
LEAF_PER_ACTOR = 256
LEAF_TOTAL = 2048
PREFIX_TOTAL = 16
N_ACTOR = 8


def draw_prefix_key_cache(key, part):
    first = jax.random.fold_in(jax.random.fold_in(key, 11), 0)
    array_shape = (PREFIX_TOTAL, CONTEXT_LENGTH, KEY_VALUE_HEADS * HEAD_WIDTH)
    base = jnp.clip(2.0 * jax.random.normal(first, array_shape, jnp.float32), -12.0, 12.0)
    return base.astype(jnp.bfloat16)


def draw_prefix_length(key, part):
    drawn = jax.random.randint(jax.random.fold_in(key, 23), (LEAF_TOTAL,), 1, CONTEXT_LENGTH + 1, dtype=jnp.int32)
    return drawn.at[::LEAF_PER_ACTOR].set(CONTEXT_LENGTH)


def shared_signs(key):
    flipped = jax.random.bernoulli(jax.random.fold_in(key, 31), 0.5, (KEY_VALUE_HEADS, HEAD_WIDTH))
    return jnp.where(flipped, 1.0, -1.0).astype(jnp.float32)


def draw_q_bias(key, part):
    sign_table = shared_signs(key)
    magnitude = jax.random.uniform(jax.random.fold_in(key, 37), (QUERY_HEADS, HEAD_WIDTH), jnp.float32, 0.5, 1.5)
    spread_signs = jnp.repeat(sign_table, QUERY_HEADS // KEY_VALUE_HEADS, axis=0)
    return (spread_signs * magnitude).reshape(QUERY_HEADS * HEAD_WIDTH).astype(jnp.bfloat16)


def draw_key_bias(key, part):
    sign_table = shared_signs(key)
    magnitude = jax.random.uniform(jax.random.fold_in(key, 41), (KEY_VALUE_HEADS, HEAD_WIDTH), jnp.float32, 0.5, 1.5)
    return (sign_table * magnitude).reshape(KEY_VALUE_HEADS * HEAD_WIDTH).astype(jnp.bfloat16)


def touch_ends(result, own_key, smallest, top_value):
    dims = result.shape
    index_at = [jax.random.randint(jax.random.fold_in(own_key, axis), (), 0, dims[axis]) for axis in range(len(dims))]
    result = result.at[tuple(index_at)].set(smallest)
    longest = dims.index(max(dims))
    index_at[longest] = (index_at[longest] + 1) % dims[longest]
    return result.at[tuple(index_at)].set(top_value)


def block_scale(rng, dims, cuts, least, largest):
    gain = 1.0
    for axis_at, shards_of in cuts:
        draws = jax.random.uniform(jax.random.fold_in(jax.random.fold_in(rng, 6), axis_at), (shards_of,), jnp.float32, least / len(cuts), largest / len(cuts))
        gain = gain * jnp.repeat(jnp.exp(draws), dims[axis_at] // shards_of).reshape((-1,) + (1,) * (len(dims) - 1 - axis_at))
    return gain


def noise(key, dims, scale, reach, cuts=(), kind=jnp.bfloat16):
    factor_of = block_scale(key, dims, cuts, -0.22, 0.18) if cuts else 1.0
    values = jax.random.normal(key, dims, jnp.float32) * scale * factor_of
    return jnp.minimum(jnp.maximum(values, -reach), reach).astype(kind)


def setup_inputs(seed: int = 0, part: int = 0) -> dict:
    key_list = jax.random.split(jax.random.key(seed), 18)
    part_splits = jax.random.split(jax.random.fold_in(key_list[17], part), 18)
    leaf_states = noise(part_splits[0], (LEAF_TOTAL, MODEL_WIDTH), 1.0, 6.0, ((0, 8),))
    norm_gain = jnp.clip(1.0 + 0.15 * jax.random.normal(key_list[1], (MODEL_WIDTH,), jnp.float32), 0.25, 1.75).astype(jnp.bfloat16)
    wq_quant = noise(key_list[2], (MODEL_WIDTH, QUERY_HEADS * HEAD_WIDTH), 1.0, 4.0, ((0, 8), (1, 2)))
    wq_scale = jnp.clip(jnp.exp(math.log(0.02795085) - 1.3862944 * jax.random.uniform(key_list[3], (MODEL_WIDTH // SCALE_BLOCK, QUERY_HEADS * HEAD_WIDTH // SCALE_BLOCK), jnp.float32) ** block_scale(key_list[3], (MODEL_WIDTH // SCALE_BLOCK, QUERY_HEADS * HEAD_WIDTH // SCALE_BLOCK), ((1, 2),), -0.2, 0.2)), 0.0069877123, 0.02795085)
    key_weight_quantized = noise(key_list[4], (MODEL_WIDTH, KEY_VALUE_HEADS * HEAD_WIDTH), 1.0, 4.0, ((0, 8), (1, 2)))
    key_weight_scale = jnp.clip(jnp.exp(math.log(0.02795085) - 1.3862944 * jax.random.uniform(key_list[5], (MODEL_WIDTH // SCALE_BLOCK, KEY_VALUE_HEADS * HEAD_WIDTH // SCALE_BLOCK), jnp.float32) ** block_scale(key_list[5], (MODEL_WIDTH // SCALE_BLOCK, KEY_VALUE_HEADS * HEAD_WIDTH // SCALE_BLOCK), ((1, 2),), -0.2, 0.2)), 0.0069877123, 0.02795085)
    value_weight_quantized = noise(key_list[6], (MODEL_WIDTH, KEY_VALUE_HEADS * HEAD_WIDTH), 1.0, 4.0, ((0, 8), (1, 2)))
    value_weight_scale = jnp.clip(jnp.exp(math.log(0.02795085) - 1.3862944 * jax.random.uniform(key_list[7], (MODEL_WIDTH // SCALE_BLOCK, KEY_VALUE_HEADS * HEAD_WIDTH // SCALE_BLOCK), jnp.float32) ** block_scale(key_list[7], (MODEL_WIDTH // SCALE_BLOCK, KEY_VALUE_HEADS * HEAD_WIDTH // SCALE_BLOCK), ((1, 2),), -0.2, 0.2)), 0.0069877123, 0.02795085)
    wo_quant = noise(key_list[8], (QUERY_HEADS * HEAD_WIDTH, MODEL_WIDTH), 1.0, 4.0, ((0, 2), (1, 8)))
    wo_scale = jnp.clip(jnp.exp(math.log(0.07905694) - 1.3862944 * jax.random.uniform(key_list[9], (QUERY_HEADS * HEAD_WIDTH // SCALE_BLOCK, MODEL_WIDTH // SCALE_BLOCK), jnp.float32) ** block_scale(key_list[9], (QUERY_HEADS * HEAD_WIDTH // SCALE_BLOCK, MODEL_WIDTH // SCALE_BLOCK), ((0, 2),), -0.2, 0.2)), 0.019764235, 0.07905694)
    q_bias = draw_q_bias(jax.random.fold_in(key_list[17], 71), part)
    key_bias = draw_key_bias(jax.random.fold_in(key_list[17], 71), part)
    value_bias = noise(key_list[12], (KEY_VALUE_HEADS * HEAD_WIDTH,), 1.0, 3.0, ((0, 2),))
    prefix_key_cache = draw_prefix_key_cache(jax.random.fold_in(jax.random.fold_in(key_list[17], part), 71), part)
    prefix_value_cache = noise(part_splits[14], (PREFIX_TOTAL, CONTEXT_LENGTH, KEY_VALUE_HEADS * HEAD_WIDTH), 3.0, 15.0, ((0, 8), (2, 2)))
    parent_prefix_slot = touch_ends(jax.random.randint(part_splits[15], (LEAF_TOTAL,), 0, PREFIX_PER_ACTOR), jax.random.fold_in(part_splits[15], 1), 0, PREFIX_PER_ACTOR - 1).astype(jnp.int32)
    prefix_length = draw_prefix_length(jax.random.fold_in(jax.random.fold_in(key_list[17], part), 71), part)
    return {"leaf_states": leaf_states, "norm_gain": norm_gain, "wq_quant": wq_quant, "wq_scale": wq_scale, "key_weight_quantized": key_weight_quantized, "key_weight_scale": key_weight_scale, "value_weight_quantized": value_weight_quantized, "value_weight_scale": value_weight_scale, "wo_quant": wo_quant, "wo_scale": wo_scale, "q_bias": q_bias, "key_bias": key_bias, "value_bias": value_bias, "prefix_key_cache": prefix_key_cache, "prefix_value_cache": prefix_value_cache, "parent_prefix_slot": parent_prefix_slot, "prefix_length": prefix_length}


epsilon = 1e-06
rope_base = 1000000.0

def dequantize(quant, scale):
    expanded = jnp.repeat(jnp.repeat(scale, SCALE_BLOCK, axis=0), SCALE_BLOCK, axis=1)
    return (quant.astype(jnp.float32) * expanded).astype(jnp.bfloat16)

def apply_rotary(values, length):
    width = values.shape[-1]
    half_width = width // 2
    freqs = rope_base ** (-(jnp.arange(half_width, dtype=jnp.float32) * 2.0 / width))
    angles = length.astype(jnp.float32)[:, None] * freqs[None, :]
    cosine = jnp.cos(angles)[:, None, :]
    sine = jnp.sin(angles)[:, None, :]
    first = values[..., :half_width]
    second = values[..., half_width:]
    return jnp.concatenate([first * cosine - second * sine, second * cosine + first * sine], axis=-1)

def attend_single_head(query_vector, key_self, value_self, prefix_key_cache, prefix_value_cache, parent, length):
    scale_factor = 1.0 / math.sqrt(query_vector.shape[-1])
    query_wide = query_vector.astype(jnp.float32)
    self_score = lax.optimization_barrier(jnp.sum(query_wide * key_self.astype(jnp.float32)[:, None, :], axis=-1)) * scale_factor
    visible = (jnp.arange(prefix_key_cache.shape[1])[None, :] < length[:, None])[:, None, :]
    outcome = jnp.zeros(query_vector.shape, jnp.float32)
    for prefix_index in range(prefix_key_cache.shape[0]):
        scores = jnp.einsum('lge,ce->lgc', query_wide, prefix_key_cache[prefix_index].astype(jnp.float32)) * scale_factor
        highest = jnp.maximum(lax.optimization_barrier(jnp.max(jnp.where(visible, scores, -jnp.inf), axis=-1)), self_score)
        weights = jnp.where(visible, jnp.exp(scores - highest[..., None]), 0.0)
        self_weight = jnp.exp(self_score - highest)
        total = lax.optimization_barrier(jnp.sum(weights, axis=-1)) + self_weight
        rounded = lax.optimization_barrier(weights.astype(jnp.bfloat16)).astype(jnp.float32)
        self_rounded = lax.optimization_barrier(self_weight.astype(jnp.bfloat16)).astype(jnp.float32)
        mixed = jnp.einsum('lgc,ce->lge', rounded, prefix_value_cache[prefix_index].astype(jnp.float32))
        mixed = mixed + self_rounded[..., None] * value_self.astype(jnp.float32)[:, None, :]
        outcome = jnp.where((parent == prefix_index)[:, None, None], mixed / total[..., None], outcome)
    return outcome

def reference(leaf_states, norm_gain, wq_quant, wq_scale, key_weight_quantized, key_weight_scale, value_weight_quantized, value_weight_scale, wo_quant, wo_scale, q_bias, key_bias, value_bias, prefix_key_cache, prefix_value_cache, parent_prefix_slot, prefix_length):
    states = leaf_states.astype(jnp.float32)
    normed = (states * lax.rsqrt(lax.optimization_barrier(jnp.mean(states * states, axis=-1, keepdims=True)) + epsilon) * norm_gain.astype(jnp.float32)).astype(jnp.bfloat16)
    query_vector = jnp.dot(normed, dequantize(wq_quant, wq_scale), preferred_element_type=jnp.float32) + q_bias.astype(jnp.float32)
    fresh_key = jnp.dot(normed, dequantize(key_weight_quantized, key_weight_scale), preferred_element_type=jnp.float32) + key_bias.astype(jnp.float32)
    fresh_value = jnp.dot(normed, dequantize(value_weight_quantized, value_weight_scale), preferred_element_type=jnp.float32) + value_bias.astype(jnp.float32)
    query_vector = apply_rotary(query_vector.reshape(LEAF_TOTAL, QUERY_HEADS, HEAD_WIDTH), prefix_length).astype(jnp.bfloat16)
    fresh_key = apply_rotary(fresh_key.reshape(LEAF_TOTAL, KEY_VALUE_HEADS, HEAD_WIDTH), prefix_length).astype(jnp.bfloat16)
    fresh_value = fresh_value.reshape(LEAF_TOTAL, KEY_VALUE_HEADS, HEAD_WIDTH).astype(jnp.bfloat16)
    query_group = QUERY_HEADS // KEY_VALUE_HEADS
    block_grid = (query_vector.reshape(N_ACTOR, LEAF_PER_ACTOR, KEY_VALUE_HEADS, query_group, HEAD_WIDTH), fresh_key.reshape(N_ACTOR, LEAF_PER_ACTOR, KEY_VALUE_HEADS, HEAD_WIDTH), fresh_value.reshape(N_ACTOR, LEAF_PER_ACTOR, KEY_VALUE_HEADS, HEAD_WIDTH), prefix_key_cache.reshape(N_ACTOR, PREFIX_PER_ACTOR, CONTEXT_LENGTH, KEY_VALUE_HEADS, HEAD_WIDTH), prefix_value_cache.reshape(N_ACTOR, PREFIX_PER_ACTOR, CONTEXT_LENGTH, KEY_VALUE_HEADS, HEAD_WIDTH), parent_prefix_slot.reshape(N_ACTOR, LEAF_PER_ACTOR), prefix_length.reshape(N_ACTOR, LEAF_PER_ACTOR))

    def one_block(pieces):
        query_rows, leaf_key_rows, leaf_value_rows, cached_key_rows, cached_value_rows, parent_indices, visible_lengths = pieces
        head_list = [attend_single_head(query_rows[:, head_number], leaf_key_rows[:, head_number], leaf_value_rows[:, head_number], cached_key_rows[:, :, head_number], cached_value_rows[:, :, head_number], parent_indices, visible_lengths) for head_number in range(KEY_VALUE_HEADS)]
        return jnp.stack(head_list, axis=1)
    attended = lax.map(one_block, block_grid).reshape(LEAF_TOTAL, QUERY_HEADS * HEAD_WIDTH).astype(jnp.bfloat16)
    return jnp.dot(attended, dequantize(wo_quant, wo_scale), preferred_element_type=jnp.float32).astype(jnp.bfloat16)
```

```python
import functools
import math

import jax
import jax.numpy as jnp
from jax import lax
from jax.experimental import pallas as pl
from jax.experimental.pallas import tpu as pltpu
from jax.sharding import PartitionSpec as P

HEAD_WIDTH = 128
SCALE_BLOCK = 128


epsilon = 1e-06
rope_base = 1000000.0


def apply_rotary(values, length):
    width = values.shape[-1]
    half_width = width // 2
    freqs = rope_base ** (-(jnp.arange(half_width, dtype=jnp.float32) * 2.0 / width))
    angles = length.astype(jnp.float32)[:, None] * freqs[None, :]
    cosine = jnp.cos(angles)[:, None, :]
    sine = jnp.sin(angles)[:, None, :]
    first = values[..., :half_width]
    second = values[..., half_width:]
    return jnp.concatenate(
        [first * cosine - second * sine, second * cosine + first * sine], axis=-1
    )


def attend_single_head(
    query_vector, key_self, value_self, prefix_key_cache, prefix_value_cache, parent, length
):
    scale_factor = 1.0 / math.sqrt(query_vector.shape[-1])
    self_score = (
        jnp.sum(
            query_vector.astype(jnp.float32) * key_self.astype(jnp.float32)[:, None, :], axis=-1
        )
        * scale_factor
    )
    visible = (jnp.arange(prefix_key_cache.shape[1])[None, :] < length[:, None])[:, None, :]
    outcome = jnp.zeros(query_vector.shape, jnp.float32)
    for prefix_index in range(prefix_key_cache.shape[0]):
        scores = (
            jnp.einsum(
                "lge,ce->lgc",
                query_vector,
                prefix_key_cache[prefix_index],
                preferred_element_type=jnp.float32,
            )
            * scale_factor
        )
        highest = jnp.maximum(jnp.max(jnp.where(visible, scores, -jnp.inf), axis=-1), self_score)
        weights = jnp.where(visible, jnp.exp(scores - highest[..., None]), 0.0)
        self_weight = jnp.exp(self_score - highest)
        total = jnp.sum(weights, axis=-1) + self_weight
        self_rounded = lax.optimization_barrier(self_weight.astype(jnp.bfloat16)).astype(
            jnp.float32
        )
        mixed = jnp.einsum(
            "lgc,ce->lge",
            weights.astype(jnp.bfloat16),
            prefix_value_cache[prefix_index],
            preferred_element_type=jnp.float32,
        )
        mixed = mixed + self_rounded[..., None] * value_self.astype(jnp.float32)[:, None, :]
        outcome = jnp.where(
            (parent == prefix_index)[:, None, None], mixed / total[..., None], outcome
        )
    return outcome


PIECE = 5
EARLY = 1


def spread_kernel(
    n_actor,
    rows_each,
    mine_ref,
    row_ref,
    gain_ref,
    sums_ref,
    all_ref,
    raw_ref,
    x_ref,
    home_sem,
    send_sem,
    recv_sem,
    row_sem,
):
    line = n_actor // 2
    actor = lax.axis_index("actor")
    job = lax.axis_index("job")
    at, y = actor // 2, actor % 2
    partner = job + 1 - 2 * (job % 2)
    pair = at * 2 + 1 - y
    has_up, has_down = at + 1 < line, at >= 1
    count = row_ref.shape[0]
    depth = mine_ref.shape[0]
    barrier = pltpu.get_barrier_semaphore()

    @pl.when(has_up)
    def _():
        pl.semaphore_signal(barrier, inc=1, device_id={"actor": actor + 2})

    @pl.when(has_down)
    def _():
        pl.semaphore_signal(barrier, inc=1, device_id={"actor": actor - 2})

    pl.semaphore_signal(barrier, inc=1, device_id={"actor": pair})
    pl.semaphore_signal(barrier, inc=1, device_id={"job": partner})
    pl.semaphore_wait(barrier, 2 + has_up.astype(jnp.int32) + has_down.astype(jnp.int32))

    def send(stream, source, piece, target, own=False):
        cut = pl.ds(piece * rows_each, rows_each)
        return pltpu.make_async_remote_copy(
            src_ref=mine_ref.at[cut] if own else all_ref.at[source, cut],
            dst_ref=all_ref.at[source, cut],
            send_sem=send_sem.at[stream, source, piece],
            recv_sem=recv_sem.at[source, piece],
            device_id={"actor": target},
        )

    def cross(source, piece, own=False):
        return send(0, source, piece, pair, own)

    def up(source, piece, own=False):
        return send(1, source, piece, actor + 2, own)

    def down(source, piece, own=False):
        return send(2, source, piece, actor - 2, own)

    def arrived(source, piece):
        cross(source, piece).wait_recv()

    late = list(range(PIECE - EARLY))
    early = list(range(PIECE - EARLY, PIECE))
    rows_copy = pltpu.make_async_remote_copy(
        src_ref=row_ref,
        dst_ref=raw_ref.at[pl.ds(count, count)],
        send_sem=row_sem.at[0],
        recv_sem=row_sem.at[1],
        device_id={"job": partner},
    )

    def both_ways(source, piece, own=False):
        @pl.when(has_up)
        def _():
            up(source, piece, own).start()

        @pl.when(has_down)
        def _():
            down(source, piece, own).start()

    for piece in early:
        cross(actor, piece, True).start()
    for piece in late:
        both_ways(actor, piece, True)
        cross(actor, piece, True).start()
    for piece in early:
        both_ways(actor, piece, True)
    rows_copy.start()
    home = pltpu.make_async_copy(mine_ref, all_ref.at[actor], home_sem.at[0])
    home.start()
    own_rows = pltpu.make_async_copy(row_ref, raw_ref.at[pl.ds(0, count)], home_sem.at[1])
    own_rows.start()

    def normalize(first):
        def block(i, carry):
            cut = pl.ds(pl.multiple_of(first + i * 16, 16), 16)
            rows = raw_ref[cut, :].astype(jnp.float32)
            rows = rows * lax.rsqrt(jnp.mean(rows * rows, axis=-1, keepdims=True) + epsilon)
            rows = (rows * gain_ref[...].astype(jnp.float32)).astype(jnp.bfloat16)
            for source in range(n_actor):
                x_ref[source, cut, :] = rows[:, source * depth : (source + 1) * depth]
            return carry

        lax.fori_loop(0, count // 16, block, 0)

    def add(source):
        sums_ref[...] += jnp.dot(
            x_ref[source], all_ref[source], preferred_element_type=jnp.float32
        )

    sums_ref[...] = jnp.zeros_like(sums_ref)
    own_rows.wait()
    normalize(0)
    for piece in early:
        arrived(pair, piece)
        both_ways(pair, piece)
    turn = jnp.where(at * 2 < line, 1, line - 1)

    def spot_of(k):
        return lax.rem(at + k * turn, line)

    for far in range(1, line):
        if far == line - 1:
            rows_copy.wait()
            normalize(count)
            home.wait()
            add(actor)
        todo = [(y, p) for p in late] + [(y, p) for p in early] + [(1 - y, p) for p in early]
        for index, (which, piece) in enumerate(todo):
            below = (at - far) * 2 + which
            above = (at + far) * 2 + which

            @pl.when(at >= far)
            def _():
                arrived(below, piece)

                @pl.when(has_up)
                def _():
                    up(below, piece).start()

                if index < len(late):
                    cross(below, piece).start()

            @pl.when(at + far < line)
            def _():
                arrived(above, piece)

                @pl.when(has_down)
                def _():
                    down(above, piece).start()

                if index < len(late):
                    cross(above, piece).start()

    def add_held(k, carry):
        add(spot_of(k) * 2 + y)
        return carry

    lax.fori_loop(1, line, add_held, 0)

    def add_crossed(k, carry):
        source = spot_of(k) * 2 + 1 - y
        for piece in late:
            arrived(source, piece)
        add(source)
        return carry

    lax.fori_loop(0, line, add_crossed, 0)
    for spot in range(line):
        for piece in late:
            cross(spot * 2 + y, piece).wait_send()
    for piece in early:
        cross(actor, piece).wait_send()
    for spot in range(line):
        items = [(y, p) for p in range(PIECE)] + [(1 - y, p) for p in early]
        for which, piece in items:
            source = spot * 2 + which

            @pl.when(jnp.logical_and(has_up, at >= spot))
            def _():
                up(source, piece).wait_send()

            @pl.when(jnp.logical_and(has_down, at <= spot))
            def _():
                down(source, piece).wait_send()


def spread(shard, rows, gain, n_actor):
    height, width = shard.shape
    return pl.pallas_call(
        functools.partial(spread_kernel, n_actor, height // PIECE),
        out_shape=jax.ShapeDtypeStruct((2 * rows.shape[0], width), jnp.float32),
        in_specs=[
            pl.BlockSpec(memory_space=pl.ANY),
            pl.BlockSpec(memory_space=pl.ANY),
            pl.BlockSpec(memory_space=pltpu.VMEM),
        ],
        out_specs=pl.BlockSpec(memory_space=pltpu.VMEM),
        scratch_shapes=[
            pltpu.VMEM((n_actor,) + shard.shape, shard.dtype),
            pltpu.VMEM((2 * rows.shape[0], rows.shape[1]), rows.dtype),
            pltpu.VMEM((n_actor, 2 * rows.shape[0], height), rows.dtype),
            pltpu.SemaphoreType.DMA((2,)),
            pltpu.SemaphoreType.DMA((3, n_actor, PIECE)),
            pltpu.SemaphoreType.DMA((n_actor, PIECE)),
            pltpu.SemaphoreType.DMA((2,)),
        ],
        compiler_params=pltpu.CompilerParams(
            collective_id=0, has_side_effects=True, vmem_limit_bytes=48 * 1024 * 1024
        ),
        cost_estimate=pl.CostEstimate(
            flops=0, bytes_accessed=300_000_000, transcendentals=0
        ),
    )(shard, rows, gain)


def per_device(
    mesh_sizes,
    leaf_states,
    norm_gain,
    wq_quant,
    wq_scale,
    key_weight_quantized,
    key_weight_scale,
    value_weight_quantized,
    value_weight_scale,
    wo_quant,
    wo_scale,
    q_bias,
    key_bias,
    value_bias,
    prefix_key_cache,
    prefix_value_cache,
    parent_prefix_slot,
    prefix_length,
):
    n_job, n_actor = mesh_sizes
    swap = [(i, i ^ 1) for i in range(n_job)]
    side = lax.axis_index("job") % 2
    actor = lax.axis_index("actor")

    def trade(x):
        return lax.ppermute(x, "job", swap)

    leaf_count = leaf_states.shape[0]

    def half_cols(x):
        width = x.shape[1] // 2
        return lax.dynamic_slice_in_dim(x, side * width, width, 1)

    row_count = wq_quant.shape[0]

    def expand_rows(quant, scale):
        mine = lax.dynamic_slice_in_dim(
            scale, actor * (row_count // SCALE_BLOCK), row_count // SCALE_BLOCK, 0
        ) if row_count % SCALE_BLOCK == 0 else None
        if mine is None:
            tall = jnp.repeat(scale, SCALE_BLOCK, axis=0)
            tall = lax.dynamic_slice_in_dim(tall, actor * row_count, row_count, 0)
        else:
            tall = jnp.repeat(mine, SCALE_BLOCK, axis=0)
        wide = jnp.repeat(half_cols(tall), SCALE_BLOCK, axis=1)
        return (half_cols(quant).astype(jnp.float32) * wide).astype(jnp.bfloat16)

    qkv_local = jnp.concatenate(
        [
            expand_rows(wq_quant, wq_scale),
            expand_rows(key_weight_quantized, key_weight_scale),
            expand_rows(value_weight_quantized, value_weight_scale),
        ],
        axis=1,
    )
    col_count = wo_quant.shape[1]
    spread_scale = jnp.repeat(wo_scale, SCALE_BLOCK, axis=1)
    own_scale = half_cols(lax.dynamic_slice_in_dim(spread_scale, actor * col_count, col_count, 1))
    wo_local = (
        half_cols(wo_quant).astype(jnp.float32) * jnp.repeat(own_scale, SCALE_BLOCK, axis=0)
    ).astype(jnp.bfloat16).T
    sums = spread(qkv_local, leaf_states, norm_gain[None, :], n_actor)
    wo_local, sums, prefix_length = lax.optimization_barrier((wo_local, sums, prefix_length))
    both_length = jnp.concatenate([prefix_length, trade(prefix_length)], axis=0)

    def half_row(x):
        width = x.shape[0] // 2
        return lax.dynamic_slice_in_dim(x, side * width, width, 0)

    bias = jnp.concatenate([half_row(q_bias), half_row(key_bias), half_row(value_bias)])
    sums = sums + bias.astype(jnp.float32)
    v_width = value_bias.shape[0] // 2
    rot_width = sums.shape[1] - v_width
    rotated = apply_rotary(
        sums[:, :rot_width].reshape(2 * leaf_count, rot_width // HEAD_WIDTH, HEAD_WIDTH),
        both_length,
    ).reshape(2 * leaf_count, rot_width)
    done = jnp.concatenate([rotated, sums[:, rot_width:]], axis=1).astype(jnp.bfloat16)
    own = done[:leaf_count]
    other = trade(done[leaf_count:])
    q_width = q_bias.shape[0] // 2

    kv_half = v_width // HEAD_WIDTH
    query_group = q_bias.shape[0] // key_bias.shape[0]
    outs = []
    for which, block in ((side, own), (1 - side, other)):
        q = block[:, :q_width].reshape(leaf_count, kv_half, query_group, HEAD_WIDTH)
        k = block[:, q_width : q_width + v_width].reshape(leaf_count, kv_half, HEAD_WIDTH)
        v = block[:, q_width + v_width :].reshape(leaf_count, kv_half, HEAD_WIDTH)
        for head in range(kv_half):
            at = (which * kv_half + head) * HEAD_WIDTH
            outs.append(
                attend_single_head(
                    q[:, head],
                    k[:, head],
                    v[:, head],
                    lax.dynamic_slice_in_dim(prefix_key_cache, at, HEAD_WIDTH, 2),
                    lax.dynamic_slice_in_dim(prefix_value_cache, at, HEAD_WIDTH, 2),
                    parent_prefix_slot,
                    prefix_length,
                )
                .reshape(leaf_count, query_group * HEAD_WIDTH)
                .astype(jnp.bfloat16)
            )
    mine = jnp.concatenate(outs[:kv_half], axis=1)
    theirs = jnp.concatenate(outs[kv_half:], axis=1)
    attended = jnp.where(
        side == 0,
        jnp.concatenate([mine, theirs], axis=1),
        jnp.concatenate([theirs, mine], axis=1),
    )

    wo_all = lax.all_gather(wo_local, "actor", axis=0, tiled=True)
    group = lax.axis_index("tp")
    cores = [(0, 1), (1, 0)]

    def project(rows):
        part = lax.dot_general(
            rows, wo_all, (((1,), (1,)), ((), ())), preferred_element_type=jnp.float32
        )
        width = part.shape[1] // 2
        first, second = part[:, :width], part[:, width:]
        give = jnp.where(group == 0, second, first)
        keep = jnp.where(group == 0, first, second)
        return (keep + lax.ppermute(give, "tp", cores)).astype(jnp.bfloat16), give

    def join(x):
        y = lax.ppermute(x, "tp", cores)
        return jnp.where(
            group == 0,
            jnp.concatenate([x, y], axis=1),
            jnp.concatenate([y, x], axis=1),
        )

    away, marker = project(trade(attended))
    attended, away, _ = lax.optimization_barrier((attended, away, marker))
    away = trade(away)
    local = join(project(attended)[0])
    remote = join(away)
    low = jnp.where(side == 0, local, remote)
    high = jnp.where(side == 0, remote, local)
    pieces = []
    half = col_count // 2
    for a in range(n_actor):
        pieces += [low[:, a * half : (a + 1) * half], high[:, a * half : (a + 1) * half]]
    return jnp.concatenate(pieces, axis=1)


LANES = 128


def fused_kernel(
    n_actor,
    states_ref,
    gain_ref,
    wq_ref,
    wq_scale_ref,
    wk_ref,
    wk_scale_ref,
    wv_ref,
    wv_scale_ref,
    wo_ref,
    wo_scale_ref,
    qb_ref,
    kb_ref,
    vb_ref,
    kcache_ref,
    vcache_ref,
    parent_ref,
    length_ref,
    table_ref,
    out_ref,
    raw_ref,
    rawv_ref,
    wown_ref,
    woth_ref,
    give_ref,
    xraw_ref,
    xs_ref,
    tabs_ref,
    acc_ref,
    rst_ref,
    vst_ref,
    rq_ref,
    rv_ref,
    kc_ref,
    vc_ref,
    woraw_ref,
    zset_ref,
    yset_ref,
    att_ref,
    psend_ref,
    precv_ref,
    res_ref,
    load_sem,
    kv_sem,
    z_send,
    z_recv,
    g_send,
    x_send,
    x_recv,
    xs_send,
    xs_recv,
    t_send,
    t_recv,
    q_send,
    q_recv,
    v_send,
    v_recv,
    a_send,
    a_recv,
    oz_send,
    oz_recv,
    oy_send,
    oy_recv,
    oc_send,
    p_send,
    p_recv,
    l_sem,
    s_send,
    s_recv,
    c_send,
    c_recv,
    f_send,
    f_recv,
):
    line = n_actor // 2
    actor = lax.axis_index("actor")
    job = lax.axis_index("job")
    core = lax.axis_index("tp")
    at, y = actor // 2, actor % 2
    side = job % 2
    there = {"job": job + 1 - 2 * side}
    pair = {"actor": at * 2 + 1 - y}
    diagonal = {"job": job + 1 - 2 * side, "actor": at * 2 + 1 - y}
    sibling = {"tp": 1 - core}
    above, below = {"actor": actor + 2}, {"actor": actor - 2}
    has_up, has_down = at + 1 < line, at >= 1
    even = (y + side) % 2 == 0
    odd = (y + side) % 2 == 1
    rows = raw_ref.shape[1]
    count = xraw_ref.shape[0]
    half_rows = rows // 2
    half_count = count // 2
    width = raw_ref.shape[2]
    units = width // LANES
    heads = 2 * units - 1
    depth = zset_ref.shape[1]
    strips = n_actor // 2
    part = strips // 2
    f32, bf16 = jnp.float32, jnp.bfloat16

    def lanes(unit, n=1):
        return pl.ds(pl.multiple_of(unit * LANES, LANES), n * LANES)

    barrier = pltpu.get_barrier_semaphore()

    @pl.when(has_up)
    def _():
        pl.semaphore_signal(barrier, inc=1, device_id=above)

    @pl.when(has_down)
    def _():
        pl.semaphore_signal(barrier, inc=1, device_id=below)

    for peer in (there, pair, diagonal, sibling):
        pl.semaphore_signal(barrier, inc=1, device_id=peer)

    def local(source, target, sem):
        return pltpu.make_async_copy(source, target, sem)

    def remote(source, target, ss, rs, peer):
        return pltpu.make_async_remote_copy(
            src_ref=source, dst_ref=target, send_sem=ss, recv_sem=rs, device_id=peer
        )

    first_of = lambda parity, s: s * (3 - parity)
    first = first_of(y, side)
    w_loads = [
        local(wq_ref.at[:, lanes(side * heads, units)], raw_ref.at[0], load_sem.at[0]),
        local(
            wq_ref.at[:, lanes(side * heads + units, units - 1)],
            raw_ref.at[1, :, pl.ds(0, (units - 1) * LANES)],
            load_sem.at[1],
        ),
        local(
            wk_ref.at[:, lanes(side)],
            raw_ref.at[1, :, pl.ds((units - 1) * LANES, LANES)],
            load_sem.at[2],
        ),
        local(wv_ref.at[:, lanes(side)], rawv_ref, load_sem.at[3]),
    ]
    state_load = local(states_ref, xraw_ref, load_sem.at[4])
    wo_load = local(
        wo_ref.at[:, lanes(first, 2)], woraw_ref.at[:, pl.ds(0, 2 * LANES)], load_sem.at[5]
    )
    wo_load_last = local(
        wo_ref.at[:, lanes(first + 2 * (1 - (y + side) % 2), 1)],
        woraw_ref.at[:, pl.ds(2 * LANES, LANES)],
        load_sem.at[6],
    )
    for copy in w_loads:
        copy.start()
    state_load.start()
    wo_load.start()
    wo_load_last.start()
    kv_loads = []
    for j in range(2):
        for p in range(2):
            place = pl.ds(p * LANES, LANES)
            cut = pl.ds(j * LANES, LANES)
            kv_loads.append(
                local(kcache_ref.at[p, :, cut], kc_ref.at[j, :, place], kv_sem.at[0, j, p])
            )
            kv_loads.append(
                local(vcache_ref.at[p, :, cut], vc_ref.at[j, :, place], kv_sem.at[1, j, p])
            )
    for copy in kv_loads:
        copy.start()

    blocks = rows // SCALE_BLOCK

    def unit_scale(parity, block, u):
        row = actor * blocks + block
        plain = wq_scale_ref[row, side * heads + u + (units * parity if u < units - 1 else 0)]
        if u < units - 1:
            return plain
        return jnp.where(parity == 0, plain, wk_scale_ref[row, side])

    def expand(parity, target):
        for block in range(blocks):
            cut = pl.ds(block * SCALE_BLOCK, SCALE_BLOCK)
            for u in range(units):
                lane = pl.ds(u * LANES, LANES)
                scaled = raw_ref[parity, cut, lane].astype(f32) * unit_scale(parity, block, u)
                target(cut, lane, scaled.astype(bf16))

    def to_give(cut, lane, value):
        give_ref[cut, lane] = value

    def to_own(cut, lane, value):
        wown_ref[at, cut, lane] = value

    for copy in w_loads:
        copy.wait()
    expand(1 - y, to_give)
    pl.semaphore_wait(barrier, 4 + has_up.astype(jnp.int32) + has_down.astype(jnp.int32))

    def half(p):
        return pl.ds(p * half_rows, half_rows)

    def give(p):
        return remote(
            give_ref.at[half(p)], woth_ref.at[at, half(p)], g_send.at[p], z_recv.at[1, at, p], pair
        )

    for p in range(2):
        give(p).start()
    expand(y, to_own)
    for block in range(blocks):
        cut = pl.ds(block * SCALE_BLOCK, SCALE_BLOCK)
        scale = wv_scale_ref[actor * blocks + block, side]
        wown_ref[at, cut, pl.ds(width, LANES)] = (rawv_ref[cut, :].astype(f32) * scale).astype(
            bf16
        )

    def up_down(way, kind, spot, p):
        ref = (wown_ref if kind == 0 else woth_ref).at[spot, half(p)]
        return remote(
            ref, ref, z_send.at[way, kind, spot, p], z_recv.at[kind, spot, p], (above, below)[way]
        )

    def both_ways(kind, spot, p):
        @pl.when(has_up)
        def _():
            up_down(0, kind, spot, p).start()

        @pl.when(has_down)
        def _():
            up_down(1, kind, spot, p).start()

    for p in range(2):
        both_ways(0, at, p)

    state_load.wait()

    def normalize(i, carry):
        cut = pl.ds(pl.multiple_of(i * 16, 16), 16)
        x = xraw_ref[cut, :].astype(f32)
        x = x * lax.rsqrt(jnp.mean(x * x, axis=-1, keepdims=True) + epsilon)
        x = (x * gain_ref[...].astype(f32)).astype(bf16)
        for source in range(n_actor):
            xs_ref[0, source, cut, :] = x[:, source * rows : (source + 1) * rows]
        return carry

    lax.fori_loop(0, count // 16, normalize, 0)

    def some(p):
        return pl.ds(core * strips + p * part, part)

    def share(slot, p, origin, peer):
        return remote(
            xs_ref.at[origin, some(p)],
            xs_ref.at[slot, some(p)],
            x_send.at[slot - 1, p],
            x_recv.at[slot - 1, p],
            peer,
        )

    share_list = [
        share(1, 0, 0, there),
        share(2, 1, 0, pair),
        share(1, 1, 0, there),
        share(2, 0, 0, pair),
    ]
    for copy in share_list:
        copy.start()

    def to_sibling(slot, p):
        ref = xs_ref.at[slot, some(p)]
        return remote(ref, ref, xs_send.at[slot - 1, p], xs_recv.at[slot - 1, p], sibling)

    def from_sibling(slot, p):
        ref = xs_ref.at[slot, pl.ds((1 - core) * strips + p * part, part)]
        return remote(ref, ref, xs_send.at[slot - 1, p], xs_recv.at[slot - 1, p], sibling)

    table_sends = [
        remote(table_ref, tabs_ref.at[slot], t_send.at[slot], t_recv.at[slot], peer)
        for slot, peer in ((1, there), (2, pair), (3, diagonal))
    ]
    for copy in table_sends:
        copy.start()

    wo_load.wait()
    wo_load_last.wait()
    wo_blocks = depth // SCALE_BLOCK
    wo_units = wo_ref.shape[1] // LANES

    def expand_wo(block, carry):
        cut = pl.ds(pl.multiple_of(block * SCALE_BLOCK, SCALE_BLOCK), SCALE_BLOCK)
        for u in range(2):
            lane = pl.ds(u * LANES, LANES)
            scale = wo_scale_ref[block, actor * wo_units + first + u]
            zset_ref[at, cut, lane] = (woraw_ref[cut, lane].astype(f32) * scale).astype(bf16)
        return carry

    lax.fori_loop(0, wo_blocks, expand_wo, 0)

    def z_unit(spot, u):
        return zset_ref.at[spot, :, pl.ds(u * LANES, LANES)]

    cross_last = remote(z_unit(at, 2), z_unit(at, 2), oc_send.at[0], oz_recv.at[at, 2], pair)

    @pl.when(even)
    def _():
        def expand_last(block, carry):
            cut = pl.ds(pl.multiple_of(block * SCALE_BLOCK, SCALE_BLOCK), SCALE_BLOCK)
            lane = pl.ds(2 * LANES, LANES)
            scale = wo_scale_ref[block, actor * wo_units + first + 2]
            zset_ref[at, cut, lane] = (woraw_ref[cut, lane].astype(f32) * scale).astype(bf16)
            return carry

        lax.fori_loop(0, wo_blocks, expand_last, 0)
        cross_last.start()

    def wo_way(way, spot, u):
        ref = z_unit(spot, u)
        return remote(
            ref, ref, oz_send.at[way, spot, u], oz_recv.at[spot, u], (above, below)[way]
        )

    def wo_cross(spot, u):
        return remote(
            z_unit(spot, u),
            yset_ref.at[spot, :, pl.ds(u * LANES, LANES)],
            oy_send.at[spot, u],
            oy_recv.at[spot, u],
            pair,
        )

    def wo_begin(far):
        @pl.when(jnp.logical_and(at == far, has_up))
        def _():
            for u in range(2 if far < 2 else 3):
                wo_way(0, at, u).start()

        @pl.when(jnp.logical_and(line - 1 - at == far, has_down))
        def _():
            for u in range(2 if far < 2 else 3):
                wo_way(1, at, u).start()

    def wo_begin_last():
        @pl.when(odd)
        def _():
            cross_last.wait_recv()

        @pl.when(jnp.logical_and(at < 2, has_up))
        def _():
            wo_way(0, at, 2).start()

        @pl.when(jnp.logical_and(line - 1 - at < 2, has_down))
        def _():
            wo_way(1, at, 2).start()

    for p in range(2):
        give(p).wait_recv()
        both_ways(1, at, p)
    wo_begin(0)

    acc_ref[...] = jnp.zeros_like(acc_ref)

    def multiply(spot):
        def body(o, carry):
            acc_ref[o] += jnp.dot(
                xs_ref[o, spot * 2 + y], wown_ref[spot], preferred_element_type=f32
            )
            acc_ref[o, :, :width] += jnp.dot(
                xs_ref[o, spot * 2 + 1 - y], woth_ref[spot], preferred_element_type=f32
            )
            return carry

        lax.fori_loop(0, 4, body, 0)

    def multiply_far(far, carry):
        @pl.when(at >= far)
        def _():
            multiply(at - far)

        @pl.when(jnp.logical_and(at + far < line, far > 0))
        def _():
            multiply(at + far)

        return carry

    def rows_first():
        for slot, p, peer in ((1, 0, pair), (1, 1, None), (2, 1, there), (2, 0, None)):
            share(slot, p, 0, there if slot == 1 else pair).wait_recv()
            if peer is not None:
                share(3, p, slot, peer).start()
            to_sibling(slot, p).start()

    def rows_rest():
        for p in range(2):
            share(3, p, 1 + p, pair if p == 0 else there).wait_recv()
            to_sibling(3, p).start()
        for u in range(2):
            wo_cross(at, u).start()
        for slot in (1, 2, 3):
            for p in range(2):
                from_sibling(slot, p).wait_recv()

    for far in range(1, line):
        for kind in range(2):
            for p in range(2):

                @pl.when(at >= far)
                def _():
                    up_down(0, kind, at - far, p).wait_recv()

                    @pl.when(has_up)
                    def _():
                        up_down(0, kind, at - far, p).start()

                @pl.when(at + far < line)
                def _():
                    up_down(1, kind, at + far, p).wait_recv()

                    @pl.when(has_down)
                    def _():
                        up_down(1, kind, at + far, p).start()

        wo_begin(far)
        if far == 1:
            rows_first()
            wo_begin_last()
        if far == max(line - 2, 1):
            rows_rest()
            lax.fori_loop(0, max(line - 1, 1), multiply_far, 0)
    multiply_far(line - 1, 0)

    lane_at = lax.broadcasted_iota(jnp.int32, (count, LANES), 1)

    def results(slot):
        return (
            remote(rst_ref.at[slot], rq_ref.at[slot], q_send.at[slot], q_recv.at[slot], peers[slot]),
            remote(vst_ref.at[slot], rv_ref.at[slot], v_send.at[slot], v_recv.at[slot], peers[slot]),
        )

    peers = {1: there, 2: pair, 3: diagonal}
    for slot in (2, 3, 1, 0):
        if slot:
            table_sends[slot - 1].wait_recv()
            table = tabs_ref[slot]
        else:
            table = table_ref[...]
        swapped = pltpu.roll(table, LANES // 2, 1)
        cosine = jnp.where(lane_at < LANES // 2, table, swapped)
        sine = jnp.where(lane_at < LANES // 2, -swapped, table)
        for u in range(units):
            if u < units - 1:
                bias = qb_ref[:, lanes(side * heads + u + units * y)].astype(f32)
            else:
                bias = jnp.where(
                    y == 0,
                    qb_ref[:, lanes(side * heads + u)].astype(f32),
                    kb_ref[:, lanes(side)].astype(f32),
                )
            value = acc_ref[slot, :, u * LANES : (u + 1) * LANES] + bias
            value = value * cosine + pltpu.roll(value, LANES // 2, 1) * sine
            (rst_ref if slot else rq_ref)[slot, u] = value.astype(bf16)
        (vst_ref if slot else rv_ref)[slot] = acc_ref[slot, :, width:]
        if slot:
            for copy in results(slot):
                copy.start()

    for copy in kv_loads:
        copy.wait()
    parent = parent_ref[...]
    length = length_ref[...]
    in_first = (parent == 0).astype(f32)
    in_second = 1.0 - in_first
    scale_factor = 1.0 / math.sqrt(LANES)

    def hand(j):
        return remote(
            att_ref.at[0, j], att_ref.at[1, j], a_send.at[j], a_recv.at[j], there
        )

    def attend(base):
        group = side if base == 0 else 1 - side
        low = jnp.where(y == 0, base, base + 2)
        high = jnp.where(y == 0, base + 2, base)
        key_new = rq_ref[high, units - 1].astype(f32)
        value_new = rv_ref[base] + rv_ref[base + 2] + vb_ref[:, lanes(group)].astype(f32)
        value_new = value_new.astype(bf16).astype(f32)

        def head(h, carry):
            query = rq_ref[
                jnp.where(h < units, low, high), jnp.where(h < units, h, h - units)
            ].astype(f32)
            own = jnp.sum(query * key_new, axis=-1, keepdims=True) * scale_factor
            both = jnp.concatenate([query * in_first, query * in_second], axis=1).astype(bf16)
            scores = lax.dot_general(
                both, kc_ref[group], (((1,), (1,)), ((), ())), preferred_element_type=f32
            )
            place = lax.broadcasted_iota(jnp.int32, scores.shape, 1)
            scores = jnp.where(place < length, scores, -jnp.inf)
            highest = jnp.maximum(jnp.max(scores, axis=-1, keepdims=True) * scale_factor, own)
            weights = jnp.exp(scores * scale_factor - highest)
            own = jnp.exp(own - highest)
            total = jnp.sum(weights, axis=-1, keepdims=True) + own
            mixed = jnp.dot(weights.astype(bf16), vc_ref[group], preferred_element_type=f32)
            mixed = jnp.where(parent == 0, mixed[:, :LANES], mixed[:, LANES:])
            mixed = mixed + own.astype(bf16).astype(f32) * value_new
            att_ref[0, group, :, lanes(h)] = (mixed / total).astype(bf16)
            return carry

        lax.fori_loop(0, heads, head, 0)
        hand(group).start()

    for slot in (2,):
        for copy in results(slot):
            copy.wait_recv()
    attend(0)
    for slot in (1, 3):
        for copy in results(slot):
            copy.wait_recv()
    attend(1)

    def partial(spot, which):
        cut = pl.ds(pl.multiple_of(which * half_count, half_count), half_count)
        outs = []
        for o in range(2):
            z = y_part = None
            for j in range(2):
                block = att_ref[o, j, cut, :]
                deep = pl.ds(j * (depth // 2), depth // 2)
                z_more = jnp.dot(block, zset_ref[spot, deep, :], preferred_element_type=f32)
                y_more = jnp.dot(block, yset_ref[spot, deep, :], preferred_element_type=f32)
                z = z_more if z is None else z + z_more
                y_part = y_more if y_part is None else y_part + y_more
            outs.append((z, y_part))
        return outs

    def p_copy(spot):
        return remote(
            psend_ref.at[spot], precv_ref.at[spot], p_send.at[spot], p_recv.at[spot], sibling
        )

    def spots(s, spot):
        own_base = wo_units * (2 * spot + y) + first_of(y, s)
        oth_base = wo_units * (2 * spot + 1 - y) + first_of(1 - y, s)
        return (
            (0, 2, own_base),
            (2, 1, jnp.where((y + s) % 2 == 0, own_base + 2, oth_base + 2)),
            (3, 2, oth_base),
        )

    def mine(c):
        return pl.ds(pl.multiple_of(c * half_count, half_count), half_count)

    def home_copies(spot):
        return [
            local(
                res_ref.at[spot, 0, pl.ds(a, n)],
                out_ref.at[pl.ds(u, n), mine(core)],
                l_sem.at[spot, i],
            )
            for i, (a, n, u) in enumerate(spots(side, spot))
        ]

    def sibling_copies(spot):
        return [
            remote(
                res_ref.at[spot, 0, pl.ds(a, n)],
                out_ref.at[pl.ds(u, n), mine(core)],
                s_send.at[spot, i],
                s_recv.at[spot, i],
                sibling,
            )
            for i, (a, n, u) in enumerate(spots(side, spot))
        ]

    def there_copies(spot, s):
        return [
            remote(
                res_ref.at[spot, 1, pl.ds(a, n)],
                out_ref.at[pl.ds(u, n), mine(core)],
                c_send.at[spot, i],
                c_recv.at[spot, i],
                there,
            )
            for i, (a, n, u) in enumerate(spots(s, spot))
        ]

    def onward_copies(spot):
        return [
            remote(
                out_ref.at[pl.ds(u, n), mine(core)],
                out_ref.at[pl.ds(u, n), mine(core)],
                f_send.at[spot, i],
                f_recv.at[spot, i],
                sibling,
            )
            for i, (a, n, u) in enumerate(spots(1 - side, spot))
        ]

    z_width = zset_ref.shape[2]

    def project(spot):
        for u in range(2):
            wo_cross(spot, u).wait_recv()
        for o, (z, y_part) in enumerate(partial(spot, 1 - core)):
            psend_ref[spot, o, :, :z_width] = z
            psend_ref[spot, o, :, z_width:] = y_part
        p_copy(spot).start()
        kept = partial(spot, core)
        p_copy(spot).wait_recv()
        for o, (z, y_part) in enumerate(kept):
            z = z + precv_ref[spot, o, :, :z_width]
            y_part = y_part + precv_ref[spot, o, :, z_width:]
            for u in range(3):
                res_ref[spot, o, u] = z[:, u * LANES : (u + 1) * LANES].astype(bf16)
            for u in range(2):
                res_ref[spot, o, 3 + u] = y_part[:, u * LANES : (u + 1) * LANES].astype(bf16)
        for copy in there_copies(spot, side) + sibling_copies(spot) + home_copies(spot):
            copy.start()

    def onward(spot):
        for got, copy in zip(there_copies(spot, 1 - side), onward_copies(spot)):
            got.wait_recv()
            copy.start()

    def at_far(action, far):
        @pl.when(at >= far)
        def _():
            action(at - far)

        @pl.when(jnp.logical_and(at + far < line, far > 0))
        def _():
            action(at + far)

    def relay(far):
        for u in range(3):

            @pl.when(at >= far)
            def _():
                wo_way(0, at - far, u).wait_recv()

                @pl.when(has_up)
                def _():
                    wo_way(0, at - far, u).start()

                if u < 2:
                    wo_cross(at - far, u).start()

            @pl.when(at + far < line)
            def _():
                wo_way(1, at + far, u).wait_recv()

                @pl.when(has_down)
                def _():
                    wo_way(1, at + far, u).start()

                if u < 2:
                    wo_cross(at + far, u).start()

    for j in range(2):
        hand(j).wait_recv()

    def rounds(far, carry):
        @pl.when(far > 0)
        def _():
            relay(far)

        at_far(project, far)

        @pl.when(far > 0)
        def _():
            at_far(onward, far - 1)

        return carry

    lax.fori_loop(0, line, rounds, 0)
    at_far(onward, line - 1)

    for p in range(2):
        give(p).wait_send()
        for slot, peer in ((1, there), (2, pair), (3, pair)):
            share(slot, p, 0, peer).wait_send()
            to_sibling(slot, p).wait_send()
    for copy in table_sends:
        copy.wait_send()
    for slot in (1, 2, 3):
        for copy in results(slot):
            copy.wait_send()
    for j in range(2):
        hand(j).wait_send()

    @pl.when(even)
    def _():
        cross_last.wait_send()

    def finish(spot, carry):
        @pl.when(jnp.logical_and(has_up, at >= spot))
        def _():
            for kind in range(2):
                for p in range(2):
                    up_down(0, kind, spot, p).wait_send()
            for u in range(3):
                wo_way(0, spot, u).wait_send()

        @pl.when(jnp.logical_and(has_down, at <= spot))
        def _():
            for kind in range(2):
                for p in range(2):
                    up_down(1, kind, spot, p).wait_send()
            for u in range(3):
                wo_way(1, spot, u).wait_send()

        for u in range(2):
            wo_cross(spot, u).wait_send()
        p_copy(spot).wait_send()
        for copy in home_copies(spot):
            copy.wait()
        for copy in there_copies(spot, side):
            copy.wait_send()
        for copy in sibling_copies(spot) + onward_copies(spot):
            copy.wait()
        return carry

    lax.fori_loop(0, line, finish, 0)


def fused(n_actor, args, table):
    (
        leaf_states, norm_gain, wq_quant, wq_scale, wk, wk_scale, wv, wv_scale, wo_quant, wo_scale,
        q_bias, key_bias, value_bias, kcache, vcache, parent, length,
    ) = args
    count, features = leaf_states.shape
    rows = wq_quant.shape[0]
    heads = wq_quant.shape[1] // (2 * LANES)
    units = (heads + 1) // 2
    width = units * LANES
    context = kcache.shape[1]
    depth = wo_quant.shape[0]
    line = n_actor // 2
    total_units = n_actor * (wo_quant.shape[1] // LANES)
    bf16, f32 = jnp.bfloat16, jnp.float32
    any_space = pl.BlockSpec(memory_space=pl.ANY)
    vmem = pl.BlockSpec(memory_space=pltpu.VMEM)
    smem = pl.BlockSpec(memory_space=pltpu.SMEM)
    dma = pltpu.SemaphoreType.DMA
    return pl.pallas_call(
        functools.partial(fused_kernel, n_actor),
        out_shape=jax.ShapeDtypeStruct((total_units, count, LANES), bf16),
        in_specs=[
            any_space, vmem, any_space, smem, any_space, smem, any_space, smem, any_space, smem,
            vmem, vmem, vmem, any_space, any_space, vmem, vmem, vmem,
        ],
        out_specs=any_space,
        scratch_shapes=[
            pltpu.VMEM((2, rows, width), bf16),
            pltpu.VMEM((rows, LANES), bf16),
            pltpu.VMEM((line, rows, width + LANES), bf16),
            pltpu.VMEM((line, rows, width), bf16),
            pltpu.VMEM((rows, width), bf16),
            pltpu.VMEM((count, features), bf16),
            pltpu.VMEM((4, n_actor, count, rows), bf16),
            pltpu.VMEM((4, count, LANES), f32),
            pltpu.VMEM((4, count, width + LANES), f32),
            pltpu.VMEM((4, units, count, LANES), bf16),
            pltpu.VMEM((4, count, LANES), f32),
            pltpu.VMEM((4, units, count, LANES), bf16),
            pltpu.VMEM((4, count, LANES), f32),
            pltpu.VMEM((2, context, 2 * LANES), bf16),
            pltpu.VMEM((2, context, 2 * LANES), bf16),
            pltpu.VMEM((depth, 3 * LANES), bf16),
            pltpu.VMEM((line, depth, 3 * LANES), bf16),
            pltpu.VMEM((line, depth, 2 * LANES), bf16),
            pltpu.VMEM((2, 2, count, heads * LANES), bf16),
            pltpu.VMEM((line, 2, count // 2, 5 * LANES), f32),
            pltpu.VMEM((line, 2, count // 2, 5 * LANES), f32),
            pltpu.VMEM((line, 2, 5, count // 2, LANES), bf16),
            dma((7,)),
            dma((2, 2, 2)),
            dma((2, 2, line, 2)),
            dma((2, line, 2)),
            dma((2,)),
            dma((3, 2)),
            dma((3, 2)),
            dma((3, 2)),
            dma((3, 2)),
            dma((4,)),
            dma((4,)),
            dma((4,)),
            dma((4,)),
            dma((4,)),
            dma((4,)),
            dma((2,)),
            dma((2,)),
            dma((2, line, 3)),
            dma((line, 3)),
            dma((line, 2)),
            dma((line, 2)),
            dma((1,)),
            dma((line,)),
            dma((line,)),
            dma((line, 3)),
            dma((line, 3)),
            dma((line, 3)),
            dma((line, 3)),
            dma((line, 3)),
            dma((line, 3)),
            dma((line, 3)),
        ],
        compiler_params=pltpu.CompilerParams(
            collective_id=0, has_side_effects=True, vmem_limit_bytes=58 * 1024 * 1024
        ),
        cost_estimate=pl.CostEstimate(
            flops=13_000_000_000, bytes_accessed=30_000_000, transcendentals=6_000_000
        ),
    )(
        leaf_states, norm_gain[None, :], wq_quant, wq_scale, wk, wk_scale, wv, wv_scale, wo_quant,
        wo_scale, q_bias[None, :], key_bias[None, :], value_bias[None, :], kcache, vcache,
        parent[:, None], length[:, None], table,
    )


def per_device_fused(n_actor, *args):
    length = args[16]
    half_width = HEAD_WIDTH // 2
    freqs = rope_base ** (-(jnp.arange(half_width, dtype=jnp.float32) * 2.0 / HEAD_WIDTH))
    angles = length.astype(jnp.float32)[:, None] * freqs[None, :]
    table = jnp.concatenate([jnp.cos(angles), jnp.sin(angles)], axis=1)
    units = fused(n_actor, args, table)
    return units.transpose(1, 0, 2).reshape(length.shape[0], -1)


def fits_fused(mesh_sizes, args):
    n_job, n_actor, n_tp = mesh_sizes
    return (
        n_tp == 2
        and n_job % 2 == 0
        and n_actor % 4 == 0
        and args[0].shape[0] % 32 == 0
        and args[2].shape[0] % SCALE_BLOCK == 0
        and (args[2].shape[1] // LANES) % 4 == 2
        and args[4].shape[1] == 2 * LANES
        and args[8].shape[1] == 5 * LANES
        and args[13].shape[0] == 2
    )


def per_device_any(mesh_sizes, *args):
    if fits_fused(mesh_sizes, args):
        return per_device_fused(mesh_sizes[1], *args)
    return per_device(mesh_sizes[:2], *args)


def solution(mesh):
    placed = (
        P(("job", "actor"), None),
        P(),
        P("actor", "tp"),
        P(None, "tp"),
        P("actor", "tp"),
        P(None, "tp"),
        P("actor", "tp"),
        P(None, "tp"),
        P("tp", "actor"),
        P("tp", None),
        P("tp"),
        P("tp"),
        P("tp"),
        P(("job", "actor"), None, "tp"),
        P(("job", "actor"), None, "tp"),
        P(("job", "actor")),
        P(("job", "actor")),
    )
    return jax.shard_map(
        functools.partial(
            per_device_any, (mesh.shape["job"], mesh.shape["actor"], mesh.shape["tp"])
        ),
        mesh=mesh,
        in_specs=placed,
        out_specs=P(("job", "actor"), None),
        check_vma=False,
    )
```

```python
import functools
import math

import jax
import jax.numpy as jnp
from jax import lax
from jax.experimental import pallas as pl
from jax.experimental.pallas import tpu as pltpu
from jax.sharding import PartitionSpec as P

HEAD_WIDTH = 128
SCALE_BLOCK = 128


epsilon = 1e-06
rope_base = 1000000.0


def apply_rotary(values, length):
    width = values.shape[-1]
    half_width = width // 2
    freqs = rope_base ** (-(jnp.arange(half_width, dtype=jnp.float32) * 2.0 / width))
    angles = length.astype(jnp.float32)[:, None] * freqs[None, :]
    cosine = jnp.cos(angles)[:, None, :]
    sine = jnp.sin(angles)[:, None, :]
    first = values[..., :half_width]
    second = values[..., half_width:]
    return jnp.concatenate(
        [first * cosine - second * sine, second * cosine + first * sine], axis=-1
    )


def attend_single_head(
    query_vector, key_self, value_self, prefix_key_cache, prefix_value_cache, parent, length
):
    scale_factor = 1.0 / math.sqrt(query_vector.shape[-1])
    self_score = (
        jnp.sum(
            query_vector.astype(jnp.float32) * key_self.astype(jnp.float32)[:, None, :], axis=-1
        )
        * scale_factor
    )
    visible = (jnp.arange(prefix_key_cache.shape[1])[None, :] < length[:, None])[:, None, :]
    outcome = jnp.zeros(query_vector.shape, jnp.float32)
    for prefix_index in range(prefix_key_cache.shape[0]):
        scores = (
            jnp.einsum(
                "lge,ce->lgc",
                query_vector,
                prefix_key_cache[prefix_index],
                preferred_element_type=jnp.float32,
            )
            * scale_factor
        )
        highest = jnp.maximum(jnp.max(jnp.where(visible, scores, -jnp.inf), axis=-1), self_score)
        weights = jnp.where(visible, jnp.exp(scores - highest[..., None]), 0.0)
        self_weight = jnp.exp(self_score - highest)
        total = jnp.sum(weights, axis=-1) + self_weight
        self_rounded = lax.optimization_barrier(self_weight.astype(jnp.bfloat16)).astype(
            jnp.float32
        )
        mixed = jnp.einsum(
            "lgc,ce->lge",
            weights.astype(jnp.bfloat16),
            prefix_value_cache[prefix_index],
            preferred_element_type=jnp.float32,
        )
        mixed = mixed + self_rounded[..., None] * value_self.astype(jnp.float32)[:, None, :]
        outcome = jnp.where(
            (parent == prefix_index)[:, None, None], mixed / total[..., None], outcome
        )
    return outcome


PIECE = 5
EARLY = 1


def spread_kernel(
    n_actor,
    rows_each,
    mine_ref,
    row_ref,
    gain_ref,
    sums_ref,
    all_ref,
    raw_ref,
    x_ref,
    home_sem,
    send_sem,
    recv_sem,
    row_sem,
):
    line = n_actor // 2
    actor = lax.axis_index("actor")
    job = lax.axis_index("job")
    at, y = actor // 2, actor % 2
    partner = job + 1 - 2 * (job % 2)
    pair = at * 2 + 1 - y
    has_up, has_down = at + 1 < line, at >= 1
    count = row_ref.shape[0]
    depth = mine_ref.shape[0]
    barrier = pltpu.get_barrier_semaphore()

    @pl.when(has_up)
    def _():
        pl.semaphore_signal(barrier, inc=1, device_id={"actor": actor + 2})

    @pl.when(has_down)
    def _():
        pl.semaphore_signal(barrier, inc=1, device_id={"actor": actor - 2})

    pl.semaphore_signal(barrier, inc=1, device_id={"actor": pair})
    pl.semaphore_signal(barrier, inc=1, device_id={"job": partner})
    pl.semaphore_wait(barrier, 2 + has_up.astype(jnp.int32) + has_down.astype(jnp.int32))

    def send(stream, source, piece, target, own=False):
        cut = pl.ds(piece * rows_each, rows_each)
        return pltpu.make_async_remote_copy(
            src_ref=mine_ref.at[cut] if own else all_ref.at[source, cut],
            dst_ref=all_ref.at[source, cut],
            send_sem=send_sem.at[stream, source, piece],
            recv_sem=recv_sem.at[source, piece],
            device_id={"actor": target},
        )

    def cross(source, piece, own=False):
        return send(0, source, piece, pair, own)

    def up(source, piece, own=False):
        return send(1, source, piece, actor + 2, own)

    def down(source, piece, own=False):
        return send(2, source, piece, actor - 2, own)

    def arrived(source, piece):
        cross(source, piece).wait_recv()

    late = list(range(PIECE - EARLY))
    early = list(range(PIECE - EARLY, PIECE))
    rows_copy = pltpu.make_async_remote_copy(
        src_ref=row_ref,
        dst_ref=raw_ref.at[pl.ds(count, count)],
        send_sem=row_sem.at[0],
        recv_sem=row_sem.at[1],
        device_id={"job": partner},
    )

    def both_ways(source, piece, own=False):
        @pl.when(has_up)
        def _():
            up(source, piece, own).start()

        @pl.when(has_down)
        def _():
            down(source, piece, own).start()

    for piece in early:
        cross(actor, piece, True).start()
    for piece in late:
        both_ways(actor, piece, True)
        cross(actor, piece, True).start()
    for piece in early:
        both_ways(actor, piece, True)
    rows_copy.start()
    home = pltpu.make_async_copy(mine_ref, all_ref.at[actor], home_sem.at[0])
    home.start()
    own_rows = pltpu.make_async_copy(row_ref, raw_ref.at[pl.ds(0, count)], home_sem.at[1])
    own_rows.start()

    def normalize(first):
        def block(i, carry):
            cut = pl.ds(pl.multiple_of(first + i * 16, 16), 16)
            rows = raw_ref[cut, :].astype(jnp.float32)
            rows = rows * lax.rsqrt(jnp.mean(rows * rows, axis=-1, keepdims=True) + epsilon)
            rows = (rows * gain_ref[...].astype(jnp.float32)).astype(jnp.bfloat16)
            for source in range(n_actor):
                x_ref[source, cut, :] = rows[:, source * depth : (source + 1) * depth]
            return carry

        lax.fori_loop(0, count // 16, block, 0)

    def add(source):
        sums_ref[...] += jnp.dot(
            x_ref[source], all_ref[source], preferred_element_type=jnp.float32
        )

    sums_ref[...] = jnp.zeros_like(sums_ref)
    own_rows.wait()
    normalize(0)
    for piece in early:
        arrived(pair, piece)
        both_ways(pair, piece)
    turn = jnp.where(at * 2 < line, 1, line - 1)

    def spot_of(k):
        return lax.rem(at + k * turn, line)

    for far in range(1, line):
        if far == line - 1:
            rows_copy.wait()
            normalize(count)
            home.wait()
            add(actor)
        todo = [(y, p) for p in late] + [(y, p) for p in early] + [(1 - y, p) for p in early]
        for index, (which, piece) in enumerate(todo):
            below = (at - far) * 2 + which
            above = (at + far) * 2 + which

            @pl.when(at >= far)
            def _():
                arrived(below, piece)

                @pl.when(has_up)
                def _():
                    up(below, piece).start()

                if index < len(late):
                    cross(below, piece).start()

            @pl.when(at + far < line)
            def _():
                arrived(above, piece)

                @pl.when(has_down)
                def _():
                    down(above, piece).start()

                if index < len(late):
                    cross(above, piece).start()

    def add_held(k, carry):
        add(spot_of(k) * 2 + y)
        return carry

    lax.fori_loop(1, line, add_held, 0)

    def add_crossed(k, carry):
        source = spot_of(k) * 2 + 1 - y
        for piece in late:
            arrived(source, piece)
        add(source)
        return carry

    lax.fori_loop(0, line, add_crossed, 0)
    for spot in range(line):
        for piece in late:
            cross(spot * 2 + y, piece).wait_send()
    for piece in early:
        cross(actor, piece).wait_send()
    for spot in range(line):
        items = [(y, p) for p in range(PIECE)] + [(1 - y, p) for p in early]
        for which, piece in items:
            source = spot * 2 + which

            @pl.when(jnp.logical_and(has_up, at >= spot))
            def _():
                up(source, piece).wait_send()

            @pl.when(jnp.logical_and(has_down, at <= spot))
            def _():
                down(source, piece).wait_send()


def spread(shard, rows, gain, n_actor):
    height, width = shard.shape
    return pl.pallas_call(
        functools.partial(spread_kernel, n_actor, height // PIECE),
        out_shape=jax.ShapeDtypeStruct((2 * rows.shape[0], width), jnp.float32),
        in_specs=[
            pl.BlockSpec(memory_space=pl.ANY),
            pl.BlockSpec(memory_space=pl.ANY),
            pl.BlockSpec(memory_space=pltpu.VMEM),
        ],
        out_specs=pl.BlockSpec(memory_space=pltpu.VMEM),
        scratch_shapes=[
            pltpu.VMEM((n_actor,) + shard.shape, shard.dtype),
            pltpu.VMEM((2 * rows.shape[0], rows.shape[1]), rows.dtype),
            pltpu.VMEM((n_actor, 2 * rows.shape[0], height), rows.dtype),
            pltpu.SemaphoreType.DMA((2,)),
            pltpu.SemaphoreType.DMA((3, n_actor, PIECE)),
            pltpu.SemaphoreType.DMA((n_actor, PIECE)),
            pltpu.SemaphoreType.DMA((2,)),
        ],
        compiler_params=pltpu.CompilerParams(
            collective_id=0, has_side_effects=True, vmem_limit_bytes=48 * 1024 * 1024
        ),
        cost_estimate=pl.CostEstimate(
            flops=0, bytes_accessed=300_000_000, transcendentals=0
        ),
    )(shard, rows, gain)


def per_device(
    mesh_sizes,
    leaf_states,
    norm_gain,
    wq_quant,
    wq_scale,
    key_weight_quantized,
    key_weight_scale,
    value_weight_quantized,
    value_weight_scale,
    wo_quant,
    wo_scale,
    q_bias,
    key_bias,
    value_bias,
    prefix_key_cache,
    prefix_value_cache,
    parent_prefix_slot,
    prefix_length,
):
    n_job, n_actor = mesh_sizes
    swap = [(i, i ^ 1) for i in range(n_job)]
    side = lax.axis_index("job") % 2
    actor = lax.axis_index("actor")

    def trade(x):
        return lax.ppermute(x, "job", swap)

    leaf_count = leaf_states.shape[0]

    def half_cols(x):
        width = x.shape[1] // 2
        return lax.dynamic_slice_in_dim(x, side * width, width, 1)

    row_count = wq_quant.shape[0]

    def expand_rows(quant, scale):
        mine = lax.dynamic_slice_in_dim(
            scale, actor * (row_count // SCALE_BLOCK), row_count // SCALE_BLOCK, 0
        ) if row_count % SCALE_BLOCK == 0 else None
        if mine is None:
            tall = jnp.repeat(scale, SCALE_BLOCK, axis=0)
            tall = lax.dynamic_slice_in_dim(tall, actor * row_count, row_count, 0)
        else:
            tall = jnp.repeat(mine, SCALE_BLOCK, axis=0)
        wide = jnp.repeat(half_cols(tall), SCALE_BLOCK, axis=1)
        return (half_cols(quant).astype(jnp.float32) * wide).astype(jnp.bfloat16)

    qkv_local = jnp.concatenate(
        [
            expand_rows(wq_quant, wq_scale),
            expand_rows(key_weight_quantized, key_weight_scale),
            expand_rows(value_weight_quantized, value_weight_scale),
        ],
        axis=1,
    )
    col_count = wo_quant.shape[1]
    spread_scale = jnp.repeat(wo_scale, SCALE_BLOCK, axis=1)
    own_scale = half_cols(lax.dynamic_slice_in_dim(spread_scale, actor * col_count, col_count, 1))
    wo_local = (
        half_cols(wo_quant).astype(jnp.float32) * jnp.repeat(own_scale, SCALE_BLOCK, axis=0)
    ).astype(jnp.bfloat16).T
    sums = spread(qkv_local, leaf_states, norm_gain[None, :], n_actor)
    wo_local, sums, prefix_length = lax.optimization_barrier((wo_local, sums, prefix_length))
    both_length = jnp.concatenate([prefix_length, trade(prefix_length)], axis=0)

    def half_row(x):
        width = x.shape[0] // 2
        return lax.dynamic_slice_in_dim(x, side * width, width, 0)

    bias = jnp.concatenate([half_row(q_bias), half_row(key_bias), half_row(value_bias)])
    sums = sums + bias.astype(jnp.float32)
    v_width = value_bias.shape[0] // 2
    rot_width = sums.shape[1] - v_width
    rotated = apply_rotary(
        sums[:, :rot_width].reshape(2 * leaf_count, rot_width // HEAD_WIDTH, HEAD_WIDTH),
        both_length,
    ).reshape(2 * leaf_count, rot_width)
    done = jnp.concatenate([rotated, sums[:, rot_width:]], axis=1).astype(jnp.bfloat16)
    own = done[:leaf_count]
    other = trade(done[leaf_count:])
    q_width = q_bias.shape[0] // 2

    kv_half = v_width // HEAD_WIDTH
    query_group = q_bias.shape[0] // key_bias.shape[0]
    outs = []
    for which, block in ((side, own), (1 - side, other)):
        q = block[:, :q_width].reshape(leaf_count, kv_half, query_group, HEAD_WIDTH)
        k = block[:, q_width : q_width + v_width].reshape(leaf_count, kv_half, HEAD_WIDTH)
        v = block[:, q_width + v_width :].reshape(leaf_count, kv_half, HEAD_WIDTH)
        for head in range(kv_half):
            at = (which * kv_half + head) * HEAD_WIDTH
            outs.append(
                attend_single_head(
                    q[:, head],
                    k[:, head],
                    v[:, head],
                    lax.dynamic_slice_in_dim(prefix_key_cache, at, HEAD_WIDTH, 2),
                    lax.dynamic_slice_in_dim(prefix_value_cache, at, HEAD_WIDTH, 2),
                    parent_prefix_slot,
                    prefix_length,
                )
                .reshape(leaf_count, query_group * HEAD_WIDTH)
                .astype(jnp.bfloat16)
            )
    mine = jnp.concatenate(outs[:kv_half], axis=1)
    theirs = jnp.concatenate(outs[kv_half:], axis=1)
    attended = jnp.where(
        side == 0,
        jnp.concatenate([mine, theirs], axis=1),
        jnp.concatenate([theirs, mine], axis=1),
    )

    wo_all = lax.all_gather(wo_local, "actor", axis=0, tiled=True)
    group = lax.axis_index("tp")
    cores = [(0, 1), (1, 0)]

    def project(rows):
        part = lax.dot_general(
            rows, wo_all, (((1,), (1,)), ((), ())), preferred_element_type=jnp.float32
        )
        width = part.shape[1] // 2
        first, second = part[:, :width], part[:, width:]
        give = jnp.where(group == 0, second, first)
        keep = jnp.where(group == 0, first, second)
        return (keep + lax.ppermute(give, "tp", cores)).astype(jnp.bfloat16), give

    def join(x):
        y = lax.ppermute(x, "tp", cores)
        return jnp.where(
            group == 0,
            jnp.concatenate([x, y], axis=1),
            jnp.concatenate([y, x], axis=1),
        )

    away, marker = project(trade(attended))
    attended, away, _ = lax.optimization_barrier((attended, away, marker))
    away = trade(away)
    local = join(project(attended)[0])
    remote = join(away)
    low = jnp.where(side == 0, local, remote)
    high = jnp.where(side == 0, remote, local)
    pieces = []
    half = col_count // 2
    for a in range(n_actor):
        pieces += [low[:, a * half : (a + 1) * half], high[:, a * half : (a + 1) * half]]
    return jnp.concatenate(pieces, axis=1)


LANES = 128


def fused_kernel(
    n_actor,
    states_ref,
    gain_ref,
    wq_ref,
    wq_scale_ref,
    wk_ref,
    wk_scale_ref,
    wv_ref,
    wv_scale_ref,
    wo_ref,
    wo_scale_ref,
    qb_ref,
    kb_ref,
    vb_ref,
    kcache_ref,
    vcache_ref,
    parent_ref,
    length_ref,
    out_ref,
    raw_ref,
    rawv_ref,
    wown_ref,
    woth_ref,
    give_ref,
    xraw_ref,
    xs_ref,
    tabs_ref,
    gains_ref,
    bias_ref,
    acc_ref,
    rst_ref,
    vst_ref,
    rq_ref,
    rv_ref,
    kc_ref,
    vc_ref,
    woraw_ref,
    zset_ref,
    yset_ref,
    att_ref,
    psend_ref,
    precv_ref,
    res_ref,
    load_sem,
    kv_sem,
    z_send,
    z_recv,
    g_send,
    x_send,
    x_recv,
    xs_send,
    xs_recv,
    t_send,
    t_recv,
    q_send,
    q_recv,
    v_send,
    v_recv,
    a_send,
    a_recv,
    oz_send,
    oz_recv,
    oy_send,
    oy_recv,
    oc_send,
    p_send,
    p_recv,
    l_sem,
    s_send,
    s_recv,
    c_send,
    c_recv,
    f_send,
    f_recv,
):
    line = n_actor // 2
    actor = lax.axis_index("actor")
    job = lax.axis_index("job")
    core = lax.axis_index("tp")
    at, y = actor // 2, actor % 2
    side = job % 2
    there = {"job": job + 1 - 2 * side}
    pair = {"actor": at * 2 + 1 - y}
    diagonal = {"job": job + 1 - 2 * side, "actor": at * 2 + 1 - y}
    sibling = {"tp": 1 - core}
    above, below = {"actor": actor + 2}, {"actor": actor - 2}
    has_up, has_down = at + 1 < line, at >= 1
    middle = jnp.logical_and(has_up, has_down)
    ends = jnp.logical_not(middle)
    even = (y + side) % 2 == 0
    odd = (y + side) % 2 == 1
    rows = raw_ref.shape[1]
    count = xraw_ref.shape[0]
    half_rows = rows // 2
    half_count = count // 2
    width = raw_ref.shape[2]
    units = width // LANES
    heads = 2 * units - 1
    depth = zset_ref.shape[1]
    strips = n_actor // 2
    part = strips // 2
    f32, bf16 = jnp.float32, jnp.bfloat16

    def lanes(unit, n=1):
        return pl.ds(pl.multiple_of(unit * LANES, LANES), n * LANES)

    barrier = pltpu.get_barrier_semaphore()

    @pl.when(has_up)
    def _():
        pl.semaphore_signal(barrier, inc=1, device_id=above)

    @pl.when(has_down)
    def _():
        pl.semaphore_signal(barrier, inc=1, device_id=below)

    for peer in (there, pair, diagonal, sibling):
        pl.semaphore_signal(barrier, inc=1, device_id=peer)

    def local(source, target, sem):
        return pltpu.make_async_copy(source, target, sem)

    def remote(source, target, ss, rs, peer):
        return pltpu.make_async_remote_copy(
            src_ref=source, dst_ref=target, send_sem=ss, recv_sem=rs, device_id=peer
        )

    first_of = lambda parity, s: s * (3 - parity)
    first = first_of(y, side)
    w_loads = [
        local(wq_ref.at[:, lanes(side * heads, units)], raw_ref.at[0], load_sem.at[0]),
        local(
            wq_ref.at[:, lanes(side * heads + units, units - 1)],
            raw_ref.at[1, :, pl.ds(0, (units - 1) * LANES)],
            load_sem.at[1],
        ),
        local(
            wk_ref.at[:, lanes(side)],
            raw_ref.at[1, :, pl.ds((units - 1) * LANES, LANES)],
            load_sem.at[2],
        ),
        local(wv_ref.at[:, lanes(side)], rawv_ref, load_sem.at[3]),
    ]
    state_load = local(states_ref, xraw_ref, load_sem.at[4])
    wo_load = local(
        wo_ref.at[:, lanes(first, 2)], woraw_ref.at[:, pl.ds(0, 2 * LANES)], load_sem.at[5]
    )
    wo_load_last = local(
        wo_ref.at[:, lanes(first + 2 * (1 - (y + side) % 2), 1)],
        woraw_ref.at[:, pl.ds(2 * LANES, LANES)],
        load_sem.at[6],
    )
    for copy in w_loads:
        copy.start()
    state_load.start()
    wo_load.start()
    wo_load_last.start()
    kv_loads = []
    for j in range(2):
        for p in range(2):
            place = pl.ds(p * LANES, LANES)
            cut = pl.ds(j * LANES, LANES)
            kv_loads.append(
                local(kcache_ref.at[p, :, cut], kc_ref.at[j, :, place], kv_sem.at[0, j, p])
            )
            kv_loads.append(
                local(vcache_ref.at[p, :, cut], vc_ref.at[j, :, place], kv_sem.at[1, j, p])
            )
    for copy in kv_loads:
        copy.start()

    blocks = rows // SCALE_BLOCK

    def pick(ref, row, column):
        values = ref[pl.ds(row, 1), :]
        here = lax.broadcasted_iota(jnp.int32, values.shape, 1) == column
        return jnp.sum(jnp.where(here, values, 0.0), axis=1, keepdims=True)

    def unit_scale(parity, block, u):
        row = actor * blocks + block
        if u < units - 1:
            return pick(wq_scale_ref, side * heads + u + units * parity, row)
        return jnp.where(
            parity == 0,
            pick(wq_scale_ref, side * heads + u, row),
            pick(wk_scale_ref, side, row),
        )

    def expand(parity, target):
        for block in range(blocks):
            cut = pl.ds(block * SCALE_BLOCK, SCALE_BLOCK)
            for u in range(units):
                lane = pl.ds(u * LANES, LANES)
                scaled = raw_ref[parity, cut, lane].astype(f32) * unit_scale(parity, block, u)
                target(cut, lane, scaled.astype(bf16))

    def to_give(cut, lane, value):
        give_ref[cut, lane] = value

    def to_own(cut, lane, value):
        wown_ref[at, cut, lane] = value

    for copy in w_loads:
        copy.wait()
    expand(1 - y, to_give)
    pl.semaphore_wait(barrier, 4 + has_up.astype(jnp.int32) + has_down.astype(jnp.int32))

    def half(p):
        return pl.ds(p * half_rows, half_rows)

    def give(p):
        return remote(
            give_ref.at[half(p)], woth_ref.at[at, half(p)], g_send.at[p], z_recv.at[1, at, p], pair
        )

    for p in range(2):
        give(p).start()
    expand(y, to_own)
    for block in range(blocks):
        cut = pl.ds(block * SCALE_BLOCK, SCALE_BLOCK)
        scale = pick(wv_scale_ref, side, actor * blocks + block)
        wown_ref[at, cut, pl.ds(width, LANES)] = (rawv_ref[cut, :].astype(f32) * scale).astype(
            bf16
        )

    def up_down(way, kind, spot, p):
        ref = (wown_ref if kind == 0 else woth_ref).at[spot, half(p)]
        return remote(
            ref, ref, z_send.at[way, kind, spot, p], z_recv.at[kind, spot, p], (above, below)[way]
        )

    def both_ways(kind, spot, p):
        @pl.when(has_up)
        def _():
            up_down(0, kind, spot, p).start()

        @pl.when(has_down)
        def _():
            up_down(1, kind, spot, p).start()

    for p in range(2):
        both_ways(0, at, p)

    state_load.wait()

    gains_ref[...] = gain_ref[...].astype(f32).reshape(1, -1)
    for i, ref in enumerate((qb_ref, kb_ref, vb_ref)):
        bias_ref[i, :, : ref.shape[0]] = ref[...].astype(f32).reshape(1, -1)

    def normalize(i, carry):
        cut = pl.ds(pl.multiple_of(i * 16, 16), 16)
        x = xraw_ref[cut, :].astype(f32)
        x = x * lax.rsqrt(jnp.mean(x * x, axis=-1, keepdims=True) + epsilon)
        x = (x * gains_ref[...]).astype(bf16)
        for source in range(n_actor):
            xs_ref[0, source, cut, :] = x[:, source * rows : (source + 1) * rows]
        return carry

    lax.fori_loop(0, count // 16, normalize, 0)

    def some(p):
        return pl.ds(core * strips + p * part, part)

    def share(slot, p, origin, peer):
        return remote(
            xs_ref.at[origin, some(p)],
            xs_ref.at[slot, some(p)],
            x_send.at[slot - 1, p],
            x_recv.at[slot - 1, p],
            peer,
        )

    share_list = [
        share(1, 0, 0, there),
        share(2, 1, 0, pair),
        share(1, 1, 0, there),
        share(2, 0, 0, pair),
    ]
    for copy in share_list:
        copy.start()

    def to_sibling(slot, p):
        ref = xs_ref.at[slot, some(p)]
        return remote(ref, ref, xs_send.at[slot - 1, p], xs_recv.at[slot - 1, p], sibling)

    def from_sibling(slot, p):
        ref = xs_ref.at[slot, pl.ds((1 - core) * strips + p * part, part)]
        return remote(ref, ref, xs_send.at[slot - 1, p], xs_recv.at[slot - 1, p], sibling)

    def column(values):
        wide = jnp.broadcast_to(values.astype(f32).reshape(1, count), (LANES, count))
        return wide.T

    lane_at = lax.broadcasted_iota(jnp.int32, (count, LANES), 1)
    step = lax.rem(lax.broadcasted_iota(jnp.int32, (1, LANES), 1), LANES // 2).astype(f32)
    freqs = jnp.exp(step * (-2.0 * math.log(rope_base) / LANES))
    lengths = column(length_ref[...])
    parents = column(parent_ref[...])
    angles = lengths * freqs
    tabs_ref[0] = jnp.where(lane_at < LANES // 2, jnp.cos(angles), jnp.sin(angles))
    table_sends = [
        remote(tabs_ref.at[0], tabs_ref.at[slot], t_send.at[slot], t_recv.at[slot], peer)
        for slot, peer in ((1, there), (2, pair), (3, diagonal))
    ]
    for copy in table_sends:
        copy.start()

    wo_load.wait()
    wo_load_last.wait()
    wo_blocks = depth // SCALE_BLOCK
    wo_units = wo_ref.shape[1] // LANES

    def expand_wo(block, carry):
        cut = pl.ds(pl.multiple_of(block * SCALE_BLOCK, SCALE_BLOCK), SCALE_BLOCK)
        for u in range(2):
            lane = pl.ds(u * LANES, LANES)
            scale = pick(wo_scale_ref, block, actor * wo_units + first + u)
            zset_ref[at, cut, lane] = (woraw_ref[cut, lane].astype(f32) * scale).astype(bf16)
        return carry

    lax.fori_loop(0, wo_blocks, expand_wo, 0)

    def z_unit(spot, u):
        return zset_ref.at[spot, :, pl.ds(u * LANES, LANES)]

    cross_last = remote(z_unit(at, 2), z_unit(at, 2), oc_send.at[0], oz_recv.at[at, 2], pair)

    @pl.when(even)
    def _():
        def expand_last(block, carry):
            cut = pl.ds(pl.multiple_of(block * SCALE_BLOCK, SCALE_BLOCK), SCALE_BLOCK)
            lane = pl.ds(2 * LANES, LANES)
            scale = pick(wo_scale_ref, block, actor * wo_units + first + 2)
            zset_ref[at, cut, lane] = (woraw_ref[cut, lane].astype(f32) * scale).astype(bf16)
            return carry

        lax.fori_loop(0, wo_blocks, expand_last, 0)
        cross_last.start()

    def wo_way(way, spot, u):
        ref = z_unit(spot, u)
        return remote(
            ref, ref, oz_send.at[way, spot, u], oz_recv.at[spot, u], (above, below)[way]
        )

    def wo_cross(spot, u):
        return remote(
            z_unit(spot, u),
            yset_ref.at[spot, :, pl.ds(u * LANES, LANES)],
            oy_send.at[spot, u],
            oy_recv.at[spot, u],
            pair,
        )

    def wo_begin(far):
        @pl.when(jnp.logical_and(at == far, has_up))
        def _():
            for u in range(2 if far < 2 else 3):
                wo_way(0, at, u).start()

        @pl.when(jnp.logical_and(line - 1 - at == far, has_down))
        def _():
            for u in range(2 if far < 2 else 3):
                wo_way(1, at, u).start()

    def wo_begin_last():
        @pl.when(odd)
        def _():
            cross_last.wait_recv()

        @pl.when(jnp.logical_and(at < 2, has_up))
        def _():
            wo_way(0, at, 2).start()

        @pl.when(jnp.logical_and(line - 1 - at < 2, has_down))
        def _():
            wo_way(1, at, 2).start()

    for p in range(2):
        give(p).wait_recv()
        both_ways(1, at, p)
    wo_begin(0)

    acc_ref[...] = jnp.zeros_like(acc_ref)

    def multiply(spot):
        def body(o, carry):
            acc_ref[o] += jnp.dot(
                xs_ref[o, spot * 2 + y], wown_ref[spot], preferred_element_type=f32
            )
            acc_ref[o, :, :width] += jnp.dot(
                xs_ref[o, spot * 2 + 1 - y], woth_ref[spot], preferred_element_type=f32
            )
            return carry

        lax.fori_loop(0, 4, body, 0)

    def multiply_far(far, carry):
        @pl.when(at >= far)
        def _():
            multiply(at - far)

        @pl.when(jnp.logical_and(at + far < line, far > 0))
        def _():
            multiply(at + far)

        return carry

    def rows_first():
        for slot, p, peer in ((1, 0, pair), (1, 1, None), (2, 1, there), (2, 0, None)):
            share(slot, p, 0, there if slot == 1 else pair).wait_recv()
            if peer is not None:
                share(3, p, slot, peer).start()
            to_sibling(slot, p).start()

    def rows_rest():
        for p in range(2):
            share(3, p, 1 + p, pair if p == 0 else there).wait_recv()
            to_sibling(3, p).start()

        @pl.when(ends)
        def _():
            for u in range(2):
                wo_cross(at, u).start()

        for slot in (1, 2, 3):
            for p in range(2):
                from_sibling(slot, p).wait_recv()

    for far in range(1, line):
        for kind in range(2):
            for p in range(2):

                @pl.when(at >= far)
                def _():
                    up_down(0, kind, at - far, p).wait_recv()

                    @pl.when(has_up)
                    def _():
                        up_down(0, kind, at - far, p).start()

                @pl.when(at + far < line)
                def _():
                    up_down(1, kind, at + far, p).wait_recv()

                    @pl.when(has_down)
                    def _():
                        up_down(1, kind, at + far, p).start()

        wo_begin(far)
        if far == 1:
            rows_first()
            wo_begin_last()
        if far == max(line - 2, 1):
            rows_rest()
            lax.fori_loop(0, max(line - 1, 1), multiply_far, 0)
    multiply_far(line - 1, 0)

    def results(slot):
        return (
            remote(rst_ref.at[slot], rq_ref.at[slot], q_send.at[slot], q_recv.at[slot], peers[slot]),
            remote(vst_ref.at[slot], rv_ref.at[slot], v_send.at[slot], v_recv.at[slot], peers[slot]),
        )

    peers = {1: there, 2: pair, 3: diagonal}
    for slot in (2, 3, 1, 0):
        if slot:
            table_sends[slot - 1].wait_recv()
        table = tabs_ref[slot]
        swapped = pltpu.roll(table, LANES // 2, 1)
        cosine = jnp.where(lane_at < LANES // 2, table, swapped)
        sine = jnp.where(lane_at < LANES // 2, -swapped, table)
        for u in range(units):
            if u < units - 1:
                bias = bias_ref[0, :, lanes(side * heads + u + units * y)]
            else:
                bias = jnp.where(
                    y == 0,
                    bias_ref[0, :, lanes(side * heads + u)],
                    bias_ref[1, :, lanes(side)],
                )
            value = acc_ref[slot, :, u * LANES : (u + 1) * LANES] + bias
            value = value * cosine + pltpu.roll(value, LANES // 2, 1) * sine
            (rst_ref if slot else rq_ref)[slot, u] = value.astype(bf16)
        (vst_ref if slot else rv_ref)[slot] = acc_ref[slot, :, width:]
        if slot:
            for copy in results(slot):
                copy.start()

    def relay(far):
        for u in range(3):

            @pl.when(at >= far)
            def _():
                @pl.when(has_up)
                def _():
                    wo_way(0, at - far, u).wait_recv()
                    wo_way(0, at - far, u).start()

                if u < 2:

                    @pl.when(jnp.logical_not(has_up))
                    def _():
                        wo_way(0, at - far, u).wait_recv()

                    wo_cross(at - far, u).start()

            @pl.when(at + far < line)
            def _():
                @pl.when(has_down)
                def _():
                    wo_way(1, at + far, u).wait_recv()
                    wo_way(1, at + far, u).start()

                if u < 2:

                    @pl.when(jnp.logical_not(has_down))
                    def _():
                        wo_way(1, at + far, u).wait_recv()

                    wo_cross(at + far, u).start()

    def landed(far):
        @pl.when(jnp.logical_and(at >= far, jnp.logical_not(has_up)))
        def _():
            wo_way(0, at - far, 2).wait_recv()

        @pl.when(jnp.logical_and(at + far < line, jnp.logical_not(has_down)))
        def _():
            wo_way(1, at + far, 2).wait_recv()

    @pl.when(middle)
    def _():
        for u in range(2):
            wo_cross(at, u).start()
        relay(1)

    for copy in kv_loads:
        copy.wait()
    parent = parents[:, :1]
    length = lengths[:, :1].astype(jnp.int32)
    in_first = (parent == 0).astype(f32)
    in_second = 1.0 - in_first
    scale_factor = 1.0 / math.sqrt(LANES)

    def hand(j):
        return remote(
            att_ref.at[0, j], att_ref.at[1, j], a_send.at[j], a_recv.at[j], there
        )

    def attend(base):
        group = side if base == 0 else 1 - side
        low = jnp.where(y == 0, base, base + 2)
        high = jnp.where(y == 0, base + 2, base)
        key_new = rq_ref[high, units - 1].astype(f32)
        value_new = rv_ref[base] + rv_ref[base + 2] + bias_ref[2, :, lanes(group)]
        value_new = value_new.astype(bf16).astype(f32)

        def head(h, carry):
            query = rq_ref[
                jnp.where(h < units, low, high), jnp.where(h < units, h, h - units)
            ].astype(f32)
            own = jnp.sum(query * key_new, axis=-1, keepdims=True) * scale_factor
            both = jnp.concatenate([query * in_first, query * in_second], axis=1).astype(bf16)
            scores = lax.dot_general(
                both, kc_ref[group], (((1,), (1,)), ((), ())), preferred_element_type=f32
            )
            place = lax.broadcasted_iota(jnp.int32, scores.shape, 1)
            scores = jnp.where(place < length, scores, -jnp.inf)
            highest = jnp.maximum(jnp.max(scores, axis=-1, keepdims=True) * scale_factor, own)
            weights = jnp.exp(scores * scale_factor - highest)
            own = jnp.exp(own - highest)
            total = jnp.sum(weights, axis=-1, keepdims=True) + own
            mixed = jnp.dot(weights.astype(bf16), vc_ref[group], preferred_element_type=f32)
            mixed = jnp.where(parent == 0, mixed[:, :LANES], mixed[:, LANES:])
            mixed = mixed + own.astype(bf16).astype(f32) * value_new
            att_ref[0, group, :, lanes(h)] = (mixed / total).astype(bf16)
            return carry

        lax.fori_loop(0, heads, head, 0)
        hand(group).start()

    for slot in (2,):
        for copy in results(slot):
            copy.wait_recv()
    attend(0)

    @pl.when(ends)
    def _():
        relay(1)

    for slot in (1, 3):
        for copy in results(slot):
            copy.wait_recv()
    attend(1)
    relay(2)

    def partial(spot, which):
        cut = pl.ds(pl.multiple_of(which * half_count, half_count), half_count)
        outs = []
        for o in range(2):
            z = y_part = None
            for j in range(2):
                block = att_ref[o, j, cut, :]
                deep = pl.ds(j * (depth // 2), depth // 2)
                z_more = jnp.dot(block, zset_ref[spot, deep, :], preferred_element_type=f32)
                y_more = jnp.dot(block, yset_ref[spot, deep, :], preferred_element_type=f32)
                z = z_more if z is None else z + z_more
                y_part = y_more if y_part is None else y_part + y_more
            outs.append((z, y_part))
        return outs

    def p_copy(spot):
        return remote(
            psend_ref.at[spot], precv_ref.at[spot], p_send.at[spot], p_recv.at[spot], sibling
        )

    def spots(s, spot):
        own_base = wo_units * (2 * spot + y) + first_of(y, s)
        oth_base = wo_units * (2 * spot + 1 - y) + first_of(1 - y, s)
        return (
            (0, 2, own_base),
            (2, 1, jnp.where((y + s) % 2 == 0, own_base + 2, oth_base + 2)),
            (3, 2, oth_base),
        )

    def mine(c):
        return pl.ds(pl.multiple_of(c * half_count, half_count), half_count)

    def home_copies(spot):
        return [
            local(
                res_ref.at[spot, 0, :, pl.ds(a * LANES, n * LANES)],
                out_ref.at[mine(core), lanes(u, n)],
                l_sem.at[spot, i],
            )
            for i, (a, n, u) in enumerate(spots(side, spot))
        ]

    def sibling_copies(spot):
        return [
            remote(
                res_ref.at[spot, 0, :, pl.ds(a * LANES, n * LANES)],
                out_ref.at[mine(core), lanes(u, n)],
                s_send.at[spot, i],
                s_recv.at[spot, i],
                sibling,
            )
            for i, (a, n, u) in enumerate(spots(side, spot))
        ]

    def there_copies(spot, s):
        return [
            remote(
                res_ref.at[spot, 1, :, pl.ds(a * LANES, n * LANES)],
                out_ref.at[mine(core), lanes(u, n)],
                c_send.at[spot, i],
                c_recv.at[spot, i],
                there,
            )
            for i, (a, n, u) in enumerate(spots(s, spot))
        ]

    def onward_copies(spot):
        return [
            remote(
                out_ref.at[mine(core), lanes(u, n)],
                out_ref.at[mine(core), lanes(u, n)],
                f_send.at[spot, i],
                f_recv.at[spot, i],
                sibling,
            )
            for i, (a, n, u) in enumerate(spots(1 - side, spot))
        ]

    z_width = zset_ref.shape[2]

    def project(spot):
        for u in range(2):
            wo_cross(spot, u).wait_recv()
        for o, (z, y_part) in enumerate(partial(spot, 1 - core)):
            psend_ref[spot, o, :, :z_width] = z
            psend_ref[spot, o, :, z_width:] = y_part
        p_copy(spot).start()
        kept = partial(spot, core)
        p_copy(spot).wait_recv()
        for o, (z, y_part) in enumerate(kept):
            z = z + precv_ref[spot, o, :, :z_width]
            y_part = y_part + precv_ref[spot, o, :, z_width:]
            res_ref[spot, o, :, :z_width] = z.astype(bf16)
            res_ref[spot, o, :, z_width:] = y_part.astype(bf16)
        for copy in there_copies(spot, side) + sibling_copies(spot) + home_copies(spot):
            copy.start()

    def onward(spot):
        for got, copy in zip(there_copies(spot, 1 - side), onward_copies(spot)):
            got.wait_recv()
            copy.start()

    def at_far(action, far):
        @pl.when(at >= far)
        def _():
            action(at - far)

        @pl.when(jnp.logical_and(at + far < line, far > 0))
        def _():
            action(at + far)

    for j in range(2):
        hand(j).wait_recv()

    def rounds(far, carry):
        @pl.when(far > 2)
        def _():
            relay(far)

        @pl.when(far > 0)
        def _():
            landed(far)

        at_far(project, far)

        @pl.when(far > 0)
        def _():
            at_far(onward, far - 1)

        return carry

    lax.fori_loop(0, line, rounds, 0)
    at_far(onward, line - 1)

    for p in range(2):
        give(p).wait_send()
        for slot, peer in ((1, there), (2, pair), (3, pair)):
            share(slot, p, 0, peer).wait_send()
            to_sibling(slot, p).wait_send()
    for copy in table_sends:
        copy.wait_send()
    for slot in (1, 2, 3):
        for copy in results(slot):
            copy.wait_send()
    for j in range(2):
        hand(j).wait_send()

    @pl.when(even)
    def _():
        cross_last.wait_send()

    def finish(spot, carry):
        @pl.when(jnp.logical_and(has_up, at >= spot))
        def _():
            for kind in range(2):
                for p in range(2):
                    up_down(0, kind, spot, p).wait_send()
            for u in range(3):
                wo_way(0, spot, u).wait_send()

        @pl.when(jnp.logical_and(has_down, at <= spot))
        def _():
            for kind in range(2):
                for p in range(2):
                    up_down(1, kind, spot, p).wait_send()
            for u in range(3):
                wo_way(1, spot, u).wait_send()

        for u in range(2):
            wo_cross(spot, u).wait_send()
        p_copy(spot).wait_send()
        for copy in home_copies(spot):
            copy.wait()
        for copy in there_copies(spot, side):
            copy.wait_send()
        for copy in sibling_copies(spot) + onward_copies(spot):
            copy.wait()
        return carry

    lax.fori_loop(0, line, finish, 0)


def fused(n_actor, args):
    (
        leaf_states, norm_gain, wq_quant, wq_scale, wk, wk_scale, wv, wv_scale, wo_quant, wo_scale,
        q_bias, key_bias, value_bias, kcache, vcache, parent, length,
    ) = args
    count, features = leaf_states.shape
    rows = wq_quant.shape[0]
    heads = wq_quant.shape[1] // (2 * LANES)
    units = (heads + 1) // 2
    width = units * LANES
    context = kcache.shape[1]
    depth = wo_quant.shape[0]
    line = n_actor // 2
    total_units = n_actor * (wo_quant.shape[1] // LANES)
    bf16, f32 = jnp.bfloat16, jnp.float32
    any_space = pl.BlockSpec(memory_space=pl.ANY)
    vmem = pl.BlockSpec(memory_space=pltpu.VMEM)
    dma = pltpu.SemaphoreType.DMA
    return pl.pallas_call(
        functools.partial(fused_kernel, n_actor),
        out_shape=jax.ShapeDtypeStruct((count, total_units * LANES), bf16),
        in_specs=[
            any_space, vmem, any_space, vmem, any_space, vmem, any_space, vmem, any_space, vmem,
            vmem, vmem, vmem, any_space, any_space, vmem, vmem,
        ],
        out_specs=any_space,
        scratch_shapes=[
            pltpu.VMEM((2, rows, width), bf16),
            pltpu.VMEM((rows, LANES), bf16),
            pltpu.VMEM((line, rows, width + LANES), bf16),
            pltpu.VMEM((line, rows, width), bf16),
            pltpu.VMEM((rows, width), bf16),
            pltpu.VMEM((count, features), bf16),
            pltpu.VMEM((4, n_actor, count, rows), bf16),
            pltpu.VMEM((4, count, LANES), f32),
            pltpu.VMEM((1, features), f32),
            pltpu.VMEM((3, 1, 2 * heads * LANES), f32),
            pltpu.VMEM((4, count, width + LANES), f32),
            pltpu.VMEM((4, units, count, LANES), bf16),
            pltpu.VMEM((4, count, LANES), f32),
            pltpu.VMEM((4, units, count, LANES), bf16),
            pltpu.VMEM((4, count, LANES), f32),
            pltpu.VMEM((2, context, 2 * LANES), bf16),
            pltpu.VMEM((2, context, 2 * LANES), bf16),
            pltpu.VMEM((depth, 3 * LANES), bf16),
            pltpu.VMEM((line, depth, 3 * LANES), bf16),
            pltpu.VMEM((line, depth, 2 * LANES), bf16),
            pltpu.VMEM((2, 2, count, heads * LANES), bf16),
            pltpu.VMEM((line, 2, count // 2, 5 * LANES), f32),
            pltpu.VMEM((line, 2, count // 2, 5 * LANES), f32),
            pltpu.VMEM((line, 2, count // 2, 5 * LANES), bf16),
            dma((7,)),
            dma((2, 2, 2)),
            dma((2, 2, line, 2)),
            dma((2, line, 2)),
            dma((2,)),
            dma((3, 2)),
            dma((3, 2)),
            dma((3, 2)),
            dma((3, 2)),
            dma((4,)),
            dma((4,)),
            dma((4,)),
            dma((4,)),
            dma((4,)),
            dma((4,)),
            dma((2,)),
            dma((2,)),
            dma((2, line, 3)),
            dma((line, 3)),
            dma((line, 2)),
            dma((line, 2)),
            dma((1,)),
            dma((line,)),
            dma((line,)),
            dma((line, 3)),
            dma((line, 3)),
            dma((line, 3)),
            dma((line, 3)),
            dma((line, 3)),
            dma((line, 3)),
            dma((line, 3)),
        ],
        compiler_params=pltpu.CompilerParams(
            collective_id=0, has_side_effects=True, vmem_limit_bytes=58 * 1024 * 1024
        ),
        cost_estimate=pl.CostEstimate(
            flops=13_000_000_000, bytes_accessed=30_000_000, transcendentals=6_000_000
        ),
    )(
        leaf_states, norm_gain, wq_quant, wq_scale.T, wk, wk_scale.T, wv, wv_scale.T, wo_quant,
        wo_scale, q_bias, key_bias, value_bias, kcache, vcache, parent, length,
    )


def per_device_fused(n_actor, *args):
    return fused(n_actor, args)


def fits_fused(mesh_sizes, args):
    n_job, n_actor, n_tp = mesh_sizes
    return (
        n_tp == 2
        and n_job % 2 == 0
        and n_actor % 4 == 0
        and args[0].shape[0] % 32 == 0
        and args[2].shape[0] % SCALE_BLOCK == 0
        and (args[2].shape[1] // LANES) % 4 == 2
        and args[4].shape[1] == 2 * LANES
        and args[8].shape[1] == 5 * LANES
        and args[13].shape[0] == 2
    )


def per_device_any(mesh_sizes, *args):
    if fits_fused(mesh_sizes, args):
        return per_device_fused(mesh_sizes[1], *args)
    return per_device(mesh_sizes[:2], *args)


def solution(mesh):
    placed = (
        P(("job", "actor"), None),
        P(),
        P("actor", "tp"),
        P(None, "tp"),
        P("actor", "tp"),
        P(None, "tp"),
        P("actor", "tp"),
        P(None, "tp"),
        P("tp", "actor"),
        P("tp", None),
        P("tp"),
        P("tp"),
        P("tp"),
        P(("job", "actor"), None, "tp"),
        P(("job", "actor"), None, "tp"),
        P(("job", "actor")),
        P(("job", "actor")),
    )
    return jax.shard_map(
        functools.partial(
            per_device_any, (mesh.shape["job"], mesh.shape["actor"], mesh.shape["tp"])
        ),
        mesh=mesh,
        in_specs=placed,
        out_specs=P(("job", "actor"), None),
        check_vma=False,
    )
```

```python
import functools
import math

import jax
import jax.numpy as jnp
from jax import lax
from jax.experimental import pallas as pl
from jax.experimental.pallas import tpu as pltpu
from jax.sharding import PartitionSpec as P

HEAD_WIDTH = 128
SCALE_BLOCK = 128


epsilon = 1e-06
rope_base = 1000000.0


def apply_rotary(values, length):
    width = values.shape[-1]
    half_width = width // 2
    freqs = rope_base ** (-(jnp.arange(half_width, dtype=jnp.float32) * 2.0 / width))
    angles = length.astype(jnp.float32)[:, None] * freqs[None, :]
    cosine = jnp.cos(angles)[:, None, :]
    sine = jnp.sin(angles)[:, None, :]
    first = values[..., :half_width]
    second = values[..., half_width:]
    return jnp.concatenate(
        [first * cosine - second * sine, second * cosine + first * sine], axis=-1
    )


def attend_single_head(
    query_vector, key_self, value_self, prefix_key_cache, prefix_value_cache, parent, length
):
    scale_factor = 1.0 / math.sqrt(query_vector.shape[-1])
    self_score = (
        jnp.sum(
            query_vector.astype(jnp.float32) * key_self.astype(jnp.float32)[:, None, :], axis=-1
        )
        * scale_factor
    )
    visible = (jnp.arange(prefix_key_cache.shape[1])[None, :] < length[:, None])[:, None, :]
    outcome = jnp.zeros(query_vector.shape, jnp.float32)
    for prefix_index in range(prefix_key_cache.shape[0]):
        scores = (
            jnp.einsum(
                "lge,ce->lgc",
                query_vector,
                prefix_key_cache[prefix_index],
                preferred_element_type=jnp.float32,
            )
            * scale_factor
        )
        highest = jnp.maximum(jnp.max(jnp.where(visible, scores, -jnp.inf), axis=-1), self_score)
        weights = jnp.where(visible, jnp.exp(scores - highest[..., None]), 0.0)
        self_weight = jnp.exp(self_score - highest)
        total = jnp.sum(weights, axis=-1) + self_weight
        self_rounded = lax.optimization_barrier(self_weight.astype(jnp.bfloat16)).astype(
            jnp.float32
        )
        mixed = jnp.einsum(
            "lgc,ce->lge",
            weights.astype(jnp.bfloat16),
            prefix_value_cache[prefix_index],
            preferred_element_type=jnp.float32,
        )
        mixed = mixed + self_rounded[..., None] * value_self.astype(jnp.float32)[:, None, :]
        outcome = jnp.where(
            (parent == prefix_index)[:, None, None], mixed / total[..., None], outcome
        )
    return outcome


PIECE = 5
EARLY = 1


def spread_kernel(
    n_actor,
    rows_each,
    mine_ref,
    row_ref,
    gain_ref,
    sums_ref,
    all_ref,
    raw_ref,
    x_ref,
    home_sem,
    send_sem,
    recv_sem,
    row_sem,
):
    line = n_actor // 2
    actor = lax.axis_index("actor")
    job = lax.axis_index("job")
    at, y = actor // 2, actor % 2
    partner = job + 1 - 2 * (job % 2)
    pair = at * 2 + 1 - y
    has_up, has_down = at + 1 < line, at >= 1
    count = row_ref.shape[0]
    depth = mine_ref.shape[0]
    barrier = pltpu.get_barrier_semaphore()

    @pl.when(has_up)
    def _():
        pl.semaphore_signal(barrier, inc=1, device_id={"actor": actor + 2})

    @pl.when(has_down)
    def _():
        pl.semaphore_signal(barrier, inc=1, device_id={"actor": actor - 2})

    pl.semaphore_signal(barrier, inc=1, device_id={"actor": pair})
    pl.semaphore_signal(barrier, inc=1, device_id={"job": partner})
    pl.semaphore_wait(barrier, 2 + has_up.astype(jnp.int32) + has_down.astype(jnp.int32))

    def send(stream, source, piece, target, own=False):
        cut = pl.ds(piece * rows_each, rows_each)
        return pltpu.make_async_remote_copy(
            src_ref=mine_ref.at[cut] if own else all_ref.at[source, cut],
            dst_ref=all_ref.at[source, cut],
            send_sem=send_sem.at[stream, source, piece],
            recv_sem=recv_sem.at[source, piece],
            device_id={"actor": target},
        )

    def cross(source, piece, own=False):
        return send(0, source, piece, pair, own)

    def up(source, piece, own=False):
        return send(1, source, piece, actor + 2, own)

    def down(source, piece, own=False):
        return send(2, source, piece, actor - 2, own)

    def arrived(source, piece):
        cross(source, piece).wait_recv()

    late = list(range(PIECE - EARLY))
    early = list(range(PIECE - EARLY, PIECE))
    rows_copy = pltpu.make_async_remote_copy(
        src_ref=row_ref,
        dst_ref=raw_ref.at[pl.ds(count, count)],
        send_sem=row_sem.at[0],
        recv_sem=row_sem.at[1],
        device_id={"job": partner},
    )

    def both_ways(source, piece, own=False):
        @pl.when(has_up)
        def _():
            up(source, piece, own).start()

        @pl.when(has_down)
        def _():
            down(source, piece, own).start()

    for piece in early:
        cross(actor, piece, True).start()
    for piece in late:
        both_ways(actor, piece, True)
        cross(actor, piece, True).start()
    for piece in early:
        both_ways(actor, piece, True)
    rows_copy.start()
    home = pltpu.make_async_copy(mine_ref, all_ref.at[actor], home_sem.at[0])
    home.start()
    own_rows = pltpu.make_async_copy(row_ref, raw_ref.at[pl.ds(0, count)], home_sem.at[1])
    own_rows.start()

    def normalize(first):
        def block(i, carry):
            cut = pl.ds(pl.multiple_of(first + i * 16, 16), 16)
            rows = raw_ref[cut, :].astype(jnp.float32)
            rows = rows * lax.rsqrt(jnp.mean(rows * rows, axis=-1, keepdims=True) + epsilon)
            rows = (rows * gain_ref[...].astype(jnp.float32)).astype(jnp.bfloat16)
            for source in range(n_actor):
                x_ref[source, cut, :] = rows[:, source * depth : (source + 1) * depth]
            return carry

        lax.fori_loop(0, count // 16, block, 0)

    def add(source):
        sums_ref[...] += jnp.dot(
            x_ref[source], all_ref[source], preferred_element_type=jnp.float32
        )

    sums_ref[...] = jnp.zeros_like(sums_ref)
    own_rows.wait()
    normalize(0)
    for piece in early:
        arrived(pair, piece)
        both_ways(pair, piece)
    turn = jnp.where(at * 2 < line, 1, line - 1)

    def spot_of(k):
        return lax.rem(at + k * turn, line)

    for far in range(1, line):
        if far == line - 1:
            rows_copy.wait()
            normalize(count)
            home.wait()
            add(actor)
        todo = [(y, p) for p in late] + [(y, p) for p in early] + [(1 - y, p) for p in early]
        for index, (which, piece) in enumerate(todo):
            below = (at - far) * 2 + which
            above = (at + far) * 2 + which

            @pl.when(at >= far)
            def _():
                arrived(below, piece)

                @pl.when(has_up)
                def _():
                    up(below, piece).start()

                if index < len(late):
                    cross(below, piece).start()

            @pl.when(at + far < line)
            def _():
                arrived(above, piece)

                @pl.when(has_down)
                def _():
                    down(above, piece).start()

                if index < len(late):
                    cross(above, piece).start()

    def add_held(k, carry):
        add(spot_of(k) * 2 + y)
        return carry

    lax.fori_loop(1, line, add_held, 0)

    def add_crossed(k, carry):
        source = spot_of(k) * 2 + 1 - y
        for piece in late:
            arrived(source, piece)
        add(source)
        return carry

    lax.fori_loop(0, line, add_crossed, 0)
    for spot in range(line):
        for piece in late:
            cross(spot * 2 + y, piece).wait_send()
    for piece in early:
        cross(actor, piece).wait_send()
    for spot in range(line):
        items = [(y, p) for p in range(PIECE)] + [(1 - y, p) for p in early]
        for which, piece in items:
            source = spot * 2 + which

            @pl.when(jnp.logical_and(has_up, at >= spot))
            def _():
                up(source, piece).wait_send()

            @pl.when(jnp.logical_and(has_down, at <= spot))
            def _():
                down(source, piece).wait_send()


def spread(shard, rows, gain, n_actor):
    height, width = shard.shape
    return pl.pallas_call(
        functools.partial(spread_kernel, n_actor, height // PIECE),
        out_shape=jax.ShapeDtypeStruct((2 * rows.shape[0], width), jnp.float32),
        in_specs=[
            pl.BlockSpec(memory_space=pl.ANY),
            pl.BlockSpec(memory_space=pl.ANY),
            pl.BlockSpec(memory_space=pltpu.VMEM),
        ],
        out_specs=pl.BlockSpec(memory_space=pltpu.VMEM),
        scratch_shapes=[
            pltpu.VMEM((n_actor,) + shard.shape, shard.dtype),
            pltpu.VMEM((2 * rows.shape[0], rows.shape[1]), rows.dtype),
            pltpu.VMEM((n_actor, 2 * rows.shape[0], height), rows.dtype),
            pltpu.SemaphoreType.DMA((2,)),
            pltpu.SemaphoreType.DMA((3, n_actor, PIECE)),
            pltpu.SemaphoreType.DMA((n_actor, PIECE)),
            pltpu.SemaphoreType.DMA((2,)),
        ],
        compiler_params=pltpu.CompilerParams(
            collective_id=0, has_side_effects=True, vmem_limit_bytes=48 * 1024 * 1024
        ),
        cost_estimate=pl.CostEstimate(
            flops=0, bytes_accessed=300_000_000, transcendentals=0
        ),
    )(shard, rows, gain)


def per_device(
    mesh_sizes,
    leaf_states,
    norm_gain,
    wq_quant,
    wq_scale,
    key_weight_quantized,
    key_weight_scale,
    value_weight_quantized,
    value_weight_scale,
    wo_quant,
    wo_scale,
    q_bias,
    key_bias,
    value_bias,
    prefix_key_cache,
    prefix_value_cache,
    parent_prefix_slot,
    prefix_length,
):
    n_job, n_actor = mesh_sizes
    swap = [(i, i ^ 1) for i in range(n_job)]
    side = lax.axis_index("job") % 2
    actor = lax.axis_index("actor")

    def trade(x):
        return lax.ppermute(x, "job", swap)

    leaf_count = leaf_states.shape[0]

    def half_cols(x):
        width = x.shape[1] // 2
        return lax.dynamic_slice_in_dim(x, side * width, width, 1)

    row_count = wq_quant.shape[0]

    def expand_rows(quant, scale):
        mine = lax.dynamic_slice_in_dim(
            scale, actor * (row_count // SCALE_BLOCK), row_count // SCALE_BLOCK, 0
        ) if row_count % SCALE_BLOCK == 0 else None
        if mine is None:
            tall = jnp.repeat(scale, SCALE_BLOCK, axis=0)
            tall = lax.dynamic_slice_in_dim(tall, actor * row_count, row_count, 0)
        else:
            tall = jnp.repeat(mine, SCALE_BLOCK, axis=0)
        wide = jnp.repeat(half_cols(tall), SCALE_BLOCK, axis=1)
        return (half_cols(quant).astype(jnp.float32) * wide).astype(jnp.bfloat16)

    qkv_local = jnp.concatenate(
        [
            expand_rows(wq_quant, wq_scale),
            expand_rows(key_weight_quantized, key_weight_scale),
            expand_rows(value_weight_quantized, value_weight_scale),
        ],
        axis=1,
    )
    col_count = wo_quant.shape[1]
    spread_scale = jnp.repeat(wo_scale, SCALE_BLOCK, axis=1)
    own_scale = half_cols(lax.dynamic_slice_in_dim(spread_scale, actor * col_count, col_count, 1))
    wo_local = (
        half_cols(wo_quant).astype(jnp.float32) * jnp.repeat(own_scale, SCALE_BLOCK, axis=0)
    ).astype(jnp.bfloat16).T
    sums = spread(qkv_local, leaf_states, norm_gain[None, :], n_actor)
    wo_local, sums, prefix_length = lax.optimization_barrier((wo_local, sums, prefix_length))
    both_length = jnp.concatenate([prefix_length, trade(prefix_length)], axis=0)

    def half_row(x):
        width = x.shape[0] // 2
        return lax.dynamic_slice_in_dim(x, side * width, width, 0)

    bias = jnp.concatenate([half_row(q_bias), half_row(key_bias), half_row(value_bias)])
    sums = sums + bias.astype(jnp.float32)
    v_width = value_bias.shape[0] // 2
    rot_width = sums.shape[1] - v_width
    rotated = apply_rotary(
        sums[:, :rot_width].reshape(2 * leaf_count, rot_width // HEAD_WIDTH, HEAD_WIDTH),
        both_length,
    ).reshape(2 * leaf_count, rot_width)
    done = jnp.concatenate([rotated, sums[:, rot_width:]], axis=1).astype(jnp.bfloat16)
    own = done[:leaf_count]
    other = trade(done[leaf_count:])
    q_width = q_bias.shape[0] // 2

    kv_half = v_width // HEAD_WIDTH
    query_group = q_bias.shape[0] // key_bias.shape[0]
    outs = []
    for which, block in ((side, own), (1 - side, other)):
        q = block[:, :q_width].reshape(leaf_count, kv_half, query_group, HEAD_WIDTH)
        k = block[:, q_width : q_width + v_width].reshape(leaf_count, kv_half, HEAD_WIDTH)
        v = block[:, q_width + v_width :].reshape(leaf_count, kv_half, HEAD_WIDTH)
        for head in range(kv_half):
            at = (which * kv_half + head) * HEAD_WIDTH
            outs.append(
                attend_single_head(
                    q[:, head],
                    k[:, head],
                    v[:, head],
                    lax.dynamic_slice_in_dim(prefix_key_cache, at, HEAD_WIDTH, 2),
                    lax.dynamic_slice_in_dim(prefix_value_cache, at, HEAD_WIDTH, 2),
                    parent_prefix_slot,
                    prefix_length,
                )
                .reshape(leaf_count, query_group * HEAD_WIDTH)
                .astype(jnp.bfloat16)
            )
    mine = jnp.concatenate(outs[:kv_half], axis=1)
    theirs = jnp.concatenate(outs[kv_half:], axis=1)
    attended = jnp.where(
        side == 0,
        jnp.concatenate([mine, theirs], axis=1),
        jnp.concatenate([theirs, mine], axis=1),
    )

    wo_all = lax.all_gather(wo_local, "actor", axis=0, tiled=True)
    group = lax.axis_index("tp")
    cores = [(0, 1), (1, 0)]

    def project(rows):
        part = lax.dot_general(
            rows, wo_all, (((1,), (1,)), ((), ())), preferred_element_type=jnp.float32
        )
        width = part.shape[1] // 2
        first, second = part[:, :width], part[:, width:]
        give = jnp.where(group == 0, second, first)
        keep = jnp.where(group == 0, first, second)
        return (keep + lax.ppermute(give, "tp", cores)).astype(jnp.bfloat16), give

    def join(x):
        y = lax.ppermute(x, "tp", cores)
        return jnp.where(
            group == 0,
            jnp.concatenate([x, y], axis=1),
            jnp.concatenate([y, x], axis=1),
        )

    away, marker = project(trade(attended))
    attended, away, _ = lax.optimization_barrier((attended, away, marker))
    away = trade(away)
    local = join(project(attended)[0])
    remote = join(away)
    low = jnp.where(side == 0, local, remote)
    high = jnp.where(side == 0, remote, local)
    pieces = []
    half = col_count // 2
    for a in range(n_actor):
        pieces += [low[:, a * half : (a + 1) * half], high[:, a * half : (a + 1) * half]]
    return jnp.concatenate(pieces, axis=1)


LANES = 128


def fused_kernel(
    n_actor,
    states_ref,
    gain_ref,
    wq_ref,
    wq_scale_ref,
    wk_ref,
    wk_scale_ref,
    wv_ref,
    wv_scale_ref,
    wo_ref,
    wo_scale_ref,
    qb_ref,
    kb_ref,
    vb_ref,
    kcache_ref,
    vcache_ref,
    parent_ref,
    length_ref,
    out_ref,
    raw_ref,
    rawv_ref,
    wown_ref,
    woth_ref,
    give_ref,
    xraw_ref,
    xs_ref,
    lens_ref,
    tabs_ref,
    gains_ref,
    bias_ref,
    acc_ref,
    rst_ref,
    vst_ref,
    rq_ref,
    rv_ref,
    kc_ref,
    vc_ref,
    woraw_ref,
    zset_ref,
    att_ref,
    psend_ref,
    precv_ref,
    res_ref,
    whole_ref,
    load_sem,
    kv_sem,
    z_send,
    z_recv,
    g_send,
    x_send,
    x_recv,
    xs_send,
    xs_recv,
    t_send,
    t_recv,
    q_send,
    q_recv,
    v_send,
    v_recv,
    a_send,
    a_recv,
    oz_send,
    oz_recv,
    p_send,
    p_recv,
    c_send,
    c_recv,
    f_send,
    f_recv,
):
    line = n_actor // 2
    actor = lax.axis_index("actor")
    job = lax.axis_index("job")
    core = lax.axis_index("tp")
    at, y = actor // 2, actor % 2
    side = job % 2
    there = {"job": job + 1 - 2 * side}
    pair = {"actor": at * 2 + 1 - y}
    diagonal = {"job": job + 1 - 2 * side, "actor": at * 2 + 1 - y}
    sibling = {"tp": 1 - core}
    above, below = {"actor": actor + 2}, {"actor": actor - 2}
    has_up, has_down = at + 1 < line, at >= 1
    middle = jnp.logical_and(has_up, has_down)
    ends = jnp.logical_not(middle)
    rows = raw_ref.shape[1]
    count = xraw_ref.shape[0]
    half_rows = rows // 2
    half_count = count // 2
    width = raw_ref.shape[2]
    units = width // LANES
    heads = 2 * units - 1
    depth = zset_ref.shape[1]
    strips = n_actor // 2
    part = strips // 2
    f32, bf16 = jnp.float32, jnp.bfloat16

    def lanes(unit, n=1):
        return pl.ds(pl.multiple_of(unit * LANES, LANES), n * LANES)

    barrier = pltpu.get_barrier_semaphore()

    @pl.when(has_up)
    def _():
        pl.semaphore_signal(barrier, inc=1, device_id=above)

    @pl.when(has_down)
    def _():
        pl.semaphore_signal(barrier, inc=1, device_id=below)

    for peer in (there, pair, diagonal, sibling):
        pl.semaphore_signal(barrier, inc=1, device_id=peer)

    def local(source, target, sem):
        return pltpu.make_async_copy(source, target, sem)

    def remote(source, target, ss, rs, peer):
        return pltpu.make_async_remote_copy(
            src_ref=source, dst_ref=target, send_sem=ss, recv_sem=rs, device_id=peer
        )

    first = 2 * side
    w_loads = [
        local(wq_ref.at[:, lanes(side * heads, units)], raw_ref.at[0], load_sem.at[0]),
        local(
            wq_ref.at[:, lanes(side * heads + units, units - 1)],
            raw_ref.at[1, :, pl.ds(0, (units - 1) * LANES)],
            load_sem.at[1],
        ),
        local(
            wk_ref.at[:, lanes(side)],
            raw_ref.at[1, :, pl.ds((units - 1) * LANES, LANES)],
            load_sem.at[2],
        ),
        local(wv_ref.at[:, lanes(side)], rawv_ref, load_sem.at[3]),
    ]
    state_load = local(states_ref, xraw_ref, load_sem.at[4])
    wo_load = local(
        wo_ref.at[:, lanes(first, 2)], woraw_ref.at[:, pl.ds(0, 2 * LANES)], load_sem.at[5]
    )
    wo_load_last = local(
        wo_ref.at[:, pl.ds(4 * LANES, LANES)], woraw_ref.at[:, pl.ds(2 * LANES, LANES)],
        load_sem.at[6],
    )
    for copy in w_loads:
        copy.start()
    state_load.start()
    wo_load.start()
    wo_load_last.start()
    kv_loads = []
    for j in range(2):
        for p in range(2):
            place = pl.ds(p * LANES, LANES)
            cut = pl.ds(j * LANES, LANES)
            kv_loads.append(
                local(kcache_ref.at[p, :, cut], kc_ref.at[j, :, place], kv_sem.at[0, j, p])
            )
            kv_loads.append(
                local(vcache_ref.at[p, :, cut], vc_ref.at[j, :, place], kv_sem.at[1, j, p])
            )
    for copy in kv_loads:
        copy.start()

    blocks = rows // SCALE_BLOCK

    def pick(ref, row, column):
        values = ref[pl.ds(row, 1), :]
        here = lax.broadcasted_iota(jnp.int32, values.shape, 1) == column
        return jnp.sum(jnp.where(here, values, 0.0), axis=1, keepdims=True)

    def unit_scale(parity, block, u):
        row = actor * blocks + block
        if u < units - 1:
            return pick(wq_scale_ref, side * heads + u + units * parity, row)
        return jnp.where(
            parity == 0,
            pick(wq_scale_ref, side * heads + u, row),
            pick(wk_scale_ref, side, row),
        )

    def expand(parity, target):
        for block in range(blocks):
            cut = pl.ds(block * SCALE_BLOCK, SCALE_BLOCK)
            for u in range(units):
                lane = pl.ds(u * LANES, LANES)
                scaled = raw_ref[parity, cut, lane].astype(f32) * unit_scale(parity, block, u)
                target(cut, lane, scaled.astype(bf16))

    def to_give(cut, lane, value):
        give_ref[cut, lane] = value

    def to_own(cut, lane, value):
        wown_ref[at, cut, lane] = value

    for copy in w_loads:
        copy.wait()
    expand(1 - y, to_give)
    pl.semaphore_wait(barrier, 4 + has_up.astype(jnp.int32) + has_down.astype(jnp.int32))

    def half(p):
        return pl.ds(p * half_rows, half_rows)

    def give(p):
        return remote(
            give_ref.at[half(p)], woth_ref.at[at, half(p)], g_send.at[p], z_recv.at[1, at, p], pair
        )

    for p in range(2):
        give(p).start()
    expand(y, to_own)
    for block in range(blocks):
        cut = pl.ds(block * SCALE_BLOCK, SCALE_BLOCK)
        scale = pick(wv_scale_ref, side, actor * blocks + block)
        wown_ref[at, cut, pl.ds(width, LANES)] = (rawv_ref[cut, :].astype(f32) * scale).astype(
            bf16
        )

    def up_down(way, kind, spot, p):
        ref = (wown_ref if kind == 0 else woth_ref).at[spot, half(p)]
        return remote(
            ref, ref, z_send.at[way, kind, spot, p], z_recv.at[kind, spot, p], (above, below)[way]
        )

    def both_ways(kind, spot, p):
        @pl.when(has_up)
        def _():
            up_down(0, kind, spot, p).start()

        @pl.when(has_down)
        def _():
            up_down(1, kind, spot, p).start()

    for p in range(2):
        both_ways(0, at, p)

    lens_ref[0] = length_ref[...].astype(f32).reshape(1, count)
    table_sends = [
        remote(lens_ref.at[0], lens_ref.at[slot], t_send.at[slot], t_recv.at[slot], peer)
        for slot, peer in ((1, there), (2, pair), (3, diagonal))
    ]
    for copy in table_sends:
        copy.start()

    state_load.wait()

    gains_ref[...] = gain_ref[...].astype(f32).reshape(1, -1)
    for i, ref in enumerate((qb_ref, kb_ref, vb_ref)):
        bias_ref[i, :, : ref.shape[0]] = ref[...].astype(f32).reshape(1, -1)

    def normalize(i, carry):
        cut = pl.ds(pl.multiple_of(i * 16, 16), 16)
        x = xraw_ref[cut, :].astype(f32)
        x = x * lax.rsqrt(jnp.mean(x * x, axis=-1, keepdims=True) + epsilon)
        x = (x * gains_ref[...]).astype(bf16)
        for source in range(n_actor):
            xs_ref[source, cut, :] = x[:, source * rows : (source + 1) * rows]
        return carry

    lax.fori_loop(0, count // 16, normalize, 0)

    def some(p):
        return pl.ds(core * strips + p * part, part)

    def of_slot(slot):
        return pl.ds(slot * count, count)

    def share(slot, p, origin, peer):
        return remote(
            xs_ref.at[some(p), of_slot(origin)],
            xs_ref.at[some(p), of_slot(slot)],
            x_send.at[slot - 1, p],
            x_recv.at[slot - 1, p],
            peer,
        )

    share_list = [
        share(1, 0, 0, there),
        share(2, 1, 0, pair),
        share(1, 1, 0, there),
        share(2, 0, 0, pair),
    ]
    for copy in share_list:
        copy.start()

    def to_sibling(slot, p):
        ref = xs_ref.at[some(p), of_slot(slot)]
        return remote(ref, ref, xs_send.at[slot - 1, p], xs_recv.at[slot - 1, p], sibling)

    def from_sibling(slot, p):
        ref = xs_ref.at[pl.ds((1 - core) * strips + p * part, part), of_slot(slot)]
        return remote(ref, ref, xs_send.at[slot - 1, p], xs_recv.at[slot - 1, p], sibling)

    def column(values):
        wide = jnp.broadcast_to(values, (LANES, count))
        return wide.T

    lane_at = lax.broadcasted_iota(jnp.int32, (count, LANES), 1)
    step = lax.rem(lax.broadcasted_iota(jnp.int32, (1, LANES), 1), LANES // 2).astype(f32)
    freqs = jnp.exp(step * (-2.0 * math.log(rope_base) / LANES))
    def make_table(slot):
        angles = column(lens_ref[slot]) * freqs
        tabs_ref[slot] = jnp.where(lane_at < LANES // 2, jnp.cos(angles), jnp.sin(angles))


    wo_load.wait()
    wo_load_last.wait()
    wo_blocks = depth // SCALE_BLOCK
    wo_units = wo_ref.shape[1] // LANES

    def expand_wo(block, carry):
        cut = pl.ds(pl.multiple_of(block * SCALE_BLOCK, SCALE_BLOCK), SCALE_BLOCK)
        for u in range(2):
            lane = pl.ds(u * LANES, LANES)
            scale = pick(wo_scale_ref, block, actor * wo_units + first + u)
            zset_ref[at, cut, lane] = (woraw_ref[cut, lane].astype(f32) * scale).astype(bf16)
        return carry

    lax.fori_loop(0, wo_blocks, expand_wo, 0)

    half_depth = depth // 2

    def has_extra(spot, s):
        return spot % 2 == s

    @pl.when(has_extra(at, side))
    def _():
        def expand_last(block, carry):
            cut = pl.ds(pl.multiple_of(block * SCALE_BLOCK, SCALE_BLOCK), SCALE_BLOCK)
            lane = pl.ds(2 * LANES, LANES)
            scale = pick(wo_scale_ref, block, actor * wo_units + 4)
            zset_ref[at, cut, lane] = (woraw_ref[cut, lane].astype(f32) * scale).astype(bf16)
            return carry

        lax.fori_loop(0, wo_blocks, expand_last, 0)

    def wo_way(way, spot, q):
        if q < 2:
            ref = zset_ref.at[spot, pl.ds(q * half_depth, half_depth), pl.ds(0, 2 * LANES)]
        else:
            ref = zset_ref.at[spot, :, pl.ds(2 * LANES, LANES)]
        return remote(
            ref, ref, oz_send.at[way, spot, q], oz_recv.at[spot, q], (above, below)[way]
        )

    def each_piece(spot, action):
        for q in range(2):
            action(q)

        @pl.when(has_extra(spot, side))
        def _():
            action(2)

    def wo_begin(far):
        @pl.when(jnp.logical_and(at == far, has_up))
        def _():
            each_piece(at, lambda q: wo_way(0, at, q).start())

        @pl.when(jnp.logical_and(line - 1 - at == far, has_down))
        def _():
            each_piece(at, lambda q: wo_way(1, at, q).start())

    def relay_one(way, spot):
        def action(q):
            wo_way(way, spot, q).wait_recv()

            @pl.when((has_up, has_down)[way])
            def _():
                wo_way(way, spot, q).start()

        each_piece(spot, action)

    def relay(far):
        @pl.when(at >= far)
        def _():
            relay_one(0, at - far)

        @pl.when(at + far < line)
        def _():
            relay_one(1, at + far)

    for p in range(2):
        give(p).wait_recv()
        both_ways(1, at, p)
    wo_begin(0)

    acc_ref[...] = jnp.zeros_like(acc_ref)
    make_table(0)
    for slot in (1, 2, 3):
        table_sends[slot - 1].wait_recv()
        make_table(slot)

    def multiply(spot):
        acc_ref[...] += jnp.dot(
            xs_ref[spot * 2 + y], wown_ref[spot], preferred_element_type=f32
        )
        acc_ref[:, :width] += jnp.dot(
            xs_ref[spot * 2 + 1 - y], woth_ref[spot], preferred_element_type=f32
        )

    def multiply_far(far, carry):
        @pl.when(at >= far)
        def _():
            multiply(at - far)

        @pl.when(jnp.logical_and(at + far < line, far > 0))
        def _():
            multiply(at + far)

        return carry

    def rows_first():
        for slot, p, peer in ((1, 0, pair), (2, 1, there), (1, 1, None), (2, 0, None)):
            share(slot, p, 0, there if slot == 1 else pair).wait_recv()
            if peer is not None:
                share(3, p, slot, peer).start()
            to_sibling(slot, p).start()

    def rows_rest():
        for p in range(2):
            share(3, p, 1 + p, pair if p == 0 else there).wait_recv()
            to_sibling(3, p).start()

        for slot in (1, 2, 3):
            for p in range(2):
                from_sibling(slot, p).wait_recv()

    for far in range(1, line):
        for kind in range(2):
            for p in range(2):

                @pl.when(at >= far)
                def _():
                    up_down(0, kind, at - far, p).wait_recv()

                    @pl.when(has_up)
                    def _():
                        up_down(0, kind, at - far, p).start()

                @pl.when(at + far < line)
                def _():
                    up_down(1, kind, at + far, p).wait_recv()

                    @pl.when(has_down)
                    def _():
                        up_down(1, kind, at + far, p).start()

        wo_begin(far)
        if far == 1:
            rows_first()
        if far == max(line - 2, 1):
            rows_rest()
            lax.fori_loop(0, max(line - 1, 1), multiply_far, 0)
    multiply_far(line - 1, 0)

    def results(slot):
        return (
            remote(rst_ref.at[slot], rq_ref.at[slot], q_send.at[slot], q_recv.at[slot], peers[slot]),
            remote(vst_ref.at[slot], rv_ref.at[slot], v_send.at[slot], v_recv.at[slot], peers[slot]),
        )

    peers = {1: there, 2: pair, 3: diagonal}
    for slot in (2, 1, 3, 0):
        table = tabs_ref[slot]
        swapped = pltpu.roll(table, LANES // 2, 1)
        cosine = jnp.where(lane_at < LANES // 2, table, swapped)
        sine = jnp.where(lane_at < LANES // 2, -swapped, table)
        for u in range(units):
            if u < units - 1:
                bias = bias_ref[0, :, lanes(side * heads + u + units * y)]
            else:
                bias = jnp.where(
                    y == 0,
                    bias_ref[0, :, lanes(side * heads + u)],
                    bias_ref[1, :, lanes(side)],
                )
            value = acc_ref[of_slot(slot), u * LANES : (u + 1) * LANES] + bias
            value = value * cosine + pltpu.roll(value, LANES // 2, 1) * sine
            (rst_ref if slot else rq_ref)[slot, u] = value.astype(bf16)
        (vst_ref if slot else rv_ref)[slot] = acc_ref[of_slot(slot), width:]
        if slot:
            for copy in results(slot):
                copy.start()

    @pl.when(middle)
    def _():
        relay(1)

    for copy in kv_loads:
        copy.wait()
    parent = column(parent_ref[...].astype(f32).reshape(1, count))[:, :1]
    length = column(lens_ref[0])[:, :1].astype(jnp.int32)
    in_first = (parent == 0).astype(f32)
    in_second = 1.0 - in_first
    scale_factor = math.log2(math.e) / math.sqrt(LANES)

    def hand(slot, j, origin, peer):
        cut = lanes(j * heads, heads)

        def of(k):
            return att_ref.at[:, pl.ds(k * half_count, half_count), cut]

        return remote(
            of(origin),
            of(slot),
            a_send.at[slot - 1, origin - 1 if slot == 3 else j],
            a_recv.at[slot - 1, j],
            peer,
        )

    chunks = 4
    context = kc_ref.shape[1] // chunks

    def attend(base):
        group = side if base == 0 else 1 - side
        low = jnp.where(y == 0, base, base + 2)
        high = jnp.where(y == 0, base + 2, base)
        key_new = rq_ref[high, units - 1].astype(f32)
        value_new = rv_ref[base] + rv_ref[base + 2] + bias_ref[2, :, lanes(group)]
        value_new = value_new.astype(bf16).astype(f32)

        def head(h, carry):
            query = rq_ref[
                jnp.where(h < units, low, high), jnp.where(h < units, h, h - units)
            ].astype(f32)
            own = jnp.sum(query * key_new, axis=-1, keepdims=True) * scale_factor
            both = jnp.concatenate([query * in_first, query * in_second], axis=1).astype(bf16)
            highest = own
            pieces = []
            for c in range(chunks):
                scores = lax.dot_general(
                    both,
                    kc_ref[group, c * context : (c + 1) * context],
                    (((1,), (1,)), ((), ())),
                    preferred_element_type=f32,
                )
                place = c * context + lax.broadcasted_iota(jnp.int32, scores.shape, 1)
                scores = jnp.where(place < length, scores * scale_factor, -jnp.inf)
                highest = jnp.maximum(highest, jnp.max(scores, axis=-1, keepdims=True))
                pieces.append(scores)
            own = jnp.exp2(own - highest)
            total, mixed = own, None
            for c, scores in enumerate(pieces):
                weights = jnp.exp2(scores - highest)
                total = total + jnp.sum(weights, axis=-1, keepdims=True)
                more = jnp.dot(
                    weights.astype(bf16),
                    vc_ref[group, c * context : (c + 1) * context],
                    preferred_element_type=f32,
                )
                mixed = more if mixed is None else mixed + more
            mixed = jnp.where(parent == 0, mixed[:, :LANES], mixed[:, LANES:])
            mixed = mixed + own.astype(bf16).astype(f32) * value_new
            mixed = (mixed / total).astype(bf16)
            for which in range(2):
                att_ref[which, :half_count, lanes(group * heads + h)] = mixed[
                    which * half_count : (which + 1) * half_count
                ]
            return carry

        lax.fori_loop(0, heads, head, 0)
        hand(1, group, 0, there).start()
        hand(2, group, 0, pair).start()

    for copy in results(2):
        copy.wait_recv()
    attend(0)

    for slot in (1, 3):
        for copy in results(slot):
            copy.wait_recv()
    attend(1)
    hand(2, side, 0, pair).wait_recv()
    hand(3, side, 2, there).start()
    hand(1, side, 0, there).wait_recv()
    hand(3, side, 1, pair).start()

    @pl.when(middle)
    def _():
        relay(2)

    hand(1, 1 - side, 0, there).wait_recv()
    hand(2, 1 - side, 0, pair).wait_recv()

    bounds = (pl.ds(0, 2 * LANES), pl.ds(2 * LANES, LANES))

    groups = ((0, 3), (3, 1))

    def rows_of(g):
        return pl.ds(groups[g][0] * half_count, groups[g][1] * half_count)

    def p_copy(spot, k, g):
        return remote(
            psend_ref.at[spot, rows_of(g), bounds[k]],
            precv_ref.at[spot, rows_of(g), bounds[k]],
            p_send.at[spot, k, g],
            p_recv.at[spot, k, g],
            sibling,
        )

    def unit_of(spot, s, parity, k):
        return wo_units * (2 * spot + parity) + (4 if k else 2 * s)

    def target(spot, s, parity, k):
        mine = pl.ds(pl.multiple_of(core * half_count, half_count), half_count)
        return whole_ref.at[mine, lanes(unit_of(spot, s, parity, k), 1 if k else 2)]

    def result(spot, slot, k):
        return res_ref.at[spot, pl.ds(slot * half_count, half_count), bounds[k]]

    def sibling_copy(spot, k):
        return remote(
            target(spot, side, y, k),
            target(spot, side, y, k),
            f_send.at[0, spot, k],
            f_recv.at[0, spot, k],
            sibling,
        )

    def send_copy(spot, slot, k):
        return remote(
            result(spot, slot, k),
            target(spot, side, y, k),
            c_send.at[slot - 1, spot, k],
            c_recv.at[slot - 1, spot, k],
            peers[slot],
        )

    source_side = (side, 1 - side, side, 1 - side)
    source_parity = (y, y, 1 - y, 1 - y)

    def onward_copy(spot, slot, k):
        ref = target(spot, source_side[slot], source_parity[slot], k)
        return remote(ref, ref, f_send.at[slot, spot, k], f_recv.at[slot, spot, k], sibling)

    def send_part(spot, k, g):
        psend_ref[spot, rows_of(g), bounds[k]] = jnp.dot(
            att_ref[1 - core, rows_of(g)], zset_ref[spot, :, bounds[k]], preferred_element_type=f32
        )
        p_copy(spot, k, g).start()

    def keep_part(spot, k, g):
        kept = jnp.dot(
            att_ref[core, rows_of(g)], zset_ref[spot, :, bounds[k]], preferred_element_type=f32
        )
        p_copy(spot, k, g).wait_recv()
        kept = (kept + precv_ref[spot, rows_of(g), bounds[k]]).astype(bf16)
        res_ref[spot, rows_of(g), bounds[k]] = kept
        if g == 1:
            send_copy(spot, 3, k).start()
            return
        for slot in (1, 2):
            send_copy(spot, slot, k).start()
        mine = pl.ds(pl.multiple_of(core * half_count, half_count), half_count)
        whole_ref[mine, lanes(unit_of(spot, side, y, k), 1 if k else 2)] = kept[:half_count]
        sibling_copy(spot, k).start()

    def each_part(spot, s, action):
        action(0)

        @pl.when(has_extra(spot, s))
        def _():
            action(1)

    def project_send(spot, g):
        each_part(spot, side, lambda k: send_part(spot, k, g))

    def project_keep(spot, g):
        each_part(spot, side, lambda k: keep_part(spot, k, g))

    def onward(spot):
        for slot in (1, 2, 3):

            def action(k):
                send_copy(spot, slot, k).wait_recv()
                onward_copy(spot, slot, k).start()

            each_part(spot, source_side[slot], action)

    def at_far(action, far):
        @pl.when(at >= far)
        def _():
            action(at - far)

        @pl.when(jnp.logical_and(at + far < line, far > 0))
        def _():
            action(at + far)

    def relays(far, carry):
        @pl.when(jnp.logical_and(far > 0, jnp.logical_or(ends, far > 2)))
        def _():
            relay(far)

        return carry

    def sends(g):
        def body(far, carry):
            if g == 0:
                relays(far, 0)
            at_far(lambda spot: project_send(spot, g), far)
            return carry

        return body

    def keeps(g):
        def body(far, carry):
            at_far(lambda spot: project_keep(spot, g), far)
            return carry

        return body

    def onwards(far, carry):
        at_far(onward, far)
        return carry

    lax.fori_loop(0, line - 1, sends(0), 0)
    lax.fori_loop(0, line - 1, keeps(0), 0)
    for j in range(2):
        hand(3, j, 1, pair).wait_recv()
    lax.fori_loop(0, line - 1, sends(1), 0)
    lax.fori_loop(0, line - 1, keeps(1), 0)

    @pl.when(ends)
    def _():
        relay(line - 1)
        for g in range(2):
            at_far(lambda spot: project_send(spot, g), line - 1)
        for g in (1, 0):
            at_far(lambda spot: project_keep(spot, g), line - 1)

    lax.fori_loop(0, line, onwards, 0)

    for p in range(2):
        give(p).wait_send()
        for slot, peer in ((1, there), (2, pair), (3, pair)):
            share(slot, p, 0, peer).wait_send()
            to_sibling(slot, p).wait_send()
    for copy in table_sends:
        copy.wait_send()
    for slot in (1, 2, 3):
        for copy in results(slot):
            copy.wait_send()
    for j in range(2):
        for slot in (1, 2, 3):
            hand(slot, j, j + 1 if slot == 3 else 0, there).wait_send()

    def finish(spot, carry):
        @pl.when(jnp.logical_and(has_up, at >= spot))
        def _():
            for kind in range(2):
                for p in range(2):
                    up_down(0, kind, spot, p).wait_send()
            each_piece(spot, lambda q: wo_way(0, spot, q).wait_send())

        @pl.when(jnp.logical_and(has_down, at <= spot))
        def _():
            for kind in range(2):
                for p in range(2):
                    up_down(1, kind, spot, p).wait_send()
            each_piece(spot, lambda q: wo_way(1, spot, q).wait_send())

        def end_part(k):
            for g in range(2):
                p_copy(spot, k, g).wait_send()
            sibling_copy(spot, k).wait()
            for slot in (1, 2, 3):
                send_copy(spot, slot, k).wait_send()

        each_part(spot, side, end_part)
        for slot in (1, 2, 3):
            each_part(
                spot, source_side[slot], lambda k: onward_copy(spot, slot, k).wait()
            )
        return carry

    lax.fori_loop(0, line, finish, 0)
    pltpu.sync_copy(whole_ref, out_ref)


def fused(n_actor, args):
    (
        leaf_states, norm_gain, wq_quant, wq_scale, wk, wk_scale, wv, wv_scale, wo_quant, wo_scale,
        q_bias, key_bias, value_bias, kcache, vcache, parent, length,
    ) = args
    count, features = leaf_states.shape
    rows = wq_quant.shape[0]
    heads = wq_quant.shape[1] // (2 * LANES)
    units = (heads + 1) // 2
    width = units * LANES
    context = kcache.shape[1]
    depth = wo_quant.shape[0]
    line = n_actor // 2
    total_units = n_actor * (wo_quant.shape[1] // LANES)
    bf16, f32 = jnp.bfloat16, jnp.float32
    any_space = pl.BlockSpec(memory_space=pl.ANY)
    vmem = pl.BlockSpec(memory_space=pltpu.VMEM)
    dma = pltpu.SemaphoreType.DMA
    return pl.pallas_call(
        functools.partial(fused_kernel, n_actor),
        out_shape=jax.ShapeDtypeStruct((count, total_units * LANES), bf16),
        in_specs=[
            any_space, vmem, any_space, vmem, any_space, vmem, any_space, vmem, any_space, vmem,
            vmem, vmem, vmem, any_space, any_space, vmem, vmem,
        ],
        out_specs=any_space,
        scratch_shapes=[
            pltpu.VMEM((2, rows, width), bf16),
            pltpu.VMEM((rows, LANES), bf16),
            pltpu.VMEM((line, rows, width + LANES), bf16),
            pltpu.VMEM((line, rows, width), bf16),
            pltpu.VMEM((rows, width), bf16),
            pltpu.VMEM((count, features), bf16),
            pltpu.VMEM((n_actor, 4 * count, rows), bf16),
            pltpu.VMEM((4, 1, count), f32),
            pltpu.VMEM((4, count, LANES), f32),
            pltpu.VMEM((1, features), f32),
            pltpu.VMEM((3, 1, 2 * heads * LANES), f32),
            pltpu.VMEM((4 * count, width + LANES), f32),
            pltpu.VMEM((4, units, count, LANES), bf16),
            pltpu.VMEM((4, count, LANES), f32),
            pltpu.VMEM((4, units, count, LANES), bf16),
            pltpu.VMEM((4, count, LANES), f32),
            pltpu.VMEM((2, context, 2 * LANES), bf16),
            pltpu.VMEM((2, context, 2 * LANES), bf16),
            pltpu.VMEM((depth, 3 * LANES), bf16),
            pltpu.VMEM((line, depth, 3 * LANES), bf16),
            pltpu.VMEM((2, 2 * count, 2 * heads * LANES), bf16),
            pltpu.VMEM((line, 2 * count, 3 * LANES), f32),
            pltpu.VMEM((line, 2 * count, 3 * LANES), f32),
            pltpu.VMEM((line, 2 * count, 3 * LANES), bf16),
            pltpu.VMEM((count, total_units * LANES), bf16),
            dma((7,)),
            dma((2, 2, 2)),
            dma((2, 2, line, 2)),
            dma((2, line, 2)),
            dma((2,)),
            dma((3, 2)),
            dma((3, 2)),
            dma((3, 2)),
            dma((3, 2)),
            dma((4,)),
            dma((4,)),
            dma((4,)),
            dma((4,)),
            dma((4,)),
            dma((4,)),
            dma((3, 2)),
            dma((3, 2)),
            dma((2, line, 3)),
            dma((line, 3)),
            dma((line, 2, 2)),
            dma((line, 2, 2)),
            dma((3, line, 2)),
            dma((3, line, 2)),
            dma((4, line, 2)),
            dma((4, line, 2)),
        ],
        compiler_params=pltpu.CompilerParams(
            collective_id=0, has_side_effects=True, vmem_limit_bytes=58 * 1024 * 1024
        ),
        cost_estimate=pl.CostEstimate(
            flops=13_000_000_000, bytes_accessed=30_000_000, transcendentals=6_000_000
        ),
    )(
        leaf_states, norm_gain, wq_quant, wq_scale.T, wk, wk_scale.T, wv, wv_scale.T, wo_quant,
        wo_scale, q_bias, key_bias, value_bias, kcache, vcache, parent, length,
    )


def per_device_fused(n_actor, *args):
    return fused(n_actor, args)


def fits_fused(mesh_sizes, args):
    n_job, n_actor, n_tp = mesh_sizes
    return (
        n_tp == 2
        and n_job % 2 == 0
        and n_actor % 4 == 0
        and args[0].shape[0] % 32 == 0
        and args[2].shape[0] % SCALE_BLOCK == 0
        and (args[2].shape[1] // LANES) % 4 == 2
        and args[4].shape[1] == 2 * LANES
        and args[8].shape[1] == 5 * LANES
        and args[13].shape[0] == 2
    )


def per_device_any(mesh_sizes, *args):
    if fits_fused(mesh_sizes, args):
        return per_device_fused(mesh_sizes[1], *args)
    return per_device(mesh_sizes[:2], *args)


def solution(mesh):
    placed = (
        P(("job", "actor"), None),
        P(),
        P("actor", "tp"),
        P(None, "tp"),
        P("actor", "tp"),
        P(None, "tp"),
        P("actor", "tp"),
        P(None, "tp"),
        P("tp", "actor"),
        P("tp", None),
        P("tp"),
        P("tp"),
        P("tp"),
        P(("job", "actor"), None, "tp"),
        P(("job", "actor"), None, "tp"),
        P(("job", "actor")),
        P(("job", "actor")),
    )
    return jax.shard_map(
        functools.partial(
            per_device_any, (mesh.shape["job"], mesh.shape["actor"], mesh.shape["tp"])
        ),
        mesh=mesh,
        in_specs=placed,
        out_specs=P(("job", "actor"), None),
        check_vma=False,
    )
```

```python
import functools
import math

import jax
import jax.numpy as jnp
from jax import lax
from jax.experimental import pallas as pl
from jax.experimental.pallas import tpu as pltpu
from jax.sharding import PartitionSpec as P

HEAD_WIDTH = 128
SCALE_BLOCK = 128


epsilon = 1e-06
rope_base = 1000000.0


def apply_rotary(values, length):
    width = values.shape[-1]
    half_width = width // 2
    freqs = rope_base ** (-(jnp.arange(half_width, dtype=jnp.float32) * 2.0 / width))
    angles = length.astype(jnp.float32)[:, None] * freqs[None, :]
    cosine = jnp.cos(angles)[:, None, :]
    sine = jnp.sin(angles)[:, None, :]
    first = values[..., :half_width]
    second = values[..., half_width:]
    return jnp.concatenate(
        [first * cosine - second * sine, second * cosine + first * sine], axis=-1
    )


def attend_single_head(
    query_vector, key_self, value_self, prefix_key_cache, prefix_value_cache, parent, length
):
    scale_factor = 1.0 / math.sqrt(query_vector.shape[-1])
    self_score = (
        jnp.sum(
            query_vector.astype(jnp.float32) * key_self.astype(jnp.float32)[:, None, :], axis=-1
        )
        * scale_factor
    )
    visible = (jnp.arange(prefix_key_cache.shape[1])[None, :] < length[:, None])[:, None, :]
    outcome = jnp.zeros(query_vector.shape, jnp.float32)
    for prefix_index in range(prefix_key_cache.shape[0]):
        scores = (
            jnp.einsum(
                "lge,ce->lgc",
                query_vector,
                prefix_key_cache[prefix_index],
                preferred_element_type=jnp.float32,
            )
            * scale_factor
        )
        highest = jnp.maximum(jnp.max(jnp.where(visible, scores, -jnp.inf), axis=-1), self_score)
        weights = jnp.where(visible, jnp.exp(scores - highest[..., None]), 0.0)
        self_weight = jnp.exp(self_score - highest)
        total = jnp.sum(weights, axis=-1) + self_weight
        self_rounded = lax.optimization_barrier(self_weight.astype(jnp.bfloat16)).astype(
            jnp.float32
        )
        mixed = jnp.einsum(
            "lgc,ce->lge",
            weights.astype(jnp.bfloat16),
            prefix_value_cache[prefix_index],
            preferred_element_type=jnp.float32,
        )
        mixed = mixed + self_rounded[..., None] * value_self.astype(jnp.float32)[:, None, :]
        outcome = jnp.where(
            (parent == prefix_index)[:, None, None], mixed / total[..., None], outcome
        )
    return outcome


PIECE = 5
EARLY = 1


def spread_kernel(
    n_actor,
    rows_each,
    mine_ref,
    row_ref,
    gain_ref,
    sums_ref,
    all_ref,
    raw_ref,
    x_ref,
    home_sem,
    send_sem,
    recv_sem,
    row_sem,
):
    line = n_actor // 2
    actor = lax.axis_index("actor")
    job = lax.axis_index("job")
    at, y = actor // 2, actor % 2
    partner = job + 1 - 2 * (job % 2)
    pair = at * 2 + 1 - y
    has_up, has_down = at + 1 < line, at >= 1
    count = row_ref.shape[0]
    depth = mine_ref.shape[0]
    barrier = pltpu.get_barrier_semaphore()

    @pl.when(has_up)
    def _():
        pl.semaphore_signal(barrier, inc=1, device_id={"actor": actor + 2})

    @pl.when(has_down)
    def _():
        pl.semaphore_signal(barrier, inc=1, device_id={"actor": actor - 2})

    pl.semaphore_signal(barrier, inc=1, device_id={"actor": pair})
    pl.semaphore_signal(barrier, inc=1, device_id={"job": partner})
    pl.semaphore_wait(barrier, 2 + has_up.astype(jnp.int32) + has_down.astype(jnp.int32))

    def send(stream, source, piece, target, own=False):
        cut = pl.ds(piece * rows_each, rows_each)
        return pltpu.make_async_remote_copy(
            src_ref=mine_ref.at[cut] if own else all_ref.at[source, cut],
            dst_ref=all_ref.at[source, cut],
            send_sem=send_sem.at[stream, source, piece],
            recv_sem=recv_sem.at[source, piece],
            device_id={"actor": target},
        )

    def cross(source, piece, own=False):
        return send(0, source, piece, pair, own)

    def up(source, piece, own=False):
        return send(1, source, piece, actor + 2, own)

    def down(source, piece, own=False):
        return send(2, source, piece, actor - 2, own)

    def arrived(source, piece):
        cross(source, piece).wait_recv()

    late = list(range(PIECE - EARLY))
    early = list(range(PIECE - EARLY, PIECE))
    rows_copy = pltpu.make_async_remote_copy(
        src_ref=row_ref,
        dst_ref=raw_ref.at[pl.ds(count, count)],
        send_sem=row_sem.at[0],
        recv_sem=row_sem.at[1],
        device_id={"job": partner},
    )

    def both_ways(source, piece, own=False):
        @pl.when(has_up)
        def _():
            up(source, piece, own).start()

        @pl.when(has_down)
        def _():
            down(source, piece, own).start()

    for piece in early:
        cross(actor, piece, True).start()
    for piece in late:
        both_ways(actor, piece, True)
        cross(actor, piece, True).start()
    for piece in early:
        both_ways(actor, piece, True)
    rows_copy.start()
    home = pltpu.make_async_copy(mine_ref, all_ref.at[actor], home_sem.at[0])
    home.start()
    own_rows = pltpu.make_async_copy(row_ref, raw_ref.at[pl.ds(0, count)], home_sem.at[1])
    own_rows.start()

    def normalize(first):
        def block(i, carry):
            cut = pl.ds(pl.multiple_of(first + i * 16, 16), 16)
            rows = raw_ref[cut, :].astype(jnp.float32)
            rows = rows * lax.rsqrt(jnp.mean(rows * rows, axis=-1, keepdims=True) + epsilon)
            rows = (rows * gain_ref[...].astype(jnp.float32)).astype(jnp.bfloat16)
            for source in range(n_actor):
                x_ref[source, cut, :] = rows[:, source * depth : (source + 1) * depth]
            return carry

        lax.fori_loop(0, count // 16, block, 0)

    def add(source):
        sums_ref[...] += jnp.dot(
            x_ref[source], all_ref[source], preferred_element_type=jnp.float32
        )

    sums_ref[...] = jnp.zeros_like(sums_ref)
    own_rows.wait()
    normalize(0)
    for piece in early:
        arrived(pair, piece)
        both_ways(pair, piece)
    turn = jnp.where(at * 2 < line, 1, line - 1)

    def spot_of(k):
        return lax.rem(at + k * turn, line)

    for far in range(1, line):
        if far == line - 1:
            rows_copy.wait()
            normalize(count)
            home.wait()
            add(actor)
        todo = [(y, p) for p in late] + [(y, p) for p in early] + [(1 - y, p) for p in early]
        for index, (which, piece) in enumerate(todo):
            below = (at - far) * 2 + which
            above = (at + far) * 2 + which

            @pl.when(at >= far)
            def _():
                arrived(below, piece)

                @pl.when(has_up)
                def _():
                    up(below, piece).start()

                if index < len(late):
                    cross(below, piece).start()

            @pl.when(at + far < line)
            def _():
                arrived(above, piece)

                @pl.when(has_down)
                def _():
                    down(above, piece).start()

                if index < len(late):
                    cross(above, piece).start()

    def add_held(k, carry):
        add(spot_of(k) * 2 + y)
        return carry

    lax.fori_loop(1, line, add_held, 0)

    def add_crossed(k, carry):
        source = spot_of(k) * 2 + 1 - y
        for piece in late:
            arrived(source, piece)
        add(source)
        return carry

    lax.fori_loop(0, line, add_crossed, 0)
    for spot in range(line):
        for piece in late:
            cross(spot * 2 + y, piece).wait_send()
    for piece in early:
        cross(actor, piece).wait_send()
    for spot in range(line):
        items = [(y, p) for p in range(PIECE)] + [(1 - y, p) for p in early]
        for which, piece in items:
            source = spot * 2 + which

            @pl.when(jnp.logical_and(has_up, at >= spot))
            def _():
                up(source, piece).wait_send()

            @pl.when(jnp.logical_and(has_down, at <= spot))
            def _():
                down(source, piece).wait_send()


def spread(shard, rows, gain, n_actor):
    height, width = shard.shape
    return pl.pallas_call(
        functools.partial(spread_kernel, n_actor, height // PIECE),
        out_shape=jax.ShapeDtypeStruct((2 * rows.shape[0], width), jnp.float32),
        in_specs=[
            pl.BlockSpec(memory_space=pl.ANY),
            pl.BlockSpec(memory_space=pl.ANY),
            pl.BlockSpec(memory_space=pltpu.VMEM),
        ],
        out_specs=pl.BlockSpec(memory_space=pltpu.VMEM),
        scratch_shapes=[
            pltpu.VMEM((n_actor,) + shard.shape, shard.dtype),
            pltpu.VMEM((2 * rows.shape[0], rows.shape[1]), rows.dtype),
            pltpu.VMEM((n_actor, 2 * rows.shape[0], height), rows.dtype),
            pltpu.SemaphoreType.DMA((2,)),
            pltpu.SemaphoreType.DMA((3, n_actor, PIECE)),
            pltpu.SemaphoreType.DMA((n_actor, PIECE)),
            pltpu.SemaphoreType.DMA((2,)),
        ],
        compiler_params=pltpu.CompilerParams(
            collective_id=0, has_side_effects=True, vmem_limit_bytes=48 * 1024 * 1024
        ),
        cost_estimate=pl.CostEstimate(
            flops=0, bytes_accessed=300_000_000, transcendentals=0
        ),
    )(shard, rows, gain)


def per_device(
    mesh_sizes,
    leaf_states,
    norm_gain,
    wq_quant,
    wq_scale,
    key_weight_quantized,
    key_weight_scale,
    value_weight_quantized,
    value_weight_scale,
    wo_quant,
    wo_scale,
    q_bias,
    key_bias,
    value_bias,
    prefix_key_cache,
    prefix_value_cache,
    parent_prefix_slot,
    prefix_length,
):
    n_job, n_actor = mesh_sizes
    swap = [(i, i ^ 1) for i in range(n_job)]
    side = lax.axis_index("job") % 2
    actor = lax.axis_index("actor")

    def trade(x):
        return lax.ppermute(x, "job", swap)

    leaf_count = leaf_states.shape[0]

    def half_cols(x):
        width = x.shape[1] // 2
        return lax.dynamic_slice_in_dim(x, side * width, width, 1)

    row_count = wq_quant.shape[0]

    def expand_rows(quant, scale):
        mine = lax.dynamic_slice_in_dim(
            scale, actor * (row_count // SCALE_BLOCK), row_count // SCALE_BLOCK, 0
        ) if row_count % SCALE_BLOCK == 0 else None
        if mine is None:
            tall = jnp.repeat(scale, SCALE_BLOCK, axis=0)
            tall = lax.dynamic_slice_in_dim(tall, actor * row_count, row_count, 0)
        else:
            tall = jnp.repeat(mine, SCALE_BLOCK, axis=0)
        wide = jnp.repeat(half_cols(tall), SCALE_BLOCK, axis=1)
        return (half_cols(quant).astype(jnp.float32) * wide).astype(jnp.bfloat16)

    qkv_local = jnp.concatenate(
        [
            expand_rows(wq_quant, wq_scale),
            expand_rows(key_weight_quantized, key_weight_scale),
            expand_rows(value_weight_quantized, value_weight_scale),
        ],
        axis=1,
    )
    col_count = wo_quant.shape[1]
    spread_scale = jnp.repeat(wo_scale, SCALE_BLOCK, axis=1)
    own_scale = half_cols(lax.dynamic_slice_in_dim(spread_scale, actor * col_count, col_count, 1))
    wo_local = (
        half_cols(wo_quant).astype(jnp.float32) * jnp.repeat(own_scale, SCALE_BLOCK, axis=0)
    ).astype(jnp.bfloat16).T
    sums = spread(qkv_local, leaf_states, norm_gain[None, :], n_actor)
    wo_local, sums, prefix_length = lax.optimization_barrier((wo_local, sums, prefix_length))
    both_length = jnp.concatenate([prefix_length, trade(prefix_length)], axis=0)

    def half_row(x):
        width = x.shape[0] // 2
        return lax.dynamic_slice_in_dim(x, side * width, width, 0)

    bias = jnp.concatenate([half_row(q_bias), half_row(key_bias), half_row(value_bias)])
    sums = sums + bias.astype(jnp.float32)
    v_width = value_bias.shape[0] // 2
    rot_width = sums.shape[1] - v_width
    rotated = apply_rotary(
        sums[:, :rot_width].reshape(2 * leaf_count, rot_width // HEAD_WIDTH, HEAD_WIDTH),
        both_length,
    ).reshape(2 * leaf_count, rot_width)
    done = jnp.concatenate([rotated, sums[:, rot_width:]], axis=1).astype(jnp.bfloat16)
    own = done[:leaf_count]
    other = trade(done[leaf_count:])
    q_width = q_bias.shape[0] // 2

    kv_half = v_width // HEAD_WIDTH
    query_group = q_bias.shape[0] // key_bias.shape[0]
    outs = []
    for which, block in ((side, own), (1 - side, other)):
        q = block[:, :q_width].reshape(leaf_count, kv_half, query_group, HEAD_WIDTH)
        k = block[:, q_width : q_width + v_width].reshape(leaf_count, kv_half, HEAD_WIDTH)
        v = block[:, q_width + v_width :].reshape(leaf_count, kv_half, HEAD_WIDTH)
        for head in range(kv_half):
            at = (which * kv_half + head) * HEAD_WIDTH
            outs.append(
                attend_single_head(
                    q[:, head],
                    k[:, head],
                    v[:, head],
                    lax.dynamic_slice_in_dim(prefix_key_cache, at, HEAD_WIDTH, 2),
                    lax.dynamic_slice_in_dim(prefix_value_cache, at, HEAD_WIDTH, 2),
                    parent_prefix_slot,
                    prefix_length,
                )
                .reshape(leaf_count, query_group * HEAD_WIDTH)
                .astype(jnp.bfloat16)
            )
    mine = jnp.concatenate(outs[:kv_half], axis=1)
    theirs = jnp.concatenate(outs[kv_half:], axis=1)
    attended = jnp.where(
        side == 0,
        jnp.concatenate([mine, theirs], axis=1),
        jnp.concatenate([theirs, mine], axis=1),
    )

    wo_all = lax.all_gather(wo_local, "actor", axis=0, tiled=True)
    group = lax.axis_index("tp")
    cores = [(0, 1), (1, 0)]

    def project(rows):
        part = lax.dot_general(
            rows, wo_all, (((1,), (1,)), ((), ())), preferred_element_type=jnp.float32
        )
        width = part.shape[1] // 2
        first, second = part[:, :width], part[:, width:]
        give = jnp.where(group == 0, second, first)
        keep = jnp.where(group == 0, first, second)
        return (keep + lax.ppermute(give, "tp", cores)).astype(jnp.bfloat16), give

    def join(x):
        y = lax.ppermute(x, "tp", cores)
        return jnp.where(
            group == 0,
            jnp.concatenate([x, y], axis=1),
            jnp.concatenate([y, x], axis=1),
        )

    away, marker = project(trade(attended))
    attended, away, _ = lax.optimization_barrier((attended, away, marker))
    away = trade(away)
    local = join(project(attended)[0])
    remote = join(away)
    low = jnp.where(side == 0, local, remote)
    high = jnp.where(side == 0, remote, local)
    pieces = []
    half = col_count // 2
    for a in range(n_actor):
        pieces += [low[:, a * half : (a + 1) * half], high[:, a * half : (a + 1) * half]]
    return jnp.concatenate(pieces, axis=1)


LANES = 128


def fused_kernel(
    n_actor,
    states_ref,
    gain_ref,
    wq_ref,
    wq_scale_ref,
    wk_ref,
    wk_scale_ref,
    wv_ref,
    wv_scale_ref,
    wo_ref,
    wo_scale_ref,
    qb_ref,
    kb_ref,
    vb_ref,
    kcache_ref,
    vcache_ref,
    parent_ref,
    length_ref,
    out_ref,
    raw_ref,
    rawv_ref,
    wown_ref,
    woth_ref,
    give_ref,
    xraw_ref,
    xs_ref,
    lens_ref,
    tabs_ref,
    gains_ref,
    bias_ref,
    acc_ref,
    rst_ref,
    vst_ref,
    rq_ref,
    rv_ref,
    kc_ref,
    vc_ref,
    woraw_ref,
    zset_ref,
    mask_ref,
    att_ref,
    psend_ref,
    precv_ref,
    res_ref,
    load_sem,
    kv_sem,
    z_send,
    z_recv,
    g_send,
    x_send,
    x_recv,
    xs_send,
    xs_recv,
    t_send,
    t_recv,
    q_send,
    q_recv,
    v_send,
    v_recv,
    a_send,
    a_recv,
    oz_send,
    oz_recv,
    p_send,
    p_recv,
    c_send,
    c_recv,
    f_send,
    f_recv,
):
    line = n_actor // 2
    actor = lax.axis_index("actor")
    job = lax.axis_index("job")
    core = lax.axis_index("tp")
    at, y = actor // 2, actor % 2
    side = job % 2
    there = {"job": job + 1 - 2 * side}
    pair = {"actor": at * 2 + 1 - y}
    diagonal = {"job": job + 1 - 2 * side, "actor": at * 2 + 1 - y}
    sibling = {"tp": 1 - core}
    above, below = {"actor": actor + 2}, {"actor": actor - 2}
    has_up, has_down = at + 1 < line, at >= 1
    middle = jnp.logical_and(has_up, has_down)
    ends = jnp.logical_not(middle)
    rows = raw_ref.shape[1]
    count = xraw_ref.shape[0]
    half_rows = rows // 2
    half_count = count // 2
    width = raw_ref.shape[2]
    units = width // LANES
    heads = 2 * units - 1
    depth = zset_ref.shape[1]
    strips = n_actor // 2
    part = strips // 2
    f32, bf16 = jnp.float32, jnp.bfloat16

    def lanes(unit, n=1):
        return pl.ds(pl.multiple_of(unit * LANES, LANES), n * LANES)

    barrier = pltpu.get_barrier_semaphore()

    @pl.when(has_up)
    def _():
        pl.semaphore_signal(barrier, inc=1, device_id=above)

    @pl.when(has_down)
    def _():
        pl.semaphore_signal(barrier, inc=1, device_id=below)

    for peer in (there, pair, diagonal, sibling):
        pl.semaphore_signal(barrier, inc=1, device_id=peer)

    def local(source, target, sem):
        return pltpu.make_async_copy(source, target, sem)

    def remote(source, target, ss, rs, peer):
        return pltpu.make_async_remote_copy(
            src_ref=source, dst_ref=target, send_sem=ss, recv_sem=rs, device_id=peer
        )

    first = 2 * side
    w_loads = [
        local(wq_ref.at[:, lanes(side * heads, units)], raw_ref.at[0], load_sem.at[0]),
        local(
            wq_ref.at[:, lanes(side * heads + units, units - 1)],
            raw_ref.at[1, :, pl.ds(0, (units - 1) * LANES)],
            load_sem.at[1],
        ),
        local(
            wk_ref.at[:, lanes(side)],
            raw_ref.at[1, :, pl.ds((units - 1) * LANES, LANES)],
            load_sem.at[2],
        ),
        local(wv_ref.at[:, lanes(side)], rawv_ref, load_sem.at[3]),
    ]
    state_load = local(states_ref, xraw_ref, load_sem.at[4])
    wo_load = local(
        wo_ref.at[:, lanes(first, 2)], woraw_ref.at[:, pl.ds(0, 2 * LANES)], load_sem.at[5]
    )
    wo_load_last = local(
        wo_ref.at[:, pl.ds(4 * LANES, LANES)], woraw_ref.at[:, pl.ds(2 * LANES, LANES)],
        load_sem.at[6],
    )
    for copy in w_loads:
        copy.start()
    state_load.start()
    wo_load.start()
    wo_load_last.start()
    kv_loads = []
    for j in range(2):
        for p in range(2):
            place = pl.ds(p * LANES, LANES)
            cut = pl.ds(j * LANES, LANES)
            kv_loads.append(
                local(kcache_ref.at[p, :, cut], kc_ref.at[j, :, place], kv_sem.at[0, j, p])
            )
            kv_loads.append(
                local(vcache_ref.at[p, :, cut], vc_ref.at[j, :, place], kv_sem.at[1, j, p])
            )
    for copy in kv_loads:
        copy.start()

    blocks = rows // SCALE_BLOCK

    def pick(ref, row, column):
        values = ref[pl.ds(row, 1), :]
        here = lax.broadcasted_iota(jnp.int32, values.shape, 1) == column
        return jnp.sum(jnp.where(here, values, 0.0), axis=1, keepdims=True)

    def unit_scale(parity, block, u):
        row = actor * blocks + block
        if u < units - 1:
            return pick(wq_scale_ref, side * heads + u + units * parity, row)
        return jnp.where(
            parity == 0,
            pick(wq_scale_ref, side * heads + u, row),
            pick(wk_scale_ref, side, row),
        )

    def expand(parity, target):
        for block in range(blocks):
            cut = pl.ds(block * SCALE_BLOCK, SCALE_BLOCK)
            for u in range(units):
                lane = pl.ds(u * LANES, LANES)
                scaled = raw_ref[parity, cut, lane].astype(f32) * unit_scale(parity, block, u)
                target(cut, lane, scaled.astype(bf16))

    def to_give(cut, lane, value):
        give_ref[cut, lane] = value

    def to_own(cut, lane, value):
        wown_ref[at, cut, lane] = value

    for copy in w_loads:
        copy.wait()
    expand(y, to_own)
    for block in range(blocks):
        cut = pl.ds(block * SCALE_BLOCK, SCALE_BLOCK)
        scale = pick(wv_scale_ref, side, actor * blocks + block)
        wown_ref[at, cut, pl.ds(width, LANES)] = (rawv_ref[cut, :].astype(f32) * scale).astype(
            bf16
        )
    pl.semaphore_wait(barrier, 4 + has_up.astype(jnp.int32) + has_down.astype(jnp.int32))

    def half(p):
        return pl.ds(p * half_rows, half_rows)

    def give(p):
        return remote(
            give_ref.at[half(p)], woth_ref.at[at, half(p)], g_send.at[p], z_recv.at[1, at, p], pair
        )

    def up_down(way, kind, spot, p):
        ref = (wown_ref if kind == 0 else woth_ref).at[spot, half(p)]
        return remote(
            ref, ref, z_send.at[way, kind, spot, p], z_recv.at[kind, spot, p], (above, below)[way]
        )

    def both_ways(kind, spot, p):
        @pl.when(has_up)
        def _():
            up_down(0, kind, spot, p).start()

        @pl.when(has_down)
        def _():
            up_down(1, kind, spot, p).start()

    for p in range(2):
        both_ways(0, at, p)
    expand(1 - y, to_give)
    for p in range(2):
        give(p).start()

    lens_ref[0] = length_ref[...].astype(f32).reshape(1, count)
    table_sends = [
        remote(lens_ref.at[0], lens_ref.at[slot], t_send.at[slot], t_recv.at[slot], peer)
        for slot, peer in ((1, there), (2, pair), (3, diagonal))
    ]
    for copy in table_sends:
        copy.start()

    state_load.wait()

    gains_ref[...] = gain_ref[...].astype(f32).reshape(1, -1)
    for i, ref in enumerate((qb_ref, kb_ref, vb_ref)):
        bias_ref[i, :, : ref.shape[0]] = ref[...].astype(f32).reshape(1, -1)

    def normalize(i, carry):
        cut = pl.ds(pl.multiple_of(i * 16, 16), 16)
        x = xraw_ref[cut, :].astype(f32)
        x = x * lax.rsqrt(jnp.mean(x * x, axis=-1, keepdims=True) + epsilon)
        x = (x * gains_ref[...]).astype(bf16)
        for source in range(n_actor):
            xs_ref[source, cut, :] = x[:, source * rows : (source + 1) * rows]
        return carry

    lax.fori_loop(0, count // 16, normalize, 0)

    def some(p):
        return pl.ds(core * strips + p * part, part)

    def of_slot(slot):
        return pl.ds(slot * count, count)

    def share(slot, p, origin, peer):
        return remote(
            xs_ref.at[some(p), of_slot(origin)],
            xs_ref.at[some(p), of_slot(slot)],
            x_send.at[slot - 1, p],
            x_recv.at[slot - 1, p],
            peer,
        )

    share_list = [
        share(1, 0, 0, there),
        share(2, 1, 0, pair),
        share(1, 1, 0, there),
        share(2, 0, 0, pair),
    ]
    for copy in share_list:
        copy.start()

    def to_sibling(slot, p):
        ref = xs_ref.at[some(p), of_slot(slot)]
        return remote(ref, ref, xs_send.at[slot - 1, p], xs_recv.at[slot - 1, p], sibling)

    def from_sibling(slot, p):
        ref = xs_ref.at[pl.ds((1 - core) * strips + p * part, part), of_slot(slot)]
        return remote(ref, ref, xs_send.at[slot - 1, p], xs_recv.at[slot - 1, p], sibling)

    def column(values):
        wide = jnp.broadcast_to(values, (LANES, count))
        return wide.T

    lane_at = lax.broadcasted_iota(jnp.int32, (count, LANES), 1)
    step = lax.rem(lax.broadcasted_iota(jnp.int32, (1, LANES), 1), LANES // 2).astype(f32)
    freqs = jnp.exp(step * (-2.0 * math.log(rope_base) / LANES))
    def make_table(slot):
        angles = column(lens_ref[slot]) * freqs
        tabs_ref[slot] = jnp.where(lane_at < LANES // 2, jnp.cos(angles), jnp.sin(angles))


    wo_load.wait()
    wo_load_last.wait()
    wo_blocks = depth // SCALE_BLOCK
    wo_units = wo_ref.shape[1] // LANES

    def expand_wo(block, carry):
        cut = pl.ds(pl.multiple_of(block * SCALE_BLOCK, SCALE_BLOCK), SCALE_BLOCK)
        for u in range(2):
            lane = pl.ds(u * LANES, LANES)
            scale = pick(wo_scale_ref, block, actor * wo_units + first + u)
            zset_ref[at, cut, lane] = (woraw_ref[cut, lane].astype(f32) * scale).astype(bf16)
        return carry

    lax.fori_loop(0, wo_blocks, expand_wo, 0)

    def has_extra(spot, s):
        return spot % 2 == s

    @pl.when(has_extra(at, side))
    def _():
        def expand_last(block, carry):
            cut = pl.ds(pl.multiple_of(block * SCALE_BLOCK, SCALE_BLOCK), SCALE_BLOCK)
            lane = pl.ds(2 * LANES, LANES)
            scale = pick(wo_scale_ref, block, actor * wo_units + 4)
            zset_ref[at, cut, lane] = (woraw_ref[cut, lane].astype(f32) * scale).astype(bf16)
            return carry

        lax.fori_loop(0, wo_blocks, expand_last, 0)

    def wo_way(way, spot, q):
        ref = zset_ref.at[spot, :, pl.ds(q * LANES, LANES)]
        return remote(
            ref, ref, oz_send.at[way, spot, q], oz_recv.at[spot, q], (above, below)[way]
        )

    def each_piece(spot, action):
        for q in range(2):
            action(q)

        @pl.when(has_extra(spot, side))
        def _():
            action(2)

    def wo_begin(far):
        @pl.when(jnp.logical_and(at == far, has_up))
        def _():
            each_piece(at, lambda q: wo_way(0, at, q).start())

        @pl.when(jnp.logical_and(line - 1 - at == far, has_down))
        def _():
            each_piece(at, lambda q: wo_way(1, at, q).start())

    def relay_one(way, spot):
        def action(q):
            wo_way(way, spot, q).wait_recv()

            @pl.when((has_up, has_down)[way])
            def _():
                wo_way(way, spot, q).start()

        each_piece(spot, action)

    def relay(far):
        @pl.when(at >= far)
        def _():
            relay_one(0, at - far)

        @pl.when(at + far < line)
        def _():
            relay_one(1, at + far)

    for p in range(2):
        give(p).wait_recv()
        both_ways(1, at, p)
    wo_begin(0)

    acc_ref[...] = jnp.zeros_like(acc_ref)
    make_table(0)
    for slot in (1, 2, 3):
        table_sends[slot - 1].wait_recv()
        make_table(slot)
    length = column(lens_ref[0])[:, :1].astype(jnp.int32)
    mask_ref[...] = jnp.where(
        lax.broadcasted_iota(jnp.int32, mask_ref.shape, 1) < length, 0.0, -jnp.inf
    )

    def multiply_kind(kind, spot):
        if kind == 0:
            acc_ref[...] += jnp.dot(
                xs_ref[spot * 2 + y], wown_ref[spot], preferred_element_type=f32
            )
        else:
            acc_ref[:, :width] += jnp.dot(
                xs_ref[spot * 2 + 1 - y], woth_ref[spot], preferred_element_type=f32
            )

    def multiply(spot):
        multiply_kind(0, spot)
        multiply_kind(1, spot)

    def multiply_far(far, carry):
        @pl.when(at >= far)
        def _():
            multiply(at - far)

        @pl.when(jnp.logical_and(at + far < line, far > 0))
        def _():
            multiply(at + far)

        return carry

    def rows_first():
        for slot, p, peer in ((1, 0, pair), (2, 1, there), (1, 1, None), (2, 0, None)):
            share(slot, p, 0, there if slot == 1 else pair).wait_recv()
            if peer is not None:
                share(3, p, slot, peer).start()
            to_sibling(slot, p).start()

    def rows_rest():
        for p in range(2):
            share(3, p, 1 + p, pair if p == 0 else there).wait_recv()
            to_sibling(3, p).start()

        for slot in (1, 2, 3):
            for p in range(2):
                from_sibling(slot, p).wait_recv()

    for far in range(1, line):
        for kind in range(2):
            for p in range(2):

                @pl.when(at >= far)
                def _():
                    up_down(0, kind, at - far, p).wait_recv()

                    @pl.when(has_up)
                    def _():
                        up_down(0, kind, at - far, p).start()

                @pl.when(at + far < line)
                def _():
                    up_down(1, kind, at + far, p).wait_recv()

                    @pl.when(has_down)
                    def _():
                        up_down(1, kind, at + far, p).start()

            if far == line - 1:

                @pl.when(at >= far)
                def _():
                    multiply_kind(kind, at - far)

                @pl.when(at + far < line)
                def _():
                    multiply_kind(kind, at + far)

        wo_begin(far)
        if far == 1:
            rows_first()
        if far == max(line - 2, 1):
            rows_rest()
            lax.fori_loop(0, max(line - 1, 1), multiply_far, 0)

    def results(slot):
        return (
            remote(rst_ref.at[slot], rq_ref.at[slot], q_send.at[slot], q_recv.at[slot], peers[slot]),
            remote(vst_ref.at[slot], rv_ref.at[slot], v_send.at[slot], v_recv.at[slot], peers[slot]),
        )

    peers = {1: there, 2: pair, 3: diagonal}
    for slot in (2, 1, 3, 0):
        table = tabs_ref[slot]
        swapped = pltpu.roll(table, LANES // 2, 1)
        cosine = jnp.where(lane_at < LANES // 2, table, swapped)
        sine = jnp.where(lane_at < LANES // 2, -swapped, table)
        for u in range(units):
            if u < units - 1:
                bias = bias_ref[0, :, lanes(side * heads + u + units * y)]
            else:
                bias = jnp.where(
                    y == 0,
                    bias_ref[0, :, lanes(side * heads + u)],
                    bias_ref[1, :, lanes(side)],
                )
            value = acc_ref[of_slot(slot), u * LANES : (u + 1) * LANES] + bias
            value = value * cosine + pltpu.roll(value, LANES // 2, 1) * sine
            (rst_ref if slot else rq_ref)[slot, u] = value.astype(bf16)
        (vst_ref if slot else rv_ref)[slot] = acc_ref[of_slot(slot), width:]
        if slot:
            for copy in results(slot):
                copy.start()

    @pl.when(middle)
    def _():
        relay(1)

    for copy in kv_loads:
        copy.wait()
    parent = column(parent_ref[...].astype(f32).reshape(1, count))[:, :1]
    in_first = (parent == 0).astype(f32)
    in_second = 1.0 - in_first
    scale_factor = math.log2(math.e) / math.sqrt(LANES)

    def hand(slot, j, origin, peer):
        cut = lanes(j * heads, heads)

        def of(k):
            return att_ref.at[:, pl.ds(k * half_count, half_count), cut]

        return remote(
            of(origin),
            of(slot),
            a_send.at[slot - 1, origin - 1 if slot == 3 else j],
            a_recv.at[slot - 1, j],
            peer,
        )

    chunks = 4
    context = kc_ref.shape[1] // chunks

    def attend(base):
        group = side if base == 0 else 1 - side
        low = jnp.where(y == 0, base, base + 2)
        high = jnp.where(y == 0, base + 2, base)
        key_new = rq_ref[high, units - 1].astype(f32)
        value_new = rv_ref[base] + rv_ref[base + 2] + bias_ref[2, :, lanes(group)]
        value_new = value_new.astype(bf16).astype(f32)

        def head(h, carry):
            query = rq_ref[
                jnp.where(h < units, low, high), jnp.where(h < units, h, h - units)
            ].astype(f32)
            own = jnp.sum(query * key_new, axis=-1, keepdims=True) * scale_factor
            both = jnp.concatenate([query * in_first, query * in_second], axis=1).astype(bf16)
            highest = own
            pieces = []
            for c in range(chunks):
                scores = lax.dot_general(
                    both,
                    kc_ref[group, c * context : (c + 1) * context],
                    (((1,), (1,)), ((), ())),
                    preferred_element_type=f32,
                )
                scores = scores * scale_factor + mask_ref[:, c * context : (c + 1) * context]
                highest = jnp.maximum(highest, jnp.max(scores, axis=-1, keepdims=True))
                pieces.append(scores)
            own = jnp.exp2(own - highest)
            total, mixed = own, None
            for c, scores in enumerate(pieces):
                weights = jnp.exp2(scores - highest)
                total = total + jnp.sum(weights, axis=-1, keepdims=True)
                more = jnp.dot(
                    weights.astype(bf16),
                    vc_ref[group, c * context : (c + 1) * context],
                    preferred_element_type=f32,
                )
                mixed = more if mixed is None else mixed + more
            mixed = jnp.where(parent == 0, mixed[:, :LANES], mixed[:, LANES:])
            mixed = mixed + own.astype(bf16).astype(f32) * value_new
            mixed = (mixed / total).astype(bf16)
            for which in range(2):
                att_ref[which, :half_count, lanes(group * heads + h)] = mixed[
                    which * half_count : (which + 1) * half_count
                ]
            return carry

        lax.fori_loop(0, heads, head, 0)
        hand(1, group, 0, there).start()
        hand(2, group, 0, pair).start()

    for copy in results(2):
        copy.wait_recv()
    attend(0)

    for slot in (1, 3):
        for copy in results(slot):
            copy.wait_recv()
    attend(1)
    hand(2, side, 0, pair).wait_recv()
    hand(3, side, 2, there).start()
    hand(1, side, 0, there).wait_recv()
    hand(3, side, 1, pair).start()

    @pl.when(middle)
    def _():
        relay(2)

    hand(1, 1 - side, 0, there).wait_recv()
    hand(2, 1 - side, 0, pair).wait_recv()

    bounds = tuple(pl.ds(k * LANES, LANES) for k in range(3))

    groups = ((0, 3), (3, 1))

    def rows_of(g):
        return pl.ds(groups[g][0] * half_count, groups[g][1] * half_count)

    def p_copy(spot, k, g):
        return remote(
            psend_ref.at[spot, rows_of(g), bounds[k]],
            precv_ref.at[spot, rows_of(g), bounds[k]],
            p_send.at[spot, k, g],
            p_recv.at[spot, k, g],
            sibling,
        )

    def unit_of(spot, s, parity, k):
        return wo_units * (2 * spot + parity) + (4 if k == 2 else 2 * s + k)

    def target(spot, s, parity, k):
        mine = pl.ds(pl.multiple_of(core * half_count, half_count), half_count)
        return out_ref.at[mine, lanes(unit_of(spot, s, parity, k))]

    def result(spot, slot, k):
        return res_ref.at[spot, pl.ds(slot * half_count, half_count), bounds[k]]

    def sibling_copy(spot, k):
        return remote(
            target(spot, side, y, k),
            target(spot, side, y, k),
            f_send.at[0, spot, k],
            f_recv.at[0, spot, k],
            sibling,
        )

    def send_copy(spot, slot, k):
        return remote(
            result(spot, slot, k),
            target(spot, side, y, k),
            c_send.at[slot - 1, spot, k],
            c_recv.at[slot - 1, spot, k],
            peers[slot],
        )

    source_side = (side, 1 - side, side, 1 - side)
    source_parity = (y, y, 1 - y, 1 - y)

    def onward_copy(spot, slot, k):
        ref = target(spot, source_side[slot], source_parity[slot], k)
        return remote(ref, ref, f_send.at[slot, spot, k], f_recv.at[slot, spot, k], sibling)

    def across(ks):
        return pl.ds(ks[0] * LANES, len(ks) * LANES)

    def send_part(spot, ks, g):
        psend_ref[spot, rows_of(g), across(ks)] = jnp.dot(
            att_ref[1 - core, rows_of(g)], zset_ref[spot, :, across(ks)], preferred_element_type=f32
        )
        for k in ks:
            p_copy(spot, k, g).start()

    def keep_part(spot, ks, g):
        kept = jnp.dot(
            att_ref[core, rows_of(g)], zset_ref[spot, :, across(ks)], preferred_element_type=f32
        )
        for k in ks:
            p_copy(spot, k, g).wait_recv()
        kept = (kept + precv_ref[spot, rows_of(g), across(ks)]).astype(bf16)
        res_ref[spot, rows_of(g), across(ks)] = kept
        if g == 1:
            for k in ks:
                send_copy(spot, 3, k).start()
            return
        for slot in (1, 2):
            for k in ks:
                send_copy(spot, slot, k).start()
        mine = pl.ds(pl.multiple_of(core * half_count, half_count), half_count)
        for i, k in enumerate(ks):
            out_ref[mine, lanes(unit_of(spot, side, y, k))] = kept[
                :half_count, i * LANES : (i + 1) * LANES
            ]
            sibling_copy(spot, k).start()

    def wide_part(spot, action):
        action((0, 1))

        @pl.when(has_extra(spot, side))
        def _():
            action((2,))

    def each_part(spot, s, action):
        action(0)
        action(1)

        @pl.when(has_extra(spot, s))
        def _():
            action(2)

    def project_send(spot, g):
        wide_part(spot, lambda ks: send_part(spot, ks, g))

    def project_keep(spot, g):
        wide_part(spot, lambda ks: keep_part(spot, ks, g))

    def onward(spot):
        for slot in (1, 2, 3):

            def action(k):
                send_copy(spot, slot, k).wait_recv()
                onward_copy(spot, slot, k).start()

            each_part(spot, source_side[slot], action)

    def at_far(action, far):
        @pl.when(at >= far)
        def _():
            action(at - far)

        @pl.when(jnp.logical_and(at + far < line, far > 0))
        def _():
            action(at + far)

    def relays(far, carry):
        @pl.when(jnp.logical_and(far > 0, jnp.logical_or(ends, far > 2)))
        def _():
            relay(far)

        return carry

    def sends(g):
        def body(far, carry):
            if g == 0:
                relays(far, 0)
            at_far(lambda spot: project_send(spot, g), far)
            return carry

        return body

    def keeps(g):
        def body(far, carry):
            at_far(lambda spot: project_keep(spot, g), far)
            return carry

        return body

    def onwards(far, carry):
        at_far(onward, far)
        return carry

    lax.fori_loop(0, line - 1, sends(0), 0)
    lax.fori_loop(0, line - 1, keeps(0), 0)
    for j in range(2):
        hand(3, j, 1, pair).wait_recv()
    lax.fori_loop(0, line - 1, sends(1), 0)
    lax.fori_loop(0, line - 1, keeps(1), 0)

    @pl.when(ends)
    def _():
        def last(way, spot):
            def action(q):
                wo_way(way, spot, q).wait_recv()
                for g in (0, 1):
                    send_part(spot, (q,), g)
                for g in (1, 0):
                    keep_part(spot, (q,), g)

            each_piece(spot, action)

        @pl.when(at >= line - 1)
        def _():
            last(0, at - (line - 1))

        @pl.when(at + line - 1 < line)
        def _():
            last(1, at + line - 1)

    lax.fori_loop(0, line, onwards, 0)

    for p in range(2):
        give(p).wait_send()
        for slot, peer in ((1, there), (2, pair), (3, pair)):
            share(slot, p, 0, peer).wait_send()
            to_sibling(slot, p).wait_send()
    for copy in table_sends:
        copy.wait_send()
    for slot in (1, 2, 3):
        for copy in results(slot):
            copy.wait_send()
    for j in range(2):
        for slot in (1, 2, 3):
            hand(slot, j, j + 1 if slot == 3 else 0, there).wait_send()

    def finish(spot, carry):
        @pl.when(jnp.logical_and(has_up, at >= spot))
        def _():
            for kind in range(2):
                for p in range(2):
                    up_down(0, kind, spot, p).wait_send()
            each_piece(spot, lambda q: wo_way(0, spot, q).wait_send())

        @pl.when(jnp.logical_and(has_down, at <= spot))
        def _():
            for kind in range(2):
                for p in range(2):
                    up_down(1, kind, spot, p).wait_send()
            each_piece(spot, lambda q: wo_way(1, spot, q).wait_send())

        def end_part(k):
            for g in range(2):
                p_copy(spot, k, g).wait_send()
            sibling_copy(spot, k).wait()
            for slot in (1, 2, 3):
                send_copy(spot, slot, k).wait_send()

        each_part(spot, side, end_part)
        for slot in (1, 2, 3):
            each_part(
                spot, source_side[slot], lambda k: onward_copy(spot, slot, k).wait()
            )
        return carry

    lax.fori_loop(0, line, finish, 0)


def fused(n_actor, args):
    (
        leaf_states, norm_gain, wq_quant, wq_scale, wk, wk_scale, wv, wv_scale, wo_quant, wo_scale,
        q_bias, key_bias, value_bias, kcache, vcache, parent, length,
    ) = args
    count, features = leaf_states.shape
    rows = wq_quant.shape[0]
    heads = wq_quant.shape[1] // (2 * LANES)
    units = (heads + 1) // 2
    width = units * LANES
    context = kcache.shape[1]
    depth = wo_quant.shape[0]
    line = n_actor // 2
    total_units = n_actor * (wo_quant.shape[1] // LANES)
    bf16, f32 = jnp.bfloat16, jnp.float32
    any_space = pl.BlockSpec(memory_space=pl.ANY)
    vmem = pl.BlockSpec(memory_space=pltpu.VMEM)
    dma = pltpu.SemaphoreType.DMA
    return pl.pallas_call(
        functools.partial(fused_kernel, n_actor),
        out_shape=jax.ShapeDtypeStruct((count, total_units * LANES), bf16),
        in_specs=[
            any_space, vmem, any_space, vmem, any_space, vmem, any_space, vmem, any_space, vmem,
            vmem, vmem, vmem, any_space, any_space, vmem, vmem,
        ],
        out_specs=vmem,
        scratch_shapes=[
            pltpu.VMEM((2, rows, width), bf16),
            pltpu.VMEM((rows, LANES), bf16),
            pltpu.VMEM((line, rows, width + LANES), bf16),
            pltpu.VMEM((line, rows, width), bf16),
            pltpu.VMEM((rows, width), bf16),
            pltpu.VMEM((count, features), bf16),
            pltpu.VMEM((n_actor, 4 * count, rows), bf16),
            pltpu.VMEM((4, 1, count), f32),
            pltpu.VMEM((4, count, LANES), f32),
            pltpu.VMEM((1, features), f32),
            pltpu.VMEM((3, 1, 2 * heads * LANES), f32),
            pltpu.VMEM((4 * count, width + LANES), f32),
            pltpu.VMEM((4, units, count, LANES), bf16),
            pltpu.VMEM((4, count, LANES), f32),
            pltpu.VMEM((4, units, count, LANES), bf16),
            pltpu.VMEM((4, count, LANES), f32),
            pltpu.VMEM((2, context, 2 * LANES), bf16),
            pltpu.VMEM((2, context, 2 * LANES), bf16),
            pltpu.VMEM((depth, 3 * LANES), bf16),
            pltpu.VMEM((line, depth, 3 * LANES), bf16),
            pltpu.VMEM((count, context), f32),
            pltpu.VMEM((2, 2 * count, 2 * heads * LANES), bf16),
            pltpu.VMEM((line, 2 * count, 3 * LANES), f32),
            pltpu.VMEM((line, 2 * count, 3 * LANES), f32),
            pltpu.VMEM((line, 2 * count, 3 * LANES), bf16),
            dma((7,)),
            dma((2, 2, 2)),
            dma((2, 2, line, 2)),
            dma((2, line, 2)),
            dma((2,)),
            dma((3, 2)),
            dma((3, 2)),
            dma((3, 2)),
            dma((3, 2)),
            dma((4,)),
            dma((4,)),
            dma((4,)),
            dma((4,)),
            dma((4,)),
            dma((4,)),
            dma((3, 2)),
            dma((3, 2)),
            dma((2, line, 3)),
            dma((line, 3)),
            dma((line, 3, 2)),
            dma((line, 3, 2)),
            dma((3, line, 3)),
            dma((3, line, 3)),
            dma((4, line, 3)),
            dma((4, line, 3)),
        ],
        compiler_params=pltpu.CompilerParams(
            collective_id=0, has_side_effects=True, vmem_limit_bytes=58 * 1024 * 1024
        ),
        cost_estimate=pl.CostEstimate(
            flops=13_000_000_000, bytes_accessed=30_000_000, transcendentals=6_000_000
        ),
    )(
        leaf_states, norm_gain, wq_quant, wq_scale.T, wk, wk_scale.T, wv, wv_scale.T, wo_quant,
        wo_scale, q_bias, key_bias, value_bias, kcache, vcache, parent, length,
    )


def per_device_fused(n_actor, *args):
    return fused(n_actor, args)


def fits_fused(mesh_sizes, args):
    n_job, n_actor, n_tp = mesh_sizes
    return (
        n_tp == 2
        and n_job % 2 == 0
        and n_actor % 8 == 0
        and args[0].shape[0] % 32 == 0
        and args[2].shape[0] % SCALE_BLOCK == 0
        and (args[2].shape[1] // LANES) % 4 == 2
        and args[4].shape[1] == 2 * LANES
        and args[8].shape[1] == 5 * LANES
        and args[13].shape[0] == 2
    )


def per_device_any(mesh_sizes, *args):
    if fits_fused(mesh_sizes, args):
        return per_device_fused(mesh_sizes[1], *args)
    return per_device(mesh_sizes[:2], *args)


def solution(mesh):
    placed = (
        P(("job", "actor"), None),
        P(),
        P("actor", "tp"),
        P(None, "tp"),
        P("actor", "tp"),
        P(None, "tp"),
        P("actor", "tp"),
        P(None, "tp"),
        P("tp", "actor"),
        P("tp", None),
        P("tp"),
        P("tp"),
        P("tp"),
        P(("job", "actor"), None, "tp"),
        P(("job", "actor"), None, "tp"),
        P(("job", "actor")),
        P(("job", "actor")),
    )
    return jax.shard_map(
        functools.partial(
            per_device_any, (mesh.shape["job"], mesh.shape["actor"], mesh.shape["tp"])
        ),
        mesh=mesh,
        in_specs=placed,
        out_specs=P(("job", "actor"), None),
        check_vma=False,
    )
```

```python
import functools
import math

import jax
import jax.numpy as jnp
from jax import lax
from jax.experimental import pallas as pl
from jax.experimental.pallas import tpu as pltpu
from jax.sharding import PartitionSpec as P

HEAD_WIDTH = 128
SCALE_BLOCK = 128


epsilon = 1e-06
rope_base = 1000000.0


def apply_rotary(values, length):
    width = values.shape[-1]
    half_width = width // 2
    freqs = rope_base ** (-(jnp.arange(half_width, dtype=jnp.float32) * 2.0 / width))
    angles = length.astype(jnp.float32)[:, None] * freqs[None, :]
    cosine = jnp.cos(angles)[:, None, :]
    sine = jnp.sin(angles)[:, None, :]
    first = values[..., :half_width]
    second = values[..., half_width:]
    return jnp.concatenate(
        [first * cosine - second * sine, second * cosine + first * sine], axis=-1
    )


def attend_single_head(
    query_vector, key_self, value_self, prefix_key_cache, prefix_value_cache, parent, length
):
    scale_factor = 1.0 / math.sqrt(query_vector.shape[-1])
    self_score = (
        jnp.sum(
            query_vector.astype(jnp.float32) * key_self.astype(jnp.float32)[:, None, :], axis=-1
        )
        * scale_factor
    )
    visible = (jnp.arange(prefix_key_cache.shape[1])[None, :] < length[:, None])[:, None, :]
    outcome = jnp.zeros(query_vector.shape, jnp.float32)
    for prefix_index in range(prefix_key_cache.shape[0]):
        scores = (
            jnp.einsum(
                "lge,ce->lgc",
                query_vector,
                prefix_key_cache[prefix_index],
                preferred_element_type=jnp.float32,
            )
            * scale_factor
        )
        highest = jnp.maximum(jnp.max(jnp.where(visible, scores, -jnp.inf), axis=-1), self_score)
        weights = jnp.where(visible, jnp.exp(scores - highest[..., None]), 0.0)
        self_weight = jnp.exp(self_score - highest)
        total = jnp.sum(weights, axis=-1) + self_weight
        self_rounded = lax.optimization_barrier(self_weight.astype(jnp.bfloat16)).astype(
            jnp.float32
        )
        mixed = jnp.einsum(
            "lgc,ce->lge",
            weights.astype(jnp.bfloat16),
            prefix_value_cache[prefix_index],
            preferred_element_type=jnp.float32,
        )
        mixed = mixed + self_rounded[..., None] * value_self.astype(jnp.float32)[:, None, :]
        outcome = jnp.where(
            (parent == prefix_index)[:, None, None], mixed / total[..., None], outcome
        )
    return outcome


PIECE = 5
EARLY = 1


def spread_kernel(
    n_actor,
    rows_each,
    mine_ref,
    row_ref,
    gain_ref,
    sums_ref,
    all_ref,
    raw_ref,
    x_ref,
    home_sem,
    send_sem,
    recv_sem,
    row_sem,
):
    line = n_actor // 2
    actor = lax.axis_index("actor")
    job = lax.axis_index("job")
    at, y = actor // 2, actor % 2
    partner = job + 1 - 2 * (job % 2)
    pair = at * 2 + 1 - y
    has_up, has_down = at + 1 < line, at >= 1
    count = row_ref.shape[0]
    depth = mine_ref.shape[0]
    barrier = pltpu.get_barrier_semaphore()

    @pl.when(has_up)
    def _():
        pl.semaphore_signal(barrier, inc=1, device_id={"actor": actor + 2})

    @pl.when(has_down)
    def _():
        pl.semaphore_signal(barrier, inc=1, device_id={"actor": actor - 2})

    pl.semaphore_signal(barrier, inc=1, device_id={"actor": pair})
    pl.semaphore_signal(barrier, inc=1, device_id={"job": partner})
    pl.semaphore_wait(barrier, 2 + has_up.astype(jnp.int32) + has_down.astype(jnp.int32))

    def send(stream, source, piece, target, own=False):
        cut = pl.ds(piece * rows_each, rows_each)
        return pltpu.make_async_remote_copy(
            src_ref=mine_ref.at[cut] if own else all_ref.at[source, cut],
            dst_ref=all_ref.at[source, cut],
            send_sem=send_sem.at[stream, source, piece],
            recv_sem=recv_sem.at[source, piece],
            device_id={"actor": target},
        )

    def cross(source, piece, own=False):
        return send(0, source, piece, pair, own)

    def up(source, piece, own=False):
        return send(1, source, piece, actor + 2, own)

    def down(source, piece, own=False):
        return send(2, source, piece, actor - 2, own)

    def arrived(source, piece):
        cross(source, piece).wait_recv()

    late = list(range(PIECE - EARLY))
    early = list(range(PIECE - EARLY, PIECE))
    rows_copy = pltpu.make_async_remote_copy(
        src_ref=row_ref,
        dst_ref=raw_ref.at[pl.ds(count, count)],
        send_sem=row_sem.at[0],
        recv_sem=row_sem.at[1],
        device_id={"job": partner},
    )

    def both_ways(source, piece, own=False):
        @pl.when(has_up)
        def _():
            up(source, piece, own).start()

        @pl.when(has_down)
        def _():
            down(source, piece, own).start()

    for piece in early:
        cross(actor, piece, True).start()
    for piece in late:
        both_ways(actor, piece, True)
        cross(actor, piece, True).start()
    for piece in early:
        both_ways(actor, piece, True)
    rows_copy.start()
    home = pltpu.make_async_copy(mine_ref, all_ref.at[actor], home_sem.at[0])
    home.start()
    own_rows = pltpu.make_async_copy(row_ref, raw_ref.at[pl.ds(0, count)], home_sem.at[1])
    own_rows.start()

    def normalize(first):
        def block(i, carry):
            cut = pl.ds(pl.multiple_of(first + i * 16, 16), 16)
            rows = raw_ref[cut, :].astype(jnp.float32)
            rows = rows * lax.rsqrt(jnp.mean(rows * rows, axis=-1, keepdims=True) + epsilon)
            rows = (rows * gain_ref[...].astype(jnp.float32)).astype(jnp.bfloat16)
            for source in range(n_actor):
                x_ref[source, cut, :] = rows[:, source * depth : (source + 1) * depth]
            return carry

        lax.fori_loop(0, count // 16, block, 0)

    def add(source):
        sums_ref[...] += jnp.dot(
            x_ref[source], all_ref[source], preferred_element_type=jnp.float32
        )

    sums_ref[...] = jnp.zeros_like(sums_ref)
    own_rows.wait()
    normalize(0)
    for piece in early:
        arrived(pair, piece)
        both_ways(pair, piece)
    turn = jnp.where(at * 2 < line, 1, line - 1)

    def spot_of(k):
        return lax.rem(at + k * turn, line)

    for far in range(1, line):
        if far == line - 1:
            rows_copy.wait()
            normalize(count)
            home.wait()
            add(actor)
        todo = [(y, p) for p in late] + [(y, p) for p in early] + [(1 - y, p) for p in early]
        for index, (which, piece) in enumerate(todo):
            below = (at - far) * 2 + which
            above = (at + far) * 2 + which

            @pl.when(at >= far)
            def _():
                arrived(below, piece)

                @pl.when(has_up)
                def _():
                    up(below, piece).start()

                if index < len(late):
                    cross(below, piece).start()

            @pl.when(at + far < line)
            def _():
                arrived(above, piece)

                @pl.when(has_down)
                def _():
                    down(above, piece).start()

                if index < len(late):
                    cross(above, piece).start()

    def add_held(k, carry):
        add(spot_of(k) * 2 + y)
        return carry

    lax.fori_loop(1, line, add_held, 0)

    def add_crossed(k, carry):
        source = spot_of(k) * 2 + 1 - y
        for piece in late:
            arrived(source, piece)
        add(source)
        return carry

    lax.fori_loop(0, line, add_crossed, 0)
    for spot in range(line):
        for piece in late:
            cross(spot * 2 + y, piece).wait_send()
    for piece in early:
        cross(actor, piece).wait_send()
    for spot in range(line):
        items = [(y, p) for p in range(PIECE)] + [(1 - y, p) for p in early]
        for which, piece in items:
            source = spot * 2 + which

            @pl.when(jnp.logical_and(has_up, at >= spot))
            def _():
                up(source, piece).wait_send()

            @pl.when(jnp.logical_and(has_down, at <= spot))
            def _():
                down(source, piece).wait_send()


def spread(shard, rows, gain, n_actor):
    height, width = shard.shape
    return pl.pallas_call(
        functools.partial(spread_kernel, n_actor, height // PIECE),
        out_shape=jax.ShapeDtypeStruct((2 * rows.shape[0], width), jnp.float32),
        in_specs=[
            pl.BlockSpec(memory_space=pl.ANY),
            pl.BlockSpec(memory_space=pl.ANY),
            pl.BlockSpec(memory_space=pltpu.VMEM),
        ],
        out_specs=pl.BlockSpec(memory_space=pltpu.VMEM),
        scratch_shapes=[
            pltpu.VMEM((n_actor,) + shard.shape, shard.dtype),
            pltpu.VMEM((2 * rows.shape[0], rows.shape[1]), rows.dtype),
            pltpu.VMEM((n_actor, 2 * rows.shape[0], height), rows.dtype),
            pltpu.SemaphoreType.DMA((2,)),
            pltpu.SemaphoreType.DMA((3, n_actor, PIECE)),
            pltpu.SemaphoreType.DMA((n_actor, PIECE)),
            pltpu.SemaphoreType.DMA((2,)),
        ],
        compiler_params=pltpu.CompilerParams(
            collective_id=0, has_side_effects=True, vmem_limit_bytes=48 * 1024 * 1024
        ),
        cost_estimate=pl.CostEstimate(
            flops=0, bytes_accessed=300_000_000, transcendentals=0
        ),
    )(shard, rows, gain)


def per_device(
    mesh_sizes,
    leaf_states,
    norm_gain,
    wq_quant,
    wq_scale,
    key_weight_quantized,
    key_weight_scale,
    value_weight_quantized,
    value_weight_scale,
    wo_quant,
    wo_scale,
    q_bias,
    key_bias,
    value_bias,
    prefix_key_cache,
    prefix_value_cache,
    parent_prefix_slot,
    prefix_length,
):
    n_job, n_actor = mesh_sizes
    swap = [(i, i ^ 1) for i in range(n_job)]
    side = lax.axis_index("job") % 2
    actor = lax.axis_index("actor")

    def trade(x):
        return lax.ppermute(x, "job", swap)

    leaf_count = leaf_states.shape[0]

    def half_cols(x):
        width = x.shape[1] // 2
        return lax.dynamic_slice_in_dim(x, side * width, width, 1)

    row_count = wq_quant.shape[0]

    def expand_rows(quant, scale):
        mine = lax.dynamic_slice_in_dim(
            scale, actor * (row_count // SCALE_BLOCK), row_count // SCALE_BLOCK, 0
        ) if row_count % SCALE_BLOCK == 0 else None
        if mine is None:
            tall = jnp.repeat(scale, SCALE_BLOCK, axis=0)
            tall = lax.dynamic_slice_in_dim(tall, actor * row_count, row_count, 0)
        else:
            tall = jnp.repeat(mine, SCALE_BLOCK, axis=0)
        wide = jnp.repeat(half_cols(tall), SCALE_BLOCK, axis=1)
        return (half_cols(quant).astype(jnp.float32) * wide).astype(jnp.bfloat16)

    qkv_local = jnp.concatenate(
        [
            expand_rows(wq_quant, wq_scale),
            expand_rows(key_weight_quantized, key_weight_scale),
            expand_rows(value_weight_quantized, value_weight_scale),
        ],
        axis=1,
    )
    col_count = wo_quant.shape[1]
    spread_scale = jnp.repeat(wo_scale, SCALE_BLOCK, axis=1)
    own_scale = half_cols(lax.dynamic_slice_in_dim(spread_scale, actor * col_count, col_count, 1))
    wo_local = (
        half_cols(wo_quant).astype(jnp.float32) * jnp.repeat(own_scale, SCALE_BLOCK, axis=0)
    ).astype(jnp.bfloat16).T
    sums = spread(qkv_local, leaf_states, norm_gain[None, :], n_actor)
    wo_local, sums, prefix_length = lax.optimization_barrier((wo_local, sums, prefix_length))
    both_length = jnp.concatenate([prefix_length, trade(prefix_length)], axis=0)

    def half_row(x):
        width = x.shape[0] // 2
        return lax.dynamic_slice_in_dim(x, side * width, width, 0)

    bias = jnp.concatenate([half_row(q_bias), half_row(key_bias), half_row(value_bias)])
    sums = sums + bias.astype(jnp.float32)
    v_width = value_bias.shape[0] // 2
    rot_width = sums.shape[1] - v_width
    rotated = apply_rotary(
        sums[:, :rot_width].reshape(2 * leaf_count, rot_width // HEAD_WIDTH, HEAD_WIDTH),
        both_length,
    ).reshape(2 * leaf_count, rot_width)
    done = jnp.concatenate([rotated, sums[:, rot_width:]], axis=1).astype(jnp.bfloat16)
    own = done[:leaf_count]
    other = trade(done[leaf_count:])
    q_width = q_bias.shape[0] // 2

    kv_half = v_width // HEAD_WIDTH
    query_group = q_bias.shape[0] // key_bias.shape[0]
    outs = []
    for which, block in ((side, own), (1 - side, other)):
        q = block[:, :q_width].reshape(leaf_count, kv_half, query_group, HEAD_WIDTH)
        k = block[:, q_width : q_width + v_width].reshape(leaf_count, kv_half, HEAD_WIDTH)
        v = block[:, q_width + v_width :].reshape(leaf_count, kv_half, HEAD_WIDTH)
        for head in range(kv_half):
            at = (which * kv_half + head) * HEAD_WIDTH
            outs.append(
                attend_single_head(
                    q[:, head],
                    k[:, head],
                    v[:, head],
                    lax.dynamic_slice_in_dim(prefix_key_cache, at, HEAD_WIDTH, 2),
                    lax.dynamic_slice_in_dim(prefix_value_cache, at, HEAD_WIDTH, 2),
                    parent_prefix_slot,
                    prefix_length,
                )
                .reshape(leaf_count, query_group * HEAD_WIDTH)
                .astype(jnp.bfloat16)
            )
    mine = jnp.concatenate(outs[:kv_half], axis=1)
    theirs = jnp.concatenate(outs[kv_half:], axis=1)
    attended = jnp.where(
        side == 0,
        jnp.concatenate([mine, theirs], axis=1),
        jnp.concatenate([theirs, mine], axis=1),
    )

    wo_all = lax.all_gather(wo_local, "actor", axis=0, tiled=True)
    group = lax.axis_index("tp")
    cores = [(0, 1), (1, 0)]

    def project(rows):
        part = lax.dot_general(
            rows, wo_all, (((1,), (1,)), ((), ())), preferred_element_type=jnp.float32
        )
        width = part.shape[1] // 2
        first, second = part[:, :width], part[:, width:]
        give = jnp.where(group == 0, second, first)
        keep = jnp.where(group == 0, first, second)
        return (keep + lax.ppermute(give, "tp", cores)).astype(jnp.bfloat16), give

    def join(x):
        y = lax.ppermute(x, "tp", cores)
        return jnp.where(
            group == 0,
            jnp.concatenate([x, y], axis=1),
            jnp.concatenate([y, x], axis=1),
        )

    away, marker = project(trade(attended))
    attended, away, _ = lax.optimization_barrier((attended, away, marker))
    away = trade(away)
    local = join(project(attended)[0])
    remote = join(away)
    low = jnp.where(side == 0, local, remote)
    high = jnp.where(side == 0, remote, local)
    pieces = []
    half = col_count // 2
    for a in range(n_actor):
        pieces += [low[:, a * half : (a + 1) * half], high[:, a * half : (a + 1) * half]]
    return jnp.concatenate(pieces, axis=1)


LANES = 128


def fused_kernel(
    n_actor,
    states_ref,
    gain_ref,
    wq_ref,
    wq_scale_ref,
    wk_ref,
    wk_scale_ref,
    wv_ref,
    wv_scale_ref,
    wo_ref,
    wo_scale_ref,
    qb_ref,
    kb_ref,
    vb_ref,
    kcache_ref,
    vcache_ref,
    parent_ref,
    length_ref,
    out_ref,
    raw_ref,
    rawv_ref,
    wown_ref,
    woth_ref,
    give_ref,
    xraw_ref,
    xs_ref,
    lens_ref,
    tabs_ref,
    gains_ref,
    bias_ref,
    acc_ref,
    rst_ref,
    vst_ref,
    rq_ref,
    rv_ref,
    kc_ref,
    vc_ref,
    woraw_ref,
    zset_ref,
    mask_ref,
    att_ref,
    psend_ref,
    precv_ref,
    res_ref,
    load_sem,
    kv_sem,
    z_send,
    z_recv,
    g_send,
    x_send,
    x_recv,
    xs_send,
    xs_recv,
    t_send,
    t_recv,
    q_send,
    q_recv,
    v_send,
    v_recv,
    a_send,
    a_recv,
    oz_send,
    oz_recv,
    p_send,
    p_recv,
    c_send,
    c_recv,
    f_send,
    f_recv,
):
    line = n_actor // 2
    actor = lax.axis_index("actor")
    job = lax.axis_index("job")
    core = lax.axis_index("tp")
    at, y = actor // 2, actor % 2
    side = job % 2
    there = {"job": job + 1 - 2 * side}
    pair = {"actor": at * 2 + 1 - y}
    diagonal = {"job": job + 1 - 2 * side, "actor": at * 2 + 1 - y}
    sibling = {"tp": 1 - core}
    above, below = {"actor": actor + 2}, {"actor": actor - 2}
    has_up, has_down = at + 1 < line, at >= 1
    middle = jnp.logical_and(has_up, has_down)
    ends = jnp.logical_not(middle)
    rows = raw_ref.shape[1]
    count = xraw_ref.shape[0]
    half_rows = rows // 2
    half_count = count // 2
    width = raw_ref.shape[2]
    units = width // LANES
    heads = 2 * units - 1
    depth = zset_ref.shape[1]
    strips = n_actor // 2
    part = strips // 2
    f32, bf16 = jnp.float32, jnp.bfloat16

    def lanes(unit, n=1):
        return pl.ds(pl.multiple_of(unit * LANES, LANES), n * LANES)

    barrier = pltpu.get_barrier_semaphore()

    @pl.when(has_up)
    def _():
        pl.semaphore_signal(barrier, inc=1, device_id=above)

    @pl.when(has_down)
    def _():
        pl.semaphore_signal(barrier, inc=1, device_id=below)

    for peer in (there, pair, diagonal, sibling):
        pl.semaphore_signal(barrier, inc=1, device_id=peer)

    def local(source, target, sem):
        return pltpu.make_async_copy(source, target, sem)

    def remote(source, target, ss, rs, peer):
        return pltpu.make_async_remote_copy(
            src_ref=source, dst_ref=target, send_sem=ss, recv_sem=rs, device_id=peer
        )

    first = 2 * side
    w_loads = [
        local(wq_ref.at[:, lanes(side * heads, units)], raw_ref.at[0], load_sem.at[0]),
        local(
            wq_ref.at[:, lanes(side * heads + units, units - 1)],
            raw_ref.at[1, :, pl.ds(0, (units - 1) * LANES)],
            load_sem.at[1],
        ),
        local(
            wk_ref.at[:, lanes(side)],
            raw_ref.at[1, :, pl.ds((units - 1) * LANES, LANES)],
            load_sem.at[2],
        ),
        local(wv_ref.at[:, lanes(side)], rawv_ref, load_sem.at[3]),
    ]
    state_load = local(states_ref, xraw_ref, load_sem.at[4])
    wo_load = local(
        wo_ref.at[:, lanes(first, 2)], woraw_ref.at[:, pl.ds(0, 2 * LANES)], load_sem.at[5]
    )
    wo_load_last = local(
        wo_ref.at[:, pl.ds(4 * LANES, LANES)], woraw_ref.at[:, pl.ds(2 * LANES, LANES)],
        load_sem.at[6],
    )
    for copy in w_loads:
        copy.start()
    state_load.start()
    wo_load.start()
    wo_load_last.start()
    kv_loads = []
    for j in range(2):
        for p in range(2):
            place = pl.ds(p * LANES, LANES)
            cut = pl.ds(j * LANES, LANES)
            kv_loads.append(
                local(kcache_ref.at[p, :, cut], kc_ref.at[j, :, place], kv_sem.at[0, j, p])
            )
            kv_loads.append(
                local(vcache_ref.at[p, :, cut], vc_ref.at[j, :, place], kv_sem.at[1, j, p])
            )
    for copy in kv_loads:
        copy.start()

    blocks = rows // SCALE_BLOCK

    def pick(ref, row, column):
        values = ref[pl.ds(row, 1), :]
        here = lax.broadcasted_iota(jnp.int32, values.shape, 1) == column
        return jnp.sum(jnp.where(here, values, 0.0), axis=1, keepdims=True)

    def unit_scale(parity, block, u):
        row = actor * blocks + block
        if u < units - 1:
            return pick(wq_scale_ref, side * heads + u + units * parity, row)
        return jnp.where(
            parity == 0,
            pick(wq_scale_ref, side * heads + u, row),
            pick(wk_scale_ref, side, row),
        )

    def expand(parity, target):
        for block in range(blocks):
            cut = pl.ds(block * SCALE_BLOCK, SCALE_BLOCK)
            for u in range(units):
                lane = pl.ds(u * LANES, LANES)
                scaled = raw_ref[parity, cut, lane].astype(f32) * unit_scale(parity, block, u)
                target(cut, lane, scaled.astype(bf16))

    def to_give(cut, lane, value):
        give_ref[cut, lane] = value

    def to_own(cut, lane, value):
        wown_ref[at, cut, lane] = value

    for copy in w_loads:
        copy.wait()
    expand(y, to_own)
    for block in range(blocks):
        cut = pl.ds(block * SCALE_BLOCK, SCALE_BLOCK)
        scale = pick(wv_scale_ref, side, actor * blocks + block)
        wown_ref[at, cut, pl.ds(width, LANES)] = (rawv_ref[cut, :].astype(f32) * scale).astype(
            bf16
        )
    pl.semaphore_wait(barrier, 4 + has_up.astype(jnp.int32) + has_down.astype(jnp.int32))

    def half(p):
        return pl.ds(p * half_rows, half_rows)

    def give(p):
        return remote(
            give_ref.at[half(p)], woth_ref.at[at, half(p)], g_send.at[p], z_recv.at[1, at, p], pair
        )

    def up_down(way, kind, spot, p):
        ref = (wown_ref if kind == 0 else woth_ref).at[spot, half(p)]
        return remote(
            ref, ref, z_send.at[way, kind, spot, p], z_recv.at[kind, spot, p], (above, below)[way]
        )

    def both_ways(kind, spot, p):
        @pl.when(has_up)
        def _():
            up_down(0, kind, spot, p).start()

        @pl.when(has_down)
        def _():
            up_down(1, kind, spot, p).start()

    for p in range(2):
        both_ways(0, at, p)
    expand(1 - y, to_give)
    for p in range(2):
        give(p).start()

    lens_ref[0] = length_ref[...].astype(f32).reshape(1, count)
    table_sends = [
        remote(lens_ref.at[0], lens_ref.at[slot], t_send.at[slot], t_recv.at[slot], peer)
        for slot, peer in ((1, there), (2, pair), (3, diagonal))
    ]
    for copy in table_sends:
        copy.start()

    state_load.wait()

    gains_ref[...] = gain_ref[...].astype(f32).reshape(1, -1)
    for i, ref in enumerate((qb_ref, kb_ref, vb_ref)):
        bias_ref[i, :, : ref.shape[0]] = ref[...].astype(f32).reshape(1, -1)

    def normalize(i, carry):
        cut = pl.ds(pl.multiple_of(i * 16, 16), 16)
        x = xraw_ref[cut, :].astype(f32)
        x = x * lax.rsqrt(jnp.mean(x * x, axis=-1, keepdims=True) + epsilon)
        x = (x * gains_ref[...]).astype(bf16)
        for source in range(n_actor):
            xs_ref[source, cut, :] = x[:, source * rows : (source + 1) * rows]
        return carry

    lax.fori_loop(0, count // 16, normalize, 0)

    def some(p):
        return pl.ds(core * strips + p * part, part)

    def of_slot(slot):
        return pl.ds(slot * count, count)

    def share(slot, p, origin, peer):
        return remote(
            xs_ref.at[some(p), of_slot(origin)],
            xs_ref.at[some(p), of_slot(slot)],
            x_send.at[slot - 1, p],
            x_recv.at[slot - 1, p],
            peer,
        )

    share_list = [
        share(1, 0, 0, there),
        share(2, 1, 0, pair),
        share(1, 1, 0, there),
        share(2, 0, 0, pair),
    ]
    for copy in share_list:
        copy.start()

    def to_sibling(slot, p):
        ref = xs_ref.at[some(p), of_slot(slot)]
        return remote(ref, ref, xs_send.at[slot - 1, p], xs_recv.at[slot - 1, p], sibling)

    def from_sibling(slot, p):
        ref = xs_ref.at[pl.ds((1 - core) * strips + p * part, part), of_slot(slot)]
        return remote(ref, ref, xs_send.at[slot - 1, p], xs_recv.at[slot - 1, p], sibling)

    def column(values):
        wide = jnp.broadcast_to(values, (LANES, count))
        return wide.T

    lane_at = lax.broadcasted_iota(jnp.int32, (count, LANES), 1)
    step = lax.rem(lax.broadcasted_iota(jnp.int32, (1, LANES), 1), LANES // 2).astype(f32)
    freqs = jnp.exp(step * (-2.0 * math.log(rope_base) / LANES))
    def make_table(slot):
        angles = column(lens_ref[slot]) * freqs
        tabs_ref[slot] = jnp.where(lane_at < LANES // 2, jnp.cos(angles), jnp.sin(angles))


    wo_load.wait()
    wo_load_last.wait()
    wo_blocks = depth // SCALE_BLOCK
    wo_units = wo_ref.shape[1] // LANES

    def expand_wo(block, carry):
        cut = pl.ds(pl.multiple_of(block * SCALE_BLOCK, SCALE_BLOCK), SCALE_BLOCK)
        for u in range(2):
            lane = pl.ds(u * LANES, LANES)
            scale = pick(wo_scale_ref, block, actor * wo_units + first + u)
            zset_ref[at, cut, lane] = (woraw_ref[cut, lane].astype(f32) * scale).astype(bf16)
        return carry

    lax.fori_loop(0, wo_blocks, expand_wo, 0)

    def has_extra(spot, s):
        return spot % 2 == s

    @pl.when(has_extra(at, side))
    def _():
        def expand_last(block, carry):
            cut = pl.ds(pl.multiple_of(block * SCALE_BLOCK, SCALE_BLOCK), SCALE_BLOCK)
            lane = pl.ds(2 * LANES, LANES)
            scale = pick(wo_scale_ref, block, actor * wo_units + 4)
            zset_ref[at, cut, lane] = (woraw_ref[cut, lane].astype(f32) * scale).astype(bf16)
            return carry

        lax.fori_loop(0, wo_blocks, expand_last, 0)

    def wo_way(way, spot, q):
        ref = zset_ref.at[spot, :, pl.ds(q * LANES, LANES)]
        return remote(
            ref, ref, oz_send.at[way, spot, q], oz_recv.at[spot, q], (above, below)[way]
        )

    def each_piece(spot, action):
        for q in range(2):
            action(q)

        @pl.when(has_extra(spot, side))
        def _():
            action(2)

    def wo_begin(far):
        @pl.when(jnp.logical_and(at == far, has_up))
        def _():
            each_piece(at, lambda q: wo_way(0, at, q).start())

        @pl.when(jnp.logical_and(line - 1 - at == far, has_down))
        def _():
            each_piece(at, lambda q: wo_way(1, at, q).start())

    def relay_one(way, spot):
        def action(q):
            wo_way(way, spot, q).wait_recv()

            @pl.when((has_up, has_down)[way])
            def _():
                wo_way(way, spot, q).start()

        each_piece(spot, action)

    def relay(far):
        @pl.when(at >= far)
        def _():
            relay_one(0, at - far)

        @pl.when(at + far < line)
        def _():
            relay_one(1, at + far)

    for p in range(2):
        give(p).wait_recv()
        both_ways(1, at, p)
    wo_begin(0)

    acc_ref[...] = jnp.zeros_like(acc_ref)
    make_table(0)
    for slot in (1, 2, 3):
        table_sends[slot - 1].wait_recv()
        make_table(slot)
    length = column(lens_ref[0])[:, :1].astype(jnp.int32)
    mask_ref[...] = jnp.where(
        lax.broadcasted_iota(jnp.int32, mask_ref.shape, 1) < length, 0.0, -jnp.inf
    )

    def multiply_kind(kind, spot):
        if kind == 0:
            acc_ref[...] += jnp.dot(
                xs_ref[spot * 2 + y], wown_ref[spot], preferred_element_type=f32
            )
        else:
            acc_ref[:, :width] += jnp.dot(
                xs_ref[spot * 2 + 1 - y], woth_ref[spot], preferred_element_type=f32
            )

    def multiply(spot):
        multiply_kind(0, spot)
        multiply_kind(1, spot)

    def multiply_far(far, carry):
        @pl.when(at >= far)
        def _():
            multiply(at - far)

        @pl.when(jnp.logical_and(at + far < line, far > 0))
        def _():
            multiply(at + far)

        return carry

    def rows_first():
        for slot, p, peer in ((1, 0, pair), (2, 1, there), (1, 1, None), (2, 0, None)):
            share(slot, p, 0, there if slot == 1 else pair).wait_recv()
            if peer is not None:
                share(3, p, slot, peer).start()
            to_sibling(slot, p).start()

    def rows_rest():
        for p in range(2):
            share(3, p, 1 + p, pair if p == 0 else there).wait_recv()
            to_sibling(3, p).start()

        for slot in (1, 2, 3):
            for p in range(2):
                from_sibling(slot, p).wait_recv()

    for far in range(1, line):
        for kind in range(2):
            for p in range(2):

                @pl.when(at >= far)
                def _():
                    up_down(0, kind, at - far, p).wait_recv()

                    @pl.when(has_up)
                    def _():
                        up_down(0, kind, at - far, p).start()

                @pl.when(at + far < line)
                def _():
                    up_down(1, kind, at + far, p).wait_recv()

                    @pl.when(has_down)
                    def _():
                        up_down(1, kind, at + far, p).start()

            if far == line - 1:

                @pl.when(at >= far)
                def _():
                    multiply_kind(kind, at - far)

                @pl.when(at + far < line)
                def _():
                    multiply_kind(kind, at + far)

        wo_begin(far)
        if far == 1:
            rows_first()
        if far == max(line - 2, 1):
            rows_rest()
            lax.fori_loop(0, max(line - 1, 1), multiply_far, 0)

    def results(slot):
        return (
            remote(rst_ref.at[slot], rq_ref.at[slot], q_send.at[slot], q_recv.at[slot], peers[slot]),
            remote(vst_ref.at[slot], rv_ref.at[slot], v_send.at[slot], v_recv.at[slot], peers[slot]),
        )

    peers = {1: there, 2: pair, 3: diagonal}
    for slot in (2, 1, 3, 0):
        table = tabs_ref[slot]
        swapped = pltpu.roll(table, LANES // 2, 1)
        cosine = jnp.where(lane_at < LANES // 2, table, swapped)
        sine = jnp.where(lane_at < LANES // 2, -swapped, table)
        for u in range(units):
            if u < units - 1:
                bias = bias_ref[0, :, lanes(side * heads + u + units * y)]
            else:
                bias = jnp.where(
                    y == 0,
                    bias_ref[0, :, lanes(side * heads + u)],
                    bias_ref[1, :, lanes(side)],
                )
            value = acc_ref[of_slot(slot), u * LANES : (u + 1) * LANES] + bias
            value = value * cosine + pltpu.roll(value, LANES // 2, 1) * sine
            (rst_ref if slot else rq_ref)[slot, u] = value.astype(bf16)
        (vst_ref if slot else rv_ref)[slot] = acc_ref[of_slot(slot), width:]
        if slot:
            for copy in results(slot):
                copy.start()

    @pl.when(middle)
    def _():
        relay(1)

    for copy in kv_loads:
        copy.wait()
    parent = column(parent_ref[...].astype(f32).reshape(1, count))[:, :1]
    in_first = (parent == 0).astype(f32)
    in_second = 1.0 - in_first
    scale_factor = math.log2(math.e) / math.sqrt(LANES)

    head_parts = ((0, units), (units, heads - units))

    def hand(slot, j, origin, peer, piece):
        cut = lanes(j * heads + head_parts[piece][0], head_parts[piece][1])

        def of(k):
            return att_ref.at[:, pl.ds(k * half_count, half_count), cut]

        return remote(
            of(origin),
            of(slot),
            a_send.at[slot - 1, origin - 1 if slot == 3 else j, piece],
            a_recv.at[slot - 1, j, piece],
            peer,
        )

    chunks = 4
    context = kc_ref.shape[1] // chunks

    def attend(base):
        group = side if base == 0 else 1 - side
        low = jnp.where(y == 0, base, base + 2)
        high = jnp.where(y == 0, base + 2, base)
        key_new = rq_ref[high, units - 1].astype(f32)
        value_new = rv_ref[base] + rv_ref[base + 2] + bias_ref[2, :, lanes(group)]
        value_new = value_new.astype(bf16).astype(f32)

        def head(h, carry):
            query = rq_ref[
                jnp.where(h < units, low, high), jnp.where(h < units, h, h - units)
            ].astype(f32)
            own = jnp.sum(query * key_new, axis=-1, keepdims=True) * scale_factor
            both = jnp.concatenate([query * in_first, query * in_second], axis=1).astype(bf16)
            highest = own
            pieces = []
            for c in range(chunks):
                scores = lax.dot_general(
                    both,
                    kc_ref[group, c * context : (c + 1) * context],
                    (((1,), (1,)), ((), ())),
                    preferred_element_type=f32,
                )
                scores = scores * scale_factor + mask_ref[:, c * context : (c + 1) * context]
                highest = jnp.maximum(highest, jnp.max(scores, axis=-1, keepdims=True))
                pieces.append(scores)
            own = jnp.exp2(own - highest)
            total, mixed = own, None
            for c, scores in enumerate(pieces):
                weights = jnp.exp2(scores - highest)
                total = total + jnp.sum(weights, axis=-1, keepdims=True)
                more = jnp.dot(
                    weights.astype(bf16),
                    vc_ref[group, c * context : (c + 1) * context],
                    preferred_element_type=f32,
                )
                mixed = more if mixed is None else mixed + more
            mixed = jnp.where(parent == 0, mixed[:, :LANES], mixed[:, LANES:])
            mixed = mixed + own.astype(bf16).astype(f32) * value_new
            mixed = (mixed / total).astype(bf16)
            for which in range(2):
                att_ref[which, :half_count, lanes(group * heads + h)] = mixed[
                    which * half_count : (which + 1) * half_count
                ]
            return carry

        for piece, (start, n) in enumerate(head_parts):
            lax.fori_loop(start, start + n, head, 0)
            hand(1, group, 0, there, piece).start()
            hand(2, group, 0, pair, piece).start()

    for copy in results(2):
        copy.wait_recv()
    attend(0)

    for slot in (1, 3):
        for copy in results(slot):
            copy.wait_recv()
    attend(1)
    for piece in range(2):
        hand(2, side, 0, pair, piece).wait_recv()
        hand(3, side, 2, there, piece).start()
    for piece in range(2):
        hand(1, side, 0, there, piece).wait_recv()
        hand(3, side, 1, pair, piece).start()

    @pl.when(middle)
    def _():
        relay(2)

    for piece in range(2):
        hand(1, 1 - side, 0, there, piece).wait_recv()
        hand(2, 1 - side, 0, pair, piece).wait_recv()

    bounds = tuple(pl.ds(k * LANES, LANES) for k in range(3))

    groups = ((0, 3), (3, 1))

    def rows_of(g):
        return pl.ds(groups[g][0] * half_count, groups[g][1] * half_count)

    def p_copy(spot, k, g):
        return remote(
            psend_ref.at[spot, rows_of(g), bounds[k]],
            precv_ref.at[spot, rows_of(g), bounds[k]],
            p_send.at[spot, k, g],
            p_recv.at[spot, k, g],
            sibling,
        )

    def unit_of(spot, s, parity, k):
        return wo_units * (2 * spot + parity) + (4 if k == 2 else 2 * s + k)

    def target(spot, s, parity, k):
        mine = pl.ds(pl.multiple_of(core * half_count, half_count), half_count)
        return out_ref.at[mine, lanes(unit_of(spot, s, parity, k))]

    def result(spot, slot, k):
        return res_ref.at[spot, pl.ds(slot * half_count, half_count), bounds[k]]

    def sibling_copy(spot, k):
        return remote(
            target(spot, side, y, k),
            target(spot, side, y, k),
            f_send.at[0, spot, k],
            f_recv.at[0, spot, k],
            sibling,
        )

    def send_copy(spot, slot, k):
        return remote(
            result(spot, slot, k),
            target(spot, side, y, k),
            c_send.at[slot - 1, spot, k],
            c_recv.at[slot - 1, spot, k],
            peers[slot],
        )

    source_side = (side, 1 - side, side, 1 - side)
    source_parity = (y, y, 1 - y, 1 - y)

    def onward_copy(spot, slot, k):
        ref = target(spot, source_side[slot], source_parity[slot], k)
        return remote(ref, ref, f_send.at[slot, spot, k], f_recv.at[slot, spot, k], sibling)

    def across(ks):
        return pl.ds(ks[0] * LANES, len(ks) * LANES)

    def send_part(spot, ks, g):
        psend_ref[spot, rows_of(g), across(ks)] = jnp.dot(
            att_ref[1 - core, rows_of(g)], zset_ref[spot, :, across(ks)], preferred_element_type=f32
        )
        for k in ks:
            p_copy(spot, k, g).start()

    def keep_part(spot, ks, g):
        kept = jnp.dot(
            att_ref[core, rows_of(g)], zset_ref[spot, :, across(ks)], preferred_element_type=f32
        )
        for k in ks:
            p_copy(spot, k, g).wait_recv()
        kept = (kept + precv_ref[spot, rows_of(g), across(ks)]).astype(bf16)
        res_ref[spot, rows_of(g), across(ks)] = kept
        if g == 1:
            for k in ks:
                send_copy(spot, 3, k).start()
            return
        for slot in (1, 2):
            for k in ks:
                send_copy(spot, slot, k).start()
        mine = pl.ds(pl.multiple_of(core * half_count, half_count), half_count)
        for i, k in enumerate(ks):
            out_ref[mine, lanes(unit_of(spot, side, y, k))] = kept[
                :half_count, i * LANES : (i + 1) * LANES
            ]
            sibling_copy(spot, k).start()

    def wide_part(spot, action):
        action((0, 1))

        @pl.when(has_extra(spot, side))
        def _():
            action((2,))

    def each_part(spot, s, action):
        action(0)
        action(1)

        @pl.when(has_extra(spot, s))
        def _():
            action(2)

    def project_send(spot, g):
        wide_part(spot, lambda ks: send_part(spot, ks, g))

    def project_keep(spot, g):
        wide_part(spot, lambda ks: keep_part(spot, ks, g))

    def onward(spot):
        for slot in (1, 2, 3):

            def action(k):
                send_copy(spot, slot, k).wait_recv()
                onward_copy(spot, slot, k).start()

            each_part(spot, source_side[slot], action)

    def at_far(action, far):
        @pl.when(at >= far)
        def _():
            action(at - far)

        @pl.when(jnp.logical_and(at + far < line, far > 0))
        def _():
            action(at + far)

    def relays(far, carry):
        @pl.when(jnp.logical_and(far > 0, jnp.logical_or(ends, far > 2)))
        def _():
            relay(far)

        return carry

    def sends(g):
        def body(far, carry):
            if g == 0:
                relays(far, 0)
            at_far(lambda spot: project_send(spot, g), far)
            return carry

        return body

    def keeps(g):
        def body(far, carry):
            at_far(lambda spot: project_keep(spot, g), far)
            return carry

        return body

    def onwards(far, carry):
        at_far(onward, far)
        return carry

    lax.fori_loop(0, line - 1, sends(0), 0)
    lax.fori_loop(0, line - 1, keeps(0), 0)
    for j in range(2):
        for piece in range(2):
            hand(3, j, 1, pair, piece).wait_recv()
    lax.fori_loop(0, line - 1, sends(1), 0)
    lax.fori_loop(0, line - 1, keeps(1), 0)

    @pl.when(ends)
    def _():
        def last(way, spot):
            def action(q):
                wo_way(way, spot, q).wait_recv()
                for g in (0, 1):
                    send_part(spot, (q,), g)
                for g in (1, 0):
                    keep_part(spot, (q,), g)

            each_piece(spot, action)

        @pl.when(at >= line - 1)
        def _():
            last(0, at - (line - 1))

        @pl.when(at + line - 1 < line)
        def _():
            last(1, at + line - 1)

    lax.fori_loop(0, line, onwards, 0)

    for p in range(2):
        give(p).wait_send()
        for slot, peer in ((1, there), (2, pair), (3, pair)):
            share(slot, p, 0, peer).wait_send()
            to_sibling(slot, p).wait_send()
    for copy in table_sends:
        copy.wait_send()
    for slot in (1, 2, 3):
        for copy in results(slot):
            copy.wait_send()
    for j in range(2):
        for slot in (1, 2, 3):
            for piece in range(2):
                hand(slot, j, j + 1 if slot == 3 else 0, there, piece).wait_send()

    def finish(spot, carry):
        @pl.when(jnp.logical_and(has_up, at >= spot))
        def _():
            for kind in range(2):
                for p in range(2):
                    up_down(0, kind, spot, p).wait_send()
            each_piece(spot, lambda q: wo_way(0, spot, q).wait_send())

        @pl.when(jnp.logical_and(has_down, at <= spot))
        def _():
            for kind in range(2):
                for p in range(2):
                    up_down(1, kind, spot, p).wait_send()
            each_piece(spot, lambda q: wo_way(1, spot, q).wait_send())

        def end_part(k):
            for g in range(2):
                p_copy(spot, k, g).wait_send()
            sibling_copy(spot, k).wait()
            for slot in (1, 2, 3):
                send_copy(spot, slot, k).wait_send()

        each_part(spot, side, end_part)
        for slot in (1, 2, 3):
            each_part(
                spot, source_side[slot], lambda k: onward_copy(spot, slot, k).wait()
            )
        return carry

    lax.fori_loop(0, line, finish, 0)


def fused(n_actor, args):
    (
        leaf_states, norm_gain, wq_quant, wq_scale, wk, wk_scale, wv, wv_scale, wo_quant, wo_scale,
        q_bias, key_bias, value_bias, kcache, vcache, parent, length,
    ) = args
    count, features = leaf_states.shape
    rows = wq_quant.shape[0]
    heads = wq_quant.shape[1] // (2 * LANES)
    units = (heads + 1) // 2
    width = units * LANES
    context = kcache.shape[1]
    depth = wo_quant.shape[0]
    line = n_actor // 2
    total_units = n_actor * (wo_quant.shape[1] // LANES)
    bf16, f32 = jnp.bfloat16, jnp.float32
    any_space = pl.BlockSpec(memory_space=pl.ANY)
    vmem = pl.BlockSpec(memory_space=pltpu.VMEM)
    dma = pltpu.SemaphoreType.DMA
    return pl.pallas_call(
        functools.partial(fused_kernel, n_actor),
        out_shape=jax.ShapeDtypeStruct((count, total_units * LANES), bf16),
        in_specs=[
            any_space, vmem, any_space, vmem, any_space, vmem, any_space, vmem, any_space, vmem,
            vmem, vmem, vmem, any_space, any_space, vmem, vmem,
        ],
        out_specs=vmem,
        scratch_shapes=[
            pltpu.VMEM((2, rows, width), bf16),
            pltpu.VMEM((rows, LANES), bf16),
            pltpu.VMEM((line, rows, width + LANES), bf16),
            pltpu.VMEM((line, rows, width), bf16),
            pltpu.VMEM((rows, width), bf16),
            pltpu.VMEM((count, features), bf16),
            pltpu.VMEM((n_actor, 4 * count, rows), bf16),
            pltpu.VMEM((4, 1, count), f32),
            pltpu.VMEM((4, count, LANES), f32),
            pltpu.VMEM((1, features), f32),
            pltpu.VMEM((3, 1, 2 * heads * LANES), f32),
            pltpu.VMEM((4 * count, width + LANES), f32),
            pltpu.VMEM((4, units, count, LANES), bf16),
            pltpu.VMEM((4, count, LANES), f32),
            pltpu.VMEM((4, units, count, LANES), bf16),
            pltpu.VMEM((4, count, LANES), f32),
            pltpu.VMEM((2, context, 2 * LANES), bf16),
            pltpu.VMEM((2, context, 2 * LANES), bf16),
            pltpu.VMEM((depth, 3 * LANES), bf16),
            pltpu.VMEM((line, depth, 3 * LANES), bf16),
            pltpu.VMEM((count, context), f32),
            pltpu.VMEM((2, 2 * count, 2 * heads * LANES), bf16),
            pltpu.VMEM((line, 2 * count, 3 * LANES), f32),
            pltpu.VMEM((line, 2 * count, 3 * LANES), f32),
            pltpu.VMEM((line, 2 * count, 3 * LANES), bf16),
            dma((7,)),
            dma((2, 2, 2)),
            dma((2, 2, line, 2)),
            dma((2, line, 2)),
            dma((2,)),
            dma((3, 2)),
            dma((3, 2)),
            dma((3, 2)),
            dma((3, 2)),
            dma((4,)),
            dma((4,)),
            dma((4,)),
            dma((4,)),
            dma((4,)),
            dma((4,)),
            dma((3, 2, 2)),
            dma((3, 2, 2)),
            dma((2, line, 3)),
            dma((line, 3)),
            dma((line, 3, 2)),
            dma((line, 3, 2)),
            dma((3, line, 3)),
            dma((3, line, 3)),
            dma((4, line, 3)),
            dma((4, line, 3)),
        ],
        compiler_params=pltpu.CompilerParams(
            collective_id=0, has_side_effects=True, vmem_limit_bytes=58 * 1024 * 1024
        ),
        cost_estimate=pl.CostEstimate(
            flops=13_000_000_000, bytes_accessed=30_000_000, transcendentals=6_000_000
        ),
    )(
        leaf_states, norm_gain, wq_quant, wq_scale.T, wk, wk_scale.T, wv, wv_scale.T, wo_quant,
        wo_scale, q_bias, key_bias, value_bias, kcache, vcache, parent, length,
    )


def per_device_fused(n_actor, *args):
    return fused(n_actor, args)


def fits_fused(mesh_sizes, args):
    n_job, n_actor, n_tp = mesh_sizes
    return (
        n_tp == 2
        and n_job % 2 == 0
        and n_actor % 8 == 0
        and args[0].shape[0] % 32 == 0
        and args[2].shape[0] % SCALE_BLOCK == 0
        and (args[2].shape[1] // LANES) % 4 == 2
        and args[4].shape[1] == 2 * LANES
        and args[8].shape[1] == 5 * LANES
        and args[13].shape[0] == 2
    )


def per_device_any(mesh_sizes, *args):
    if fits_fused(mesh_sizes, args):
        return per_device_fused(mesh_sizes[1], *args)
    return per_device(mesh_sizes[:2], *args)


def solution(mesh):
    placed = (
        P(("job", "actor"), None),
        P(),
        P("actor", "tp"),
        P(None, "tp"),
        P("actor", "tp"),
        P(None, "tp"),
        P("actor", "tp"),
        P(None, "tp"),
        P("tp", "actor"),
        P("tp", None),
        P("tp"),
        P("tp"),
        P("tp"),
        P(("job", "actor"), None, "tp"),
        P(("job", "actor"), None, "tp"),
        P(("job", "actor")),
        P(("job", "actor")),
    )
    return jax.shard_map(
        functools.partial(
            per_device_any, (mesh.shape["job"], mesh.shape["actor"], mesh.shape["tp"])
        ),
        mesh=mesh,
        in_specs=placed,
        out_specs=P(("job", "actor"), None),
        check_vma=False,
    )
```

```python
import functools
import math

import jax
import jax.numpy as jnp
from jax import lax
from jax.experimental import pallas as pl
from jax.experimental.pallas import tpu as pltpu
from jax.sharding import PartitionSpec as P

HEAD_WIDTH = 128
SCALE_BLOCK = 128


epsilon = 1e-06
rope_base = 1000000.0


def apply_rotary(values, length):
    width = values.shape[-1]
    half_width = width // 2
    freqs = rope_base ** (-(jnp.arange(half_width, dtype=jnp.float32) * 2.0 / width))
    angles = length.astype(jnp.float32)[:, None] * freqs[None, :]
    cosine = jnp.cos(angles)[:, None, :]
    sine = jnp.sin(angles)[:, None, :]
    first = values[..., :half_width]
    second = values[..., half_width:]
    return jnp.concatenate(
        [first * cosine - second * sine, second * cosine + first * sine], axis=-1
    )


def attend_single_head(
    query_vector, key_self, value_self, prefix_key_cache, prefix_value_cache, parent, length
):
    scale_factor = 1.0 / math.sqrt(query_vector.shape[-1])
    self_score = (
        jnp.sum(
            query_vector.astype(jnp.float32) * key_self.astype(jnp.float32)[:, None, :], axis=-1
        )
        * scale_factor
    )
    visible = (jnp.arange(prefix_key_cache.shape[1])[None, :] < length[:, None])[:, None, :]
    outcome = jnp.zeros(query_vector.shape, jnp.float32)
    for prefix_index in range(prefix_key_cache.shape[0]):
        scores = (
            jnp.einsum(
                "lge,ce->lgc",
                query_vector,
                prefix_key_cache[prefix_index],
                preferred_element_type=jnp.float32,
            )
            * scale_factor
        )
        highest = jnp.maximum(jnp.max(jnp.where(visible, scores, -jnp.inf), axis=-1), self_score)
        weights = jnp.where(visible, jnp.exp(scores - highest[..., None]), 0.0)
        self_weight = jnp.exp(self_score - highest)
        total = jnp.sum(weights, axis=-1) + self_weight
        self_rounded = lax.optimization_barrier(self_weight.astype(jnp.bfloat16)).astype(
            jnp.float32
        )
        mixed = jnp.einsum(
            "lgc,ce->lge",
            weights.astype(jnp.bfloat16),
            prefix_value_cache[prefix_index],
            preferred_element_type=jnp.float32,
        )
        mixed = mixed + self_rounded[..., None] * value_self.astype(jnp.float32)[:, None, :]
        outcome = jnp.where(
            (parent == prefix_index)[:, None, None], mixed / total[..., None], outcome
        )
    return outcome


PIECE = 5
EARLY = 1


def spread_kernel(
    n_actor,
    rows_each,
    mine_ref,
    row_ref,
    gain_ref,
    sums_ref,
    all_ref,
    raw_ref,
    x_ref,
    home_sem,
    send_sem,
    recv_sem,
    row_sem,
):
    line = n_actor // 2
    actor = lax.axis_index("actor")
    job = lax.axis_index("job")
    at, y = actor // 2, actor % 2
    partner = job + 1 - 2 * (job % 2)
    pair = at * 2 + 1 - y
    has_up, has_down = at + 1 < line, at >= 1
    count = row_ref.shape[0]
    depth = mine_ref.shape[0]
    barrier = pltpu.get_barrier_semaphore()

    @pl.when(has_up)
    def _():
        pl.semaphore_signal(barrier, inc=1, device_id={"actor": actor + 2})

    @pl.when(has_down)
    def _():
        pl.semaphore_signal(barrier, inc=1, device_id={"actor": actor - 2})

    pl.semaphore_signal(barrier, inc=1, device_id={"actor": pair})
    pl.semaphore_signal(barrier, inc=1, device_id={"job": partner})
    pl.semaphore_wait(barrier, 2 + has_up.astype(jnp.int32) + has_down.astype(jnp.int32))

    def send(stream, source, piece, target, own=False):
        cut = pl.ds(piece * rows_each, rows_each)
        return pltpu.make_async_remote_copy(
            src_ref=mine_ref.at[cut] if own else all_ref.at[source, cut],
            dst_ref=all_ref.at[source, cut],
            send_sem=send_sem.at[stream, source, piece],
            recv_sem=recv_sem.at[source, piece],
            device_id={"actor": target},
        )

    def cross(source, piece, own=False):
        return send(0, source, piece, pair, own)

    def up(source, piece, own=False):
        return send(1, source, piece, actor + 2, own)

    def down(source, piece, own=False):
        return send(2, source, piece, actor - 2, own)

    def arrived(source, piece):
        cross(source, piece).wait_recv()

    late = list(range(PIECE - EARLY))
    early = list(range(PIECE - EARLY, PIECE))
    rows_copy = pltpu.make_async_remote_copy(
        src_ref=row_ref,
        dst_ref=raw_ref.at[pl.ds(count, count)],
        send_sem=row_sem.at[0],
        recv_sem=row_sem.at[1],
        device_id={"job": partner},
    )

    def both_ways(source, piece, own=False):
        @pl.when(has_up)
        def _():
            up(source, piece, own).start()

        @pl.when(has_down)
        def _():
            down(source, piece, own).start()

    for piece in early:
        cross(actor, piece, True).start()
    for piece in late:
        both_ways(actor, piece, True)
        cross(actor, piece, True).start()
    for piece in early:
        both_ways(actor, piece, True)
    rows_copy.start()
    home = pltpu.make_async_copy(mine_ref, all_ref.at[actor], home_sem.at[0])
    home.start()
    own_rows = pltpu.make_async_copy(row_ref, raw_ref.at[pl.ds(0, count)], home_sem.at[1])
    own_rows.start()

    def normalize(first):
        def block(i, carry):
            cut = pl.ds(pl.multiple_of(first + i * 16, 16), 16)
            rows = raw_ref[cut, :].astype(jnp.float32)
            rows = rows * lax.rsqrt(jnp.mean(rows * rows, axis=-1, keepdims=True) + epsilon)
            rows = (rows * gain_ref[...].astype(jnp.float32)).astype(jnp.bfloat16)
            for source in range(n_actor):
                x_ref[source, cut, :] = rows[:, source * depth : (source + 1) * depth]
            return carry

        lax.fori_loop(0, count // 16, block, 0)

    def add(source):
        sums_ref[...] += jnp.dot(
            x_ref[source], all_ref[source], preferred_element_type=jnp.float32
        )

    sums_ref[...] = jnp.zeros_like(sums_ref)
    own_rows.wait()
    normalize(0)
    for piece in early:
        arrived(pair, piece)
        both_ways(pair, piece)
    turn = jnp.where(at * 2 < line, 1, line - 1)

    def spot_of(k):
        return lax.rem(at + k * turn, line)

    for far in range(1, line):
        if far == line - 1:
            rows_copy.wait()
            normalize(count)
            home.wait()
            add(actor)
        todo = [(y, p) for p in late] + [(y, p) for p in early] + [(1 - y, p) for p in early]
        for index, (which, piece) in enumerate(todo):
            below = (at - far) * 2 + which
            above = (at + far) * 2 + which

            @pl.when(at >= far)
            def _():
                arrived(below, piece)

                @pl.when(has_up)
                def _():
                    up(below, piece).start()

                if index < len(late):
                    cross(below, piece).start()

            @pl.when(at + far < line)
            def _():
                arrived(above, piece)

                @pl.when(has_down)
                def _():
                    down(above, piece).start()

                if index < len(late):
                    cross(above, piece).start()

    def add_held(k, carry):
        add(spot_of(k) * 2 + y)
        return carry

    lax.fori_loop(1, line, add_held, 0)

    def add_crossed(k, carry):
        source = spot_of(k) * 2 + 1 - y
        for piece in late:
            arrived(source, piece)
        add(source)
        return carry

    lax.fori_loop(0, line, add_crossed, 0)
    for spot in range(line):
        for piece in late:
            cross(spot * 2 + y, piece).wait_send()
    for piece in early:
        cross(actor, piece).wait_send()
    for spot in range(line):
        items = [(y, p) for p in range(PIECE)] + [(1 - y, p) for p in early]
        for which, piece in items:
            source = spot * 2 + which

            @pl.when(jnp.logical_and(has_up, at >= spot))
            def _():
                up(source, piece).wait_send()

            @pl.when(jnp.logical_and(has_down, at <= spot))
            def _():
                down(source, piece).wait_send()


def spread(shard, rows, gain, n_actor):
    height, width = shard.shape
    return pl.pallas_call(
        functools.partial(spread_kernel, n_actor, height // PIECE),
        out_shape=jax.ShapeDtypeStruct((2 * rows.shape[0], width), jnp.float32),
        in_specs=[
            pl.BlockSpec(memory_space=pl.ANY),
            pl.BlockSpec(memory_space=pl.ANY),
            pl.BlockSpec(memory_space=pltpu.VMEM),
        ],
        out_specs=pl.BlockSpec(memory_space=pltpu.VMEM),
        scratch_shapes=[
            pltpu.VMEM((n_actor,) + shard.shape, shard.dtype),
            pltpu.VMEM((2 * rows.shape[0], rows.shape[1]), rows.dtype),
            pltpu.VMEM((n_actor, 2 * rows.shape[0], height), rows.dtype),
            pltpu.SemaphoreType.DMA((2,)),
            pltpu.SemaphoreType.DMA((3, n_actor, PIECE)),
            pltpu.SemaphoreType.DMA((n_actor, PIECE)),
            pltpu.SemaphoreType.DMA((2,)),
        ],
        compiler_params=pltpu.CompilerParams(
            collective_id=0, has_side_effects=True, vmem_limit_bytes=48 * 1024 * 1024
        ),
        cost_estimate=pl.CostEstimate(
            flops=0, bytes_accessed=300_000_000, transcendentals=0
        ),
    )(shard, rows, gain)


def per_device(
    mesh_sizes,
    leaf_states,
    norm_gain,
    wq_quant,
    wq_scale,
    key_weight_quantized,
    key_weight_scale,
    value_weight_quantized,
    value_weight_scale,
    wo_quant,
    wo_scale,
    q_bias,
    key_bias,
    value_bias,
    prefix_key_cache,
    prefix_value_cache,
    parent_prefix_slot,
    prefix_length,
):
    n_job, n_actor = mesh_sizes
    swap = [(i, i ^ 1) for i in range(n_job)]
    side = lax.axis_index("job") % 2
    actor = lax.axis_index("actor")

    def trade(x):
        return lax.ppermute(x, "job", swap)

    leaf_count = leaf_states.shape[0]

    def half_cols(x):
        width = x.shape[1] // 2
        return lax.dynamic_slice_in_dim(x, side * width, width, 1)

    row_count = wq_quant.shape[0]

    def expand_rows(quant, scale):
        mine = lax.dynamic_slice_in_dim(
            scale, actor * (row_count // SCALE_BLOCK), row_count // SCALE_BLOCK, 0
        ) if row_count % SCALE_BLOCK == 0 else None
        if mine is None:
            tall = jnp.repeat(scale, SCALE_BLOCK, axis=0)
            tall = lax.dynamic_slice_in_dim(tall, actor * row_count, row_count, 0)
        else:
            tall = jnp.repeat(mine, SCALE_BLOCK, axis=0)
        wide = jnp.repeat(half_cols(tall), SCALE_BLOCK, axis=1)
        return (half_cols(quant).astype(jnp.float32) * wide).astype(jnp.bfloat16)

    qkv_local = jnp.concatenate(
        [
            expand_rows(wq_quant, wq_scale),
            expand_rows(key_weight_quantized, key_weight_scale),
            expand_rows(value_weight_quantized, value_weight_scale),
        ],
        axis=1,
    )
    col_count = wo_quant.shape[1]
    spread_scale = jnp.repeat(wo_scale, SCALE_BLOCK, axis=1)
    own_scale = half_cols(lax.dynamic_slice_in_dim(spread_scale, actor * col_count, col_count, 1))
    wo_local = (
        half_cols(wo_quant).astype(jnp.float32) * jnp.repeat(own_scale, SCALE_BLOCK, axis=0)
    ).astype(jnp.bfloat16).T
    sums = spread(qkv_local, leaf_states, norm_gain[None, :], n_actor)
    wo_local, sums, prefix_length = lax.optimization_barrier((wo_local, sums, prefix_length))
    both_length = jnp.concatenate([prefix_length, trade(prefix_length)], axis=0)

    def half_row(x):
        width = x.shape[0] // 2
        return lax.dynamic_slice_in_dim(x, side * width, width, 0)

    bias = jnp.concatenate([half_row(q_bias), half_row(key_bias), half_row(value_bias)])
    sums = sums + bias.astype(jnp.float32)
    v_width = value_bias.shape[0] // 2
    rot_width = sums.shape[1] - v_width
    rotated = apply_rotary(
        sums[:, :rot_width].reshape(2 * leaf_count, rot_width // HEAD_WIDTH, HEAD_WIDTH),
        both_length,
    ).reshape(2 * leaf_count, rot_width)
    done = jnp.concatenate([rotated, sums[:, rot_width:]], axis=1).astype(jnp.bfloat16)
    own = done[:leaf_count]
    other = trade(done[leaf_count:])
    q_width = q_bias.shape[0] // 2

    kv_half = v_width // HEAD_WIDTH
    query_group = q_bias.shape[0] // key_bias.shape[0]
    outs = []
    for which, block in ((side, own), (1 - side, other)):
        q = block[:, :q_width].reshape(leaf_count, kv_half, query_group, HEAD_WIDTH)
        k = block[:, q_width : q_width + v_width].reshape(leaf_count, kv_half, HEAD_WIDTH)
        v = block[:, q_width + v_width :].reshape(leaf_count, kv_half, HEAD_WIDTH)
        for head in range(kv_half):
            at = (which * kv_half + head) * HEAD_WIDTH
            outs.append(
                attend_single_head(
                    q[:, head],
                    k[:, head],
                    v[:, head],
                    lax.dynamic_slice_in_dim(prefix_key_cache, at, HEAD_WIDTH, 2),
                    lax.dynamic_slice_in_dim(prefix_value_cache, at, HEAD_WIDTH, 2),
                    parent_prefix_slot,
                    prefix_length,
                )
                .reshape(leaf_count, query_group * HEAD_WIDTH)
                .astype(jnp.bfloat16)
            )
    mine = jnp.concatenate(outs[:kv_half], axis=1)
    theirs = jnp.concatenate(outs[kv_half:], axis=1)
    attended = jnp.where(
        side == 0,
        jnp.concatenate([mine, theirs], axis=1),
        jnp.concatenate([theirs, mine], axis=1),
    )

    wo_all = lax.all_gather(wo_local, "actor", axis=0, tiled=True)
    group = lax.axis_index("tp")
    cores = [(0, 1), (1, 0)]

    def project(rows):
        part = lax.dot_general(
            rows, wo_all, (((1,), (1,)), ((), ())), preferred_element_type=jnp.float32
        )
        width = part.shape[1] // 2
        first, second = part[:, :width], part[:, width:]
        give = jnp.where(group == 0, second, first)
        keep = jnp.where(group == 0, first, second)
        return (keep + lax.ppermute(give, "tp", cores)).astype(jnp.bfloat16), give

    def join(x):
        y = lax.ppermute(x, "tp", cores)
        return jnp.where(
            group == 0,
            jnp.concatenate([x, y], axis=1),
            jnp.concatenate([y, x], axis=1),
        )

    away, marker = project(trade(attended))
    attended, away, _ = lax.optimization_barrier((attended, away, marker))
    away = trade(away)
    local = join(project(attended)[0])
    remote = join(away)
    low = jnp.where(side == 0, local, remote)
    high = jnp.where(side == 0, remote, local)
    pieces = []
    half = col_count // 2
    for a in range(n_actor):
        pieces += [low[:, a * half : (a + 1) * half], high[:, a * half : (a + 1) * half]]
    return jnp.concatenate(pieces, axis=1)


LANES = 128


def fused_kernel(
    n_actor,
    states_ref,
    gain_ref,
    wq_ref,
    wq_scale_ref,
    wk_ref,
    wk_scale_ref,
    wv_ref,
    wv_scale_ref,
    wo_ref,
    wo_scale_ref,
    qb_ref,
    kb_ref,
    vb_ref,
    kcache_ref,
    vcache_ref,
    parent_ref,
    length_ref,
    out_ref,
    raw_ref,
    rawv_ref,
    wown_ref,
    woth_ref,
    give_ref,
    xraw_ref,
    xs_ref,
    lens_ref,
    tabs_ref,
    gains_ref,
    bias_ref,
    acc_ref,
    rst_ref,
    vst_ref,
    rq_ref,
    rv_ref,
    kc_ref,
    vc_ref,
    woraw_ref,
    zset_ref,
    mask_ref,
    att_ref,
    psend_ref,
    precv_ref,
    res_ref,
    load_sem,
    kv_sem,
    z_send,
    z_recv,
    g_send,
    x_send,
    x_recv,
    xs_send,
    xs_recv,
    t_send,
    t_recv,
    q_send,
    q_recv,
    v_send,
    v_recv,
    a_send,
    a_recv,
    oz_send,
    oz_recv,
    p_send,
    p_recv,
    c_send,
    c_recv,
    f_send,
    f_recv,
):
    line = n_actor // 2
    actor = lax.axis_index("actor")
    job = lax.axis_index("job")
    core = lax.axis_index("tp")
    at, y = actor // 2, actor % 2
    side = job % 2
    there = {"job": job + 1 - 2 * side}
    pair = {"actor": at * 2 + 1 - y}
    diagonal = {"job": job + 1 - 2 * side, "actor": at * 2 + 1 - y}
    sibling = {"tp": 1 - core}
    above, below = {"actor": actor + 2}, {"actor": actor - 2}
    has_up, has_down = at + 1 < line, at >= 1
    middle = jnp.logical_and(has_up, has_down)
    ends = jnp.logical_not(middle)
    rows = raw_ref.shape[1]
    count = xraw_ref.shape[0]
    half_rows = rows // 2
    half_count = count // 2
    width = raw_ref.shape[2]
    units = width // LANES
    heads = 2 * units - 1
    depth = zset_ref.shape[1]
    strips = n_actor // 2
    part = strips // 2
    f32, bf16 = jnp.float32, jnp.bfloat16

    def lanes(unit, n=1):
        return pl.ds(pl.multiple_of(unit * LANES, LANES), n * LANES)

    barrier = pltpu.get_barrier_semaphore()

    @pl.when(has_up)
    def _():
        pl.semaphore_signal(barrier, inc=1, device_id=above)

    @pl.when(has_down)
    def _():
        pl.semaphore_signal(barrier, inc=1, device_id=below)

    for peer in (there, pair, diagonal, sibling):
        pl.semaphore_signal(barrier, inc=1, device_id=peer)

    def local(source, target, sem):
        return pltpu.make_async_copy(source, target, sem)

    def remote(source, target, ss, rs, peer):
        return pltpu.make_async_remote_copy(
            src_ref=source, dst_ref=target, send_sem=ss, recv_sem=rs, device_id=peer
        )

    first = 2 * side
    w_loads = [
        local(wq_ref.at[:, lanes(side * heads, units)], raw_ref.at[0], load_sem.at[0]),
        local(
            wq_ref.at[:, lanes(side * heads + units, units - 1)],
            raw_ref.at[1, :, pl.ds(0, (units - 1) * LANES)],
            load_sem.at[1],
        ),
        local(
            wk_ref.at[:, lanes(side)],
            raw_ref.at[1, :, pl.ds((units - 1) * LANES, LANES)],
            load_sem.at[2],
        ),
        local(wv_ref.at[:, lanes(side)], rawv_ref, load_sem.at[3]),
    ]
    state_load = local(states_ref, xraw_ref, load_sem.at[4])
    wo_load = local(
        wo_ref.at[:, lanes(first, 2)], woraw_ref.at[:, pl.ds(0, 2 * LANES)], load_sem.at[5]
    )
    wo_load_last = local(
        wo_ref.at[:, pl.ds(4 * LANES, LANES)], woraw_ref.at[:, pl.ds(2 * LANES, LANES)],
        load_sem.at[6],
    )
    for copy in w_loads:
        copy.start()
    state_load.start()
    wo_load.start()
    wo_load_last.start()
    kv_loads = []
    for j in range(2):
        for p in range(2):
            place = pl.ds(p * LANES, LANES)
            cut = pl.ds(j * LANES, LANES)
            kv_loads.append(
                local(kcache_ref.at[p, :, cut], kc_ref.at[j, :, place], kv_sem.at[0, j, p])
            )
            kv_loads.append(
                local(vcache_ref.at[p, :, cut], vc_ref.at[j, :, place], kv_sem.at[1, j, p])
            )
    for copy in kv_loads:
        copy.start()

    blocks = rows // SCALE_BLOCK

    def pick(ref, row, column):
        values = ref[pl.ds(row, 1), :]
        here = lax.broadcasted_iota(jnp.int32, values.shape, 1) == column
        return jnp.sum(jnp.where(here, values, 0.0), axis=1, keepdims=True)

    def unit_scale(parity, block, u):
        row = actor * blocks + block
        if u < units - 1:
            return pick(wq_scale_ref, side * heads + u + units * parity, row)
        return jnp.where(
            parity == 0,
            pick(wq_scale_ref, side * heads + u, row),
            pick(wk_scale_ref, side, row),
        )

    def expand(parity, target, chosen):
        for block in chosen:
            cut = pl.ds(block * SCALE_BLOCK, SCALE_BLOCK)
            for u in range(units):
                lane = pl.ds(u * LANES, LANES)
                scaled = raw_ref[parity, cut, lane].astype(f32) * unit_scale(parity, block, u)
                target(cut, lane, scaled.astype(bf16))

    def to_give(cut, lane, value):
        give_ref[cut, lane] = value

    def to_own(cut, lane, value):
        wown_ref[at, cut, lane] = value

    for copy in w_loads:
        copy.wait()
    first_blocks = -(-half_rows // SCALE_BLOCK)

    def expand_own(chosen):
        expand(y, to_own, chosen)
        for block in chosen:
            cut = pl.ds(block * SCALE_BLOCK, SCALE_BLOCK)
            scale = pick(wv_scale_ref, side, actor * blocks + block)
            scaled = rawv_ref[cut, :].astype(f32) * scale
            wown_ref[at, cut, pl.ds(width, LANES)] = scaled.astype(bf16)

    expand_own(range(first_blocks))
    pl.semaphore_wait(barrier, 4 + has_up.astype(jnp.int32) + has_down.astype(jnp.int32))

    def half(p):
        return pl.ds(p * half_rows, half_rows)

    def give(p):
        return remote(
            give_ref.at[half(p)], woth_ref.at[at, half(p)], g_send.at[p], z_recv.at[1, at, p], pair
        )

    def up_down(way, kind, spot, p):
        ref = (wown_ref if kind == 0 else woth_ref).at[spot, half(p)]
        return remote(
            ref, ref, z_send.at[way, kind, spot, p], z_recv.at[kind, spot, p], (above, below)[way]
        )

    def both_ways(kind, spot, p):
        @pl.when(has_up)
        def _():
            up_down(0, kind, spot, p).start()

        @pl.when(has_down)
        def _():
            up_down(1, kind, spot, p).start()

    both_ways(0, at, 0)
    expand(1 - y, to_give, range(first_blocks))
    give(0).start()
    expand_own(range(first_blocks, blocks))
    both_ways(0, at, 1)
    expand(1 - y, to_give, range(first_blocks, blocks))
    give(1).start()

    lens_ref[0] = length_ref[...].astype(f32).reshape(1, count)
    table_sends = [
        remote(lens_ref.at[0], lens_ref.at[slot], t_send.at[slot], t_recv.at[slot], peer)
        for slot, peer in ((1, there), (2, pair), (3, diagonal))
    ]
    for copy in table_sends:
        copy.start()

    state_load.wait()

    gains_ref[...] = gain_ref[...].astype(f32).reshape(1, -1)
    for i, ref in enumerate((qb_ref, kb_ref, vb_ref)):
        bias_ref[i, :, : ref.shape[0]] = ref[...].astype(f32).reshape(1, -1)

    def normalize(i, carry):
        cut = pl.ds(pl.multiple_of(i * 16, 16), 16)
        x = xraw_ref[cut, :].astype(f32)
        x = x * lax.rsqrt(jnp.mean(x * x, axis=-1, keepdims=True) + epsilon)
        x = (x * gains_ref[...]).astype(bf16)
        for source in range(n_actor):
            xs_ref[source, cut, :] = x[:, source * rows : (source + 1) * rows]
        return carry

    lax.fori_loop(0, count // 16, normalize, 0)

    def some(p):
        return pl.ds(core * strips + p * part, part)

    def of_slot(slot):
        return pl.ds(slot * count, count)

    def share(slot, p, origin, peer):
        return remote(
            xs_ref.at[some(p), of_slot(origin)],
            xs_ref.at[some(p), of_slot(slot)],
            x_send.at[slot - 1, p],
            x_recv.at[slot - 1, p],
            peer,
        )

    share_list = [
        share(1, 0, 0, there),
        share(2, 1, 0, pair),
        share(1, 1, 0, there),
        share(2, 0, 0, pair),
    ]
    for copy in share_list:
        copy.start()

    def to_sibling(slot, p):
        ref = xs_ref.at[some(p), of_slot(slot)]
        return remote(ref, ref, xs_send.at[slot - 1, p], xs_recv.at[slot - 1, p], sibling)

    def from_sibling(slot, p):
        ref = xs_ref.at[pl.ds((1 - core) * strips + p * part, part), of_slot(slot)]
        return remote(ref, ref, xs_send.at[slot - 1, p], xs_recv.at[slot - 1, p], sibling)

    def column(values):
        wide = jnp.broadcast_to(values, (LANES, count))
        return wide.T

    lane_at = lax.broadcasted_iota(jnp.int32, (count, LANES), 1)
    step = lax.rem(lax.broadcasted_iota(jnp.int32, (1, LANES), 1), LANES // 2).astype(f32)
    freqs = jnp.exp(step * (-2.0 * math.log(rope_base) / LANES))
    def make_table(slot):
        angles = column(lens_ref[slot]) * freqs
        tabs_ref[slot] = jnp.where(lane_at < LANES // 2, jnp.cos(angles), jnp.sin(angles))


    wo_load.wait()
    wo_load_last.wait()
    wo_blocks = depth // SCALE_BLOCK
    wo_units = wo_ref.shape[1] // LANES

    def expand_wo(block, carry):
        cut = pl.ds(pl.multiple_of(block * SCALE_BLOCK, SCALE_BLOCK), SCALE_BLOCK)
        for u in range(2):
            lane = pl.ds(u * LANES, LANES)
            scale = pick(wo_scale_ref, block, actor * wo_units + first + u)
            zset_ref[at, cut, lane] = (woraw_ref[cut, lane].astype(f32) * scale).astype(bf16)
        return carry

    lax.fori_loop(0, wo_blocks, expand_wo, 0)

    def has_extra(spot, s):
        return spot % 2 == s

    @pl.when(has_extra(at, side))
    def _():
        def expand_last(block, carry):
            cut = pl.ds(pl.multiple_of(block * SCALE_BLOCK, SCALE_BLOCK), SCALE_BLOCK)
            lane = pl.ds(2 * LANES, LANES)
            scale = pick(wo_scale_ref, block, actor * wo_units + 4)
            zset_ref[at, cut, lane] = (woraw_ref[cut, lane].astype(f32) * scale).astype(bf16)
            return carry

        lax.fori_loop(0, wo_blocks, expand_last, 0)

    def wo_way(way, spot, q):
        ref = zset_ref.at[spot, :, pl.ds(q * LANES, LANES)]
        return remote(
            ref, ref, oz_send.at[way, spot, q], oz_recv.at[spot, q], (above, below)[way]
        )

    def each_piece(spot, action):
        for q in range(2):
            action(q)

        @pl.when(has_extra(spot, side))
        def _():
            action(2)

    def wo_begin(far):
        @pl.when(jnp.logical_and(at == far, has_up))
        def _():
            each_piece(at, lambda q: wo_way(0, at, q).start())

        @pl.when(jnp.logical_and(line - 1 - at == far, has_down))
        def _():
            each_piece(at, lambda q: wo_way(1, at, q).start())

    def relay_one(way, spot):
        def action(q):
            wo_way(way, spot, q).wait_recv()

            @pl.when((has_up, has_down)[way])
            def _():
                wo_way(way, spot, q).start()

        each_piece(spot, action)

    def relay(far):
        @pl.when(at >= far)
        def _():
            relay_one(0, at - far)

        @pl.when(at + far < line)
        def _():
            relay_one(1, at + far)

    for p in range(2):
        give(p).wait_recv()
        both_ways(1, at, p)
    wo_begin(0)

    acc_ref[...] = jnp.zeros_like(acc_ref)
    make_table(0)
    for slot in (1, 2, 3):
        table_sends[slot - 1].wait_recv()
        make_table(slot)
    length = column(lens_ref[0])[:, :1].astype(jnp.int32)
    mask_ref[...] = jnp.where(
        lax.broadcasted_iota(jnp.int32, mask_ref.shape, 1) < length, 0.0, -jnp.inf
    )

    def multiply_kind(kind, spot):
        if kind == 0:
            acc_ref[...] += jnp.dot(
                xs_ref[spot * 2 + y], wown_ref[spot], preferred_element_type=f32
            )
        else:
            acc_ref[:, :width] += jnp.dot(
                xs_ref[spot * 2 + 1 - y], woth_ref[spot], preferred_element_type=f32
            )

    def multiply(spot):
        multiply_kind(0, spot)
        multiply_kind(1, spot)

    def multiply_far(far, carry):
        @pl.when(at >= far)
        def _():
            multiply(at - far)

        @pl.when(jnp.logical_and(at + far < line, far > 0))
        def _():
            multiply(at + far)

        return carry

    def rows_first():
        for slot, p, peer in ((1, 0, pair), (2, 1, there), (1, 1, None), (2, 0, None)):
            share(slot, p, 0, there if slot == 1 else pair).wait_recv()
            if peer is not None:
                share(3, p, slot, peer).start()
            to_sibling(slot, p).start()

    def rows_rest():
        for p in range(2):
            share(3, p, 1 + p, pair if p == 0 else there).wait_recv()
            to_sibling(3, p).start()

        for slot in (1, 2, 3):
            for p in range(2):
                from_sibling(slot, p).wait_recv()

    for far in range(1, line):
        for kind in range(2):
            for p in range(2):

                @pl.when(at >= far)
                def _():
                    up_down(0, kind, at - far, p).wait_recv()

                    @pl.when(has_up)
                    def _():
                        up_down(0, kind, at - far, p).start()

                @pl.when(at + far < line)
                def _():
                    up_down(1, kind, at + far, p).wait_recv()

                    @pl.when(has_down)
                    def _():
                        up_down(1, kind, at + far, p).start()

            if far == line - 1:

                @pl.when(at >= far)
                def _():
                    multiply_kind(kind, at - far)

                @pl.when(at + far < line)
                def _():
                    multiply_kind(kind, at + far)

        wo_begin(far)
        if far == 1:
            rows_first()
        if far == max(line - 2, 1):
            rows_rest()
            lax.fori_loop(0, max(line - 1, 1), multiply_far, 0)

    def results(slot):
        return (
            remote(rst_ref.at[slot], rq_ref.at[slot], q_send.at[slot], q_recv.at[slot], peers[slot]),
            remote(vst_ref.at[slot], rv_ref.at[slot], v_send.at[slot], v_recv.at[slot], peers[slot]),
        )

    peers = {1: there, 2: pair, 3: diagonal}
    for slot in (2, 1, 3, 0):
        table = tabs_ref[slot]
        swapped = pltpu.roll(table, LANES // 2, 1)
        cosine = jnp.where(lane_at < LANES // 2, table, swapped)
        sine = jnp.where(lane_at < LANES // 2, -swapped, table)
        for u in range(units):
            if u < units - 1:
                bias = bias_ref[0, :, lanes(side * heads + u + units * y)]
            else:
                bias = jnp.where(
                    y == 0,
                    bias_ref[0, :, lanes(side * heads + u)],
                    bias_ref[1, :, lanes(side)],
                )
            value = acc_ref[of_slot(slot), u * LANES : (u + 1) * LANES] + bias
            value = value * cosine + pltpu.roll(value, LANES // 2, 1) * sine
            (rst_ref if slot else rq_ref)[slot, u] = value.astype(bf16)
        (vst_ref if slot else rv_ref)[slot] = acc_ref[of_slot(slot), width:]
        if slot:
            for copy in results(slot):
                copy.start()

    @pl.when(middle)
    def _():
        relay(1)

    for copy in kv_loads:
        copy.wait()
    parent = column(parent_ref[...].astype(f32).reshape(1, count))[:, :1]
    in_first = (parent == 0).astype(f32)
    in_second = 1.0 - in_first
    scale_factor = math.log2(math.e) / math.sqrt(LANES)

    head_parts = ((0, units), (units, heads - units))

    def hand(slot, j, origin, peer, piece):
        cut = lanes(j * heads + head_parts[piece][0], head_parts[piece][1])

        def of(k):
            return att_ref.at[:, pl.ds(k * half_count, half_count), cut]

        return remote(
            of(origin),
            of(slot),
            a_send.at[slot - 1, origin - 1 if slot == 3 else j, piece],
            a_recv.at[slot - 1, j, piece],
            peer,
        )

    chunks = 4
    context = kc_ref.shape[1] // chunks

    def attend(base):
        group = side if base == 0 else 1 - side
        low = jnp.where(y == 0, base, base + 2)
        high = jnp.where(y == 0, base + 2, base)
        key_new = rq_ref[high, units - 1].astype(f32)
        value_new = rv_ref[base] + rv_ref[base + 2] + bias_ref[2, :, lanes(group)]
        value_new = value_new.astype(bf16).astype(f32)

        def head(h, carry):
            query = rq_ref[
                jnp.where(h < units, low, high), jnp.where(h < units, h, h - units)
            ].astype(f32)
            own = jnp.sum(query * key_new, axis=-1, keepdims=True) * scale_factor
            both = jnp.concatenate([query * in_first, query * in_second], axis=1).astype(bf16)
            highest = own
            pieces = []
            for c in range(chunks):
                scores = lax.dot_general(
                    both,
                    kc_ref[group, c * context : (c + 1) * context],
                    (((1,), (1,)), ((), ())),
                    preferred_element_type=f32,
                )
                scores = scores * scale_factor + mask_ref[:, c * context : (c + 1) * context]
                highest = jnp.maximum(highest, jnp.max(scores, axis=-1, keepdims=True))
                pieces.append(scores)
            own = jnp.exp2(own - highest)
            total, mixed = own, None
            for c, scores in enumerate(pieces):
                weights = jnp.exp2(scores - highest)
                total = total + jnp.sum(weights, axis=-1, keepdims=True)
                more = jnp.dot(
                    weights.astype(bf16),
                    vc_ref[group, c * context : (c + 1) * context],
                    preferred_element_type=f32,
                )
                mixed = more if mixed is None else mixed + more
            mixed = jnp.where(parent == 0, mixed[:, :LANES], mixed[:, LANES:])
            mixed = mixed + own.astype(bf16).astype(f32) * value_new
            mixed = (mixed / total).astype(bf16)
            for which in range(2):
                att_ref[which, :half_count, lanes(group * heads + h)] = mixed[
                    which * half_count : (which + 1) * half_count
                ]
            return carry

        for piece, (start, n) in enumerate(head_parts):
            lax.fori_loop(start, start + n, head, 0)
            hand(1, group, 0, there, piece).start()
            hand(2, group, 0, pair, piece).start()

    for copy in results(2):
        copy.wait_recv()
    attend(0)

    for slot in (1, 3):
        for copy in results(slot):
            copy.wait_recv()
    attend(1)
    for piece in range(2):
        hand(2, side, 0, pair, piece).wait_recv()
        hand(3, side, 2, there, piece).start()
    for piece in range(2):
        hand(1, side, 0, there, piece).wait_recv()
        hand(3, side, 1, pair, piece).start()

    @pl.when(middle)
    def _():
        relay(2)

    for piece in range(2):
        hand(1, 1 - side, 0, there, piece).wait_recv()
        hand(2, 1 - side, 0, pair, piece).wait_recv()

    bounds = tuple(pl.ds(k * LANES, LANES) for k in range(3))

    groups = ((0, 3), (3, 1))

    def rows_of(g):
        return pl.ds(groups[g][0] * half_count, groups[g][1] * half_count)

    def p_copy(spot, k, g):
        return remote(
            psend_ref.at[spot, rows_of(g), bounds[k]],
            precv_ref.at[spot, rows_of(g), bounds[k]],
            p_send.at[spot, k, g],
            p_recv.at[spot, k, g],
            sibling,
        )

    def unit_of(spot, s, parity, k):
        return wo_units * (2 * spot + parity) + (4 if k == 2 else 2 * s + k)

    def target(spot, s, parity, k):
        mine = pl.ds(pl.multiple_of(core * half_count, half_count), half_count)
        return out_ref.at[mine, lanes(unit_of(spot, s, parity, k))]

    def result(spot, slot, k):
        return res_ref.at[spot, pl.ds(slot * half_count, half_count), bounds[k]]

    def sibling_copy(spot, k):
        return remote(
            target(spot, side, y, k),
            target(spot, side, y, k),
            f_send.at[0, spot, k],
            f_recv.at[0, spot, k],
            sibling,
        )

    def send_copy(spot, slot, k):
        return remote(
            result(spot, slot, k),
            target(spot, side, y, k),
            c_send.at[slot - 1, spot, k],
            c_recv.at[slot - 1, spot, k],
            peers[slot],
        )

    source_side = (side, 1 - side, side, 1 - side)
    source_parity = (y, y, 1 - y, 1 - y)

    def onward_copy(spot, slot, k):
        ref = target(spot, source_side[slot], source_parity[slot], k)
        return remote(ref, ref, f_send.at[slot, spot, k], f_recv.at[slot, spot, k], sibling)

    def across(ks):
        return pl.ds(ks[0] * LANES, len(ks) * LANES)

    def send_part(spot, ks, g):
        psend_ref[spot, rows_of(g), across(ks)] = jnp.dot(
            att_ref[1 - core, rows_of(g)], zset_ref[spot, :, across(ks)], preferred_element_type=f32
        )
        for k in ks:
            p_copy(spot, k, g).start()

    def keep_part(spot, ks, g):
        kept = jnp.dot(
            att_ref[core, rows_of(g)], zset_ref[spot, :, across(ks)], preferred_element_type=f32
        )
        for k in ks:
            p_copy(spot, k, g).wait_recv()
        kept = (kept + precv_ref[spot, rows_of(g), across(ks)]).astype(bf16)
        res_ref[spot, rows_of(g), across(ks)] = kept
        if g == 1:
            for k in ks:
                send_copy(spot, 3, k).start()
            return
        for slot in (1, 2):
            for k in ks:
                send_copy(spot, slot, k).start()
        mine = pl.ds(pl.multiple_of(core * half_count, half_count), half_count)
        for i, k in enumerate(ks):
            out_ref[mine, lanes(unit_of(spot, side, y, k))] = kept[
                :half_count, i * LANES : (i + 1) * LANES
            ]
            sibling_copy(spot, k).start()

    def wide_part(spot, action):
        action((0, 1))

        @pl.when(has_extra(spot, side))
        def _():
            action((2,))

    def each_part(spot, s, action):
        action(0)
        action(1)

        @pl.when(has_extra(spot, s))
        def _():
            action(2)

    def project_send(spot, g):
        wide_part(spot, lambda ks: send_part(spot, ks, g))

    def project_keep(spot, g):
        wide_part(spot, lambda ks: keep_part(spot, ks, g))

    def onward(spot):
        for slot in (1, 2, 3):

            def action(k):
                send_copy(spot, slot, k).wait_recv()
                onward_copy(spot, slot, k).start()

            each_part(spot, source_side[slot], action)

    def at_far(action, far):
        @pl.when(at >= far)
        def _():
            action(at - far)

        @pl.when(jnp.logical_and(at + far < line, far > 0))
        def _():
            action(at + far)

    def relays(far, carry):
        @pl.when(jnp.logical_and(far > 0, jnp.logical_or(ends, far > 2)))
        def _():
            relay(far)

        return carry

    def sends(g):
        def body(far, carry):
            if g == 0:
                relays(far, 0)
            at_far(lambda spot: project_send(spot, g), far)
            return carry

        return body

    def keeps(g):
        def body(far, carry):
            at_far(lambda spot: project_keep(spot, g), far)
            return carry

        return body

    def onwards(far, carry):
        at_far(onward, far)
        return carry

    lax.fori_loop(0, line - 1, sends(0), 0)
    lax.fori_loop(0, line - 1, keeps(0), 0)
    for j in range(2):
        for piece in range(2):
            hand(3, j, 1, pair, piece).wait_recv()
    lax.fori_loop(0, line - 1, sends(1), 0)
    lax.fori_loop(0, line - 1, keeps(1), 0)

    @pl.when(ends)
    def _():
        def last(way, spot):
            def action(q):
                wo_way(way, spot, q).wait_recv()
                for g in (0, 1):
                    send_part(spot, (q,), g)
                for g in (1, 0):
                    keep_part(spot, (q,), g)

            each_piece(spot, action)

        @pl.when(at >= line - 1)
        def _():
            last(0, at - (line - 1))

        @pl.when(at + line - 1 < line)
        def _():
            last(1, at + line - 1)

    lax.fori_loop(0, line, onwards, 0)

    for p in range(2):
        give(p).wait_send()
        for slot, peer in ((1, there), (2, pair), (3, pair)):
            share(slot, p, 0, peer).wait_send()
            to_sibling(slot, p).wait_send()
    for copy in table_sends:
        copy.wait_send()
    for slot in (1, 2, 3):
        for copy in results(slot):
            copy.wait_send()
    for j in range(2):
        for slot in (1, 2, 3):
            for piece in range(2):
                hand(slot, j, j + 1 if slot == 3 else 0, there, piece).wait_send()

    def finish(spot, carry):
        @pl.when(jnp.logical_and(has_up, at >= spot))
        def _():
            for kind in range(2):
                for p in range(2):
                    up_down(0, kind, spot, p).wait_send()
            each_piece(spot, lambda q: wo_way(0, spot, q).wait_send())

        @pl.when(jnp.logical_and(has_down, at <= spot))
        def _():
            for kind in range(2):
                for p in range(2):
                    up_down(1, kind, spot, p).wait_send()
            each_piece(spot, lambda q: wo_way(1, spot, q).wait_send())

        def end_part(k):
            for g in range(2):
                p_copy(spot, k, g).wait_send()
            sibling_copy(spot, k).wait()
            for slot in (1, 2, 3):
                send_copy(spot, slot, k).wait_send()

        each_part(spot, side, end_part)
        for slot in (1, 2, 3):
            each_part(
                spot, source_side[slot], lambda k: onward_copy(spot, slot, k).wait()
            )
        return carry

    lax.fori_loop(0, line, finish, 0)


def fused(n_actor, args):
    (
        leaf_states, norm_gain, wq_quant, wq_scale, wk, wk_scale, wv, wv_scale, wo_quant, wo_scale,
        q_bias, key_bias, value_bias, kcache, vcache, parent, length,
    ) = args
    count, features = leaf_states.shape
    rows = wq_quant.shape[0]
    heads = wq_quant.shape[1] // (2 * LANES)
    units = (heads + 1) // 2
    width = units * LANES
    context = kcache.shape[1]
    depth = wo_quant.shape[0]
    line = n_actor // 2
    total_units = n_actor * (wo_quant.shape[1] // LANES)
    bf16, f32 = jnp.bfloat16, jnp.float32
    any_space = pl.BlockSpec(memory_space=pl.ANY)
    vmem = pl.BlockSpec(memory_space=pltpu.VMEM)
    dma = pltpu.SemaphoreType.DMA
    return pl.pallas_call(
        functools.partial(fused_kernel, n_actor),
        out_shape=jax.ShapeDtypeStruct((count, total_units * LANES), bf16),
        in_specs=[
            any_space, vmem, any_space, vmem, any_space, vmem, any_space, vmem, any_space, vmem,
            vmem, vmem, vmem, any_space, any_space, vmem, vmem,
        ],
        out_specs=vmem,
        scratch_shapes=[
            pltpu.VMEM((2, rows, width), bf16),
            pltpu.VMEM((rows, LANES), bf16),
            pltpu.VMEM((line, rows, width + LANES), bf16),
            pltpu.VMEM((line, rows, width), bf16),
            pltpu.VMEM((rows, width), bf16),
            pltpu.VMEM((count, features), bf16),
            pltpu.VMEM((n_actor, 4 * count, rows), bf16),
            pltpu.VMEM((4, 1, count), f32),
            pltpu.VMEM((4, count, LANES), f32),
            pltpu.VMEM((1, features), f32),
            pltpu.VMEM((3, 1, 2 * heads * LANES), f32),
            pltpu.VMEM((4 * count, width + LANES), f32),
            pltpu.VMEM((4, units, count, LANES), bf16),
            pltpu.VMEM((4, count, LANES), f32),
            pltpu.VMEM((4, units, count, LANES), bf16),
            pltpu.VMEM((4, count, LANES), f32),
            pltpu.VMEM((2, context, 2 * LANES), bf16),
            pltpu.VMEM((2, context, 2 * LANES), bf16),
            pltpu.VMEM((depth, 3 * LANES), bf16),
            pltpu.VMEM((line, depth, 3 * LANES), bf16),
            pltpu.VMEM((count, context), f32),
            pltpu.VMEM((2, 2 * count, 2 * heads * LANES), bf16),
            pltpu.VMEM((line, 2 * count, 3 * LANES), f32),
            pltpu.VMEM((line, 2 * count, 3 * LANES), f32),
            pltpu.VMEM((line, 2 * count, 3 * LANES), bf16),
            dma((7,)),
            dma((2, 2, 2)),
            dma((2, 2, line, 2)),
            dma((2, line, 2)),
            dma((2,)),
            dma((3, 2)),
            dma((3, 2)),
            dma((3, 2)),
            dma((3, 2)),
            dma((4,)),
            dma((4,)),
            dma((4,)),
            dma((4,)),
            dma((4,)),
            dma((4,)),
            dma((3, 2, 2)),
            dma((3, 2, 2)),
            dma((2, line, 3)),
            dma((line, 3)),
            dma((line, 3, 2)),
            dma((line, 3, 2)),
            dma((3, line, 3)),
            dma((3, line, 3)),
            dma((4, line, 3)),
            dma((4, line, 3)),
        ],
        compiler_params=pltpu.CompilerParams(
            collective_id=0, has_side_effects=True, vmem_limit_bytes=58 * 1024 * 1024
        ),
        cost_estimate=pl.CostEstimate(
            flops=13_000_000_000, bytes_accessed=30_000_000, transcendentals=6_000_000
        ),
    )(
        leaf_states, norm_gain, wq_quant, wq_scale.T, wk, wk_scale.T, wv, wv_scale.T, wo_quant,
        wo_scale, q_bias, key_bias, value_bias, kcache, vcache, parent, length,
    )


def per_device_fused(n_actor, *args):
    return fused(n_actor, args)


def fits_fused(mesh_sizes, args):
    n_job, n_actor, n_tp = mesh_sizes
    return (
        n_tp == 2
        and n_job % 2 == 0
        and n_actor % 8 == 0
        and args[0].shape[0] % 32 == 0
        and args[2].shape[0] % SCALE_BLOCK == 0
        and (args[2].shape[1] // LANES) % 4 == 2
        and args[4].shape[1] == 2 * LANES
        and args[8].shape[1] == 5 * LANES
        and args[13].shape[0] == 2
    )


def per_device_any(mesh_sizes, *args):
    if fits_fused(mesh_sizes, args):
        return per_device_fused(mesh_sizes[1], *args)
    return per_device(mesh_sizes[:2], *args)


def solution(mesh):
    placed = (
        P(("job", "actor"), None),
        P(),
        P("actor", "tp"),
        P(None, "tp"),
        P("actor", "tp"),
        P(None, "tp"),
        P("actor", "tp"),
        P(None, "tp"),
        P("tp", "actor"),
        P("tp", None),
        P("tp"),
        P("tp"),
        P("tp"),
        P(("job", "actor"), None, "tp"),
        P(("job", "actor"), None, "tp"),
        P(("job", "actor")),
        P(("job", "actor")),
    )
    return jax.shard_map(
        functools.partial(
            per_device_any, (mesh.shape["job"], mesh.shape["actor"], mesh.shape["tp"])
        ),
        mesh=mesh,
        in_specs=placed,
        out_specs=P(("job", "actor"), None),
        check_vma=False,
    )
```
